256 devices in a mesh: ctx: 16 (over z, x_hi), head: 8 (over y, x_lo), dp: 2 (over core).
Axes of the slice: x: 4 (x_hi: 2, x_lo: 2; x = x_hi * 2 + x_lo), y: 4, z: 8, core: 2. Of those that a mesh axis runs over, the one named last changes fastest.
Arguments:
- query: bfloat16 [2, 8192, 5120], P('dp', 'ctx', 'head'), may hold values from -6 to 6
- key: bfloat16 [2, 8192, 1024], P('dp', 'ctx', 'head'), may hold values from -6 to 6
- value: bfloat16 [2, 8192, 1024], P('dp', 'ctx', 'head'), may hold values from -6 to 6
- output: bfloat16 [2, 8192, 5120], P('dp', 'ctx', 'head'), may hold values from -1.796875 to 1.796875
- output_gradient: bfloat16 [2, 8192, 5120], P('dp', 'ctx', 'head'), may hold values from -96 to 96
- parent: int32 [2, 16], P('dp'), may hold values from -1 to 14, as said below
- owner: int32 [2, 16], P('dp'), may hold values from 0 to 15, each once within a row
Outputs:
- d_query: bfloat16 [2, 8192, 5120], P('dp', 'ctx', 'head')
- d_key: bfloat16 [2, 8192, 1024], P('dp', 'ctx', 'head')
- d_value: bfloat16 [2, 8192, 1024], P('dp', 'ctx', 'head')
- bias_q_grad: float32 [5120], P('head')
- bias_k_grad: float32 [1024], P('head')
- bias_v_grad: float32 [1024], P('head')
The draws below stay inside these ranges and needn't reach their ends.
Inputs may be any that keep to these rules, and one draw needn't show every extreme that they name: In each tree, tiles 0 to 1 form the prompt, each with parent t - 1 (tile 0 has -1); the later tiles form 8 consecutive runs (responses) of 1 or 2 tiles, some run of 2 in every tree; a run's first tile has as parent the last prompt tile, its second tile has the run's first tile.
All inputs are finite; a program needn't handle non-finite values.
Results may differ from the reference program's by a relative error of at most 0.005.
Values may be sent and summed in bfloat16 or wider, within the bound.
A program may use at most 64 MiB of HBM per device.

```python
import jax
import jax.numpy as jnp
from jax import lax

QUERY_HEADS = 40
KEY_HEADS = 8
HEAD_WIDTH = 128
MASK_TILE = 512
QUERY_PER_KV = 5
PROMPT_TREES = 2
TREE_TILES = 16
TREE_TOKENS = 8192
PROMPT_TILES = 2
RESPONSES = 8
RESP_TILES = 14


def drawn_pair(key):
    base = jax.random.fold_in(key, 17)
    key_q, key_k = jax.random.split(base, 2)
    query_layout = (PROMPT_TREES, TREE_TOKENS, KEY_HEADS, QUERY_PER_KV, HEAD_WIDTH)
    key_layout = (PROMPT_TREES, TREE_TOKENS, KEY_HEADS, HEAD_WIDTH)
    query_rows = jnp.clip(jax.random.normal(key_q, query_layout, jnp.float32), -6.0, 6.0)
    key_rows = jnp.clip(jax.random.normal(key_k, key_layout, jnp.float32), -6.0, 6.0)
    return (query_rows.reshape(PROMPT_TREES, TREE_TOKENS, QUERY_HEADS * HEAD_WIDTH), key_rows.reshape(PROMPT_TREES, TREE_TOKENS, KEY_HEADS * HEAD_WIDTH))


def draw_query(key, part):
    return drawn_pair(key)[0].astype(jnp.bfloat16)


def draw_key(key, part):
    return drawn_pair(key)[1].astype(jnp.bfloat16)


def draw_parent(key, part):

    def one_tree(subkey):
        order = jax.random.permutation(subkey, RESPONSES).astype(jnp.int32)
        lengths = 1 + (order < RESP_TILES - RESPONSES).astype(jnp.int32)
        starts = PROMPT_TILES + jnp.cumsum(lengths) - lengths
        tiles = jnp.arange(TREE_TILES, dtype=jnp.int32)
        first = jnp.any(tiles[:, None] == starts[None, :], axis=1)
        first = jnp.logical_and(first, tiles >= PROMPT_TILES)
        return jnp.where(first, PROMPT_TILES - 1, tiles - 1).astype(jnp.int32)
    return jax.vmap(one_tree)(jax.random.split(jax.random.fold_in(key, 3), PROMPT_TREES))


def block_levels(own_key, extent, shards, least, high):
    loudness, own = 1.0, jax.random.fold_in(own_key, 6)
    for position, parts in shards:
        steps = jnp.exp(jax.random.uniform(jax.random.fold_in(own, position), (parts,), jnp.float32, least / len(shards), high / len(shards)))
        loudness = loudness * jnp.repeat(steps, extent[position] // parts).reshape([-1 if axis == position else 1 for axis in range(len(extent))])
    return loudness


def centred(key, dims, width, limit, cuts=(), kind=jnp.bfloat16):
    factor_of = block_levels(key, dims, cuts, -0.22, 0.18) if cuts else 1.0
    entries = jax.random.normal(key, dims, jnp.float32) * width * factor_of
    return jnp.minimum(jnp.maximum(entries, -limit), limit).astype(kind)


def setup_inputs(seed: int = 0) -> dict:
    key_of = jax.random.split(jax.random.key(seed), 8)
    return {
        "query": draw_query(jax.random.fold_in(key_of[7], 71), 0),
        "key": draw_key(jax.random.fold_in(key_of[7], 71), 0),
        "value": centred(key_of[2], (PROMPT_TREES, TREE_TOKENS, KEY_HEADS * HEAD_WIDTH), 1.0, 6.0, ((0, 2), (1, 16), (2, 8))),
        "output": centred(key_of[3], (PROMPT_TREES, TREE_TOKENS, QUERY_HEADS * HEAD_WIDTH), 0.3, 1.796875, ((0, 2), (1, 16), (2, 8))),
        "output_gradient": centred(key_of[4], (PROMPT_TREES, TREE_TOKENS, QUERY_HEADS * HEAD_WIDTH), 16.0, 96.0, ((0, 2), (1, 16), (2, 8))),
        "parent": draw_parent(jax.random.fold_in(key_of[7], 71), 0),
        "owner": jax.vmap(lambda own: jax.random.permutation(own, TREE_TILES))(jax.random.split(key_of[6], PROMPT_TREES)).reshape((PROMPT_TREES, TREE_TILES)).astype(jnp.int32),
    }


NEGATIVE_FILL = -1e30


def tree_tables(parent_row, owner_row):
    count = parent_row.shape[0]
    tiles = jnp.arange(count, dtype=jnp.int32)
    tile_at = jnp.sum(jnp.where(owner_row[None, :] == tiles[:, None], tiles[None, :], 0), axis=1).astype(jnp.int32)

    def climb(step, state):
        reach, current = state
        match = current[:, None] == tiles[None, :]
        reach = jnp.logical_or(reach, match)
        upward = jnp.sum(jnp.where(match, parent_row[None, :], 0), axis=1)
        upward = jnp.where(current < 0, -1, upward).astype(jnp.int32)
        return reach, upward

    reach, _ = lax.fori_loop(0, count, climb, (jnp.zeros((count, count), bool), tiles))
    select = (tile_at[:, None] == tiles[None, :]).astype(jnp.float32)
    packed = jnp.dot(jnp.dot(select, reach.astype(jnp.float32), precision=lax.Precision.HIGHEST), select.T, precision=lax.Precision.HIGHEST)
    seen = (packed > 0.5).astype(jnp.int32)
    return tile_at, seen


def one_tree(query, key, value, output, output_gradient, seen, trained):
    scale_factor = HEAD_WIDTH ** -0.5
    high = lax.Precision.HIGHEST
    query_grouped5 = query.reshape(TREE_TILES, MASK_TILE, KEY_HEADS, QUERY_PER_KV, HEAD_WIDTH).astype(jnp.float32)
    gradient_grouped5 = output_gradient.reshape(TREE_TILES, MASK_TILE, KEY_HEADS, QUERY_PER_KV, HEAD_WIDTH).astype(jnp.float32)
    output_grouped5 = output.reshape(TREE_TILES, MASK_TILE, KEY_HEADS, QUERY_PER_KV, HEAD_WIDTH).astype(jnp.float32)
    key_tensor4 = key.reshape(TREE_TILES, MASK_TILE, KEY_HEADS, HEAD_WIDTH).astype(jnp.float32)
    value_tensor4 = value.reshape(TREE_TILES, MASK_TILE, KEY_HEADS, HEAD_WIDTH).astype(jnp.float32)
    causal = jnp.arange(MASK_TILE)[:, None] >= jnp.arange(MASK_TILE)[None, :]

    def scores_of(i, j):
        scores = jnp.einsum('ignd,jgd->gnij', query_grouped5[i], key_tensor4[j], precision=high) * scale_factor
        keep = jnp.logical_or(i != j, causal)
        return scores, keep

    def row_stats(i):
        def visit(j, state):
            def update(st):
                top, total = st
                scores, keep = scores_of(i, j)
                scores = jnp.where(keep, scores, NEGATIVE_FILL)
                top_new = jnp.maximum(top, jnp.max(scores, axis=-1))
                probs = jnp.where(keep, jnp.exp(scores - top_new[..., None]), 0.0)
                return top_new, total * jnp.exp(top - top_new) + jnp.sum(probs, axis=-1)
            return lax.cond(seen[i, j] > 0, update, lambda st: st, state)

        start_index = (jnp.full((KEY_HEADS, QUERY_PER_KV, MASK_TILE), NEGATIVE_FILL, jnp.float32), jnp.zeros((KEY_HEADS, QUERY_PER_KV, MASK_TILE), jnp.float32))
        top, total = lax.fori_loop(0, TREE_TILES, visit, start_index)
        return top + jnp.log(total)

    lse_all = lax.map(row_stats, jnp.arange(TREE_TILES))

    def row_grads(i, carry):
        delta = jnp.sum(gradient_grouped5[i] * output_grouped5[i], axis=-1).transpose(1, 2, 0)

        def visit(j, inner):
            def update(st):
                query_gradient, key_gradient, value_gradient = st
                scores, keep = scores_of(i, j)
                probs = jnp.where(keep, jnp.exp(scores - lse_all[i][..., None]), 0.0)
                p16 = lax.optimization_barrier(probs.astype(jnp.bfloat16)).astype(jnp.float32)
                value_gradient = value_gradient.at[j].add(jnp.einsum('gnij,ignd->jgd', p16, gradient_grouped5[i], precision=high))
                dprobs = jnp.einsum('ignd,jgd->gnij', gradient_grouped5[i], value_tensor4[j], precision=high)
                ds = probs * (dprobs - delta[..., None])
                ds16 = lax.optimization_barrier(ds.astype(jnp.bfloat16)).astype(jnp.float32)
                query_gradient = query_gradient.at[i].add(jnp.einsum('gnij,jgd->ignd', ds16, key_tensor4[j], precision=high) * scale_factor)
                key_gradient = key_gradient.at[j].add(jnp.einsum('gnij,ignd->jgd', ds16, query_grouped5[i], precision=high) * scale_factor)
                return query_gradient, key_gradient, value_gradient
            return lax.cond(seen[i, j] > 0, update, lambda st: st, inner)

        return lax.cond(trained[i], lambda c: lax.fori_loop(0, TREE_TILES, visit, c), lambda c: c, carry)

    start_index = (jnp.zeros((TREE_TILES, MASK_TILE, KEY_HEADS, QUERY_PER_KV, HEAD_WIDTH), jnp.float32),
             jnp.zeros((TREE_TILES, MASK_TILE, KEY_HEADS, HEAD_WIDTH), jnp.float32),
             jnp.zeros((TREE_TILES, MASK_TILE, KEY_HEADS, HEAD_WIDTH), jnp.float32))
    query_gradient, key_gradient, value_gradient = lax.fori_loop(0, TREE_TILES, row_grads, start_index)
    return query_gradient.reshape(TREE_TOKENS, QUERY_HEADS * HEAD_WIDTH), key_gradient.reshape(TREE_TOKENS, KEY_HEADS * HEAD_WIDTH), value_gradient.reshape(TREE_TOKENS, KEY_HEADS * HEAD_WIDTH)


def reference(query, key, value, output, output_gradient, parent, owner):
    norm = (PROMPT_TREES * TREE_TOKENS) ** -0.5
    query_rows, key_rows, values = [], [], []
    bias_q = jnp.zeros((QUERY_HEADS * HEAD_WIDTH,), jnp.float32)
    key_bias_term = jnp.zeros((KEY_HEADS * HEAD_WIDTH,), jnp.float32)
    value_bias_term = jnp.zeros((KEY_HEADS * HEAD_WIDTH,), jnp.float32)
    for tree in range(PROMPT_TREES):
        tile_at, seen = tree_tables(parent[tree], owner[tree])
        trained = tile_at >= PROMPT_TILES
        query_gradient, key_gradient, value_gradient = one_tree(query[tree], key[tree], value[tree], output[tree], output_gradient[tree], seen, trained)
        bias_q = bias_q + jnp.sum(query_gradient, axis=0)
        key_bias_term = key_bias_term + jnp.sum(key_gradient, axis=0)
        value_bias_term = value_bias_term + jnp.sum(value_gradient, axis=0)
        query_rows.append(query_gradient.astype(jnp.bfloat16))
        key_rows.append(key_gradient.astype(jnp.bfloat16))
        values.append(value_gradient.astype(jnp.bfloat16))
    return (jnp.stack(query_rows), jnp.stack(key_rows), jnp.stack(values), bias_q * norm, key_bias_term * norm, value_bias_term * norm)
```

```python
import functools

import jax
import jax.numpy as jnp
from jax import lax
from jax.experimental import pallas as pl
from jax.experimental.pallas import tpu as pltpu
from jax.sharding import PartitionSpec as P

HEAD_WIDTH = 128

NEGATIVE_FILL = -1e30


def tree_tables(parent_row, owner_row):
    count = parent_row.shape[0]
    tiles = jnp.arange(count, dtype=jnp.int32)
    tile_at = jnp.sum(jnp.where(owner_row[None, :] == tiles[:, None], tiles[None, :], 0), axis=1)

    def climb(step, state):
        reach, current = state
        match = current[:, None] == tiles[None, :]
        reach = jnp.logical_or(reach, match)
        upward = jnp.sum(jnp.where(match, parent_row[None, :], 0), axis=1)
        upward = jnp.where(current < 0, -1, upward)
        return (reach, upward)

    reach, _ = lax.fori_loop(0, count, climb, (jnp.zeros((count, count), bool), tiles))
    return tile_at, reach


def pick_entry(vector, index):
    spots = jnp.arange(vector.shape[0], dtype=jnp.int32)
    return jnp.sum(jnp.where(spots == index, vector, 0), axis=0)


def attention_grads_kernel(flags_ref, q_ref, g_ref, o_ref, k_ref, v_ref,
                           dq_ref, dk_ref, dv_ref, s_scr, *, slots, scale):
    head = pl.program_id(0)

    @pl.when(head == 0)
    def _():
        dk_ref[...] = jnp.zeros_like(dk_ref)
        dv_ref[...] = jnp.zeros_like(dv_ref)

    q = q_ref[...]
    g = g_ref[...]
    o = o_ref[...]
    rows = q.shape[0]
    delta = jnp.sum(g.astype(jnp.float32) * o.astype(jnp.float32), axis=1, keepdims=True)
    causal = (lax.broadcasted_iota(jnp.int32, (rows, rows), 0)
              >= lax.broadcasted_iota(jnp.int32, (rows, rows), 1))
    nt = (((1,), (1,)), ((), ()))
    tn = (((0,), (0,)), ((), ()))

    top = jnp.full((rows, 1), NEGATIVE_FILL, jnp.float32)
    for j in range(slots):
        keep = flags_ref[j] > 0
        if j == slots - 1:
            keep = jnp.logical_and(keep, causal)
        scores = lax.dot_general(q, k_ref[j], nt, preferred_element_type=jnp.float32) * scale
        scores = jnp.where(keep, scores, NEGATIVE_FILL)
        s_scr[j] = scores
        top = jnp.maximum(top, jnp.max(scores, axis=1, keepdims=True))

    total = jnp.zeros((rows, 1), jnp.float32)
    for j in range(slots):
        keep = flags_ref[j] > 0
        if j == slots - 1:
            keep = jnp.logical_and(keep, causal)
        probs = jnp.where(keep, jnp.exp(s_scr[j] - top), 0.0)
        s_scr[j] = probs
        total = total + jnp.sum(probs, axis=1, keepdims=True)
    inverse = jnp.where(total > 0, 1.0 / jnp.where(total > 0, total, 1.0), 0.0)

    dq = jnp.zeros((rows, q.shape[1]), jnp.float32)
    for j in range(slots):
        probs = s_scr[j] * inverse
        dv_ref[j] += lax.dot_general(probs.astype(jnp.bfloat16), g, tn,
                                     preferred_element_type=jnp.float32)
        dprobs = lax.dot_general(g, v_ref[j], nt, preferred_element_type=jnp.float32)
        dscores = (probs * (dprobs - delta)).astype(jnp.bfloat16)
        dq = dq + jnp.dot(dscores, k_ref[j], preferred_element_type=jnp.float32)
        dk_ref[j] += lax.dot_general(dscores, q, tn, preferred_element_type=jnp.float32) * scale
    dq_ref[...] = dq * scale


def attention_grads(flags, q, g, o, keys, values, scale):
    rows, wide = q.shape
    slots = keys.shape[0]
    heads = wide // HEAD_WIDTH
    col = pl.BlockSpec((rows, HEAD_WIDTH), lambda h, f: (0, h))
    whole = pl.BlockSpec((slots, rows, HEAD_WIDTH), lambda h, f: (0, 0, 0))
    return pl.pallas_call(
        functools.partial(attention_grads_kernel, slots=slots, scale=scale),
        grid_spec=pltpu.PrefetchScalarGridSpec(
            num_scalar_prefetch=1,
            grid=(heads,),
            in_specs=[col, col, col, whole, whole],
            out_specs=[col, whole, whole],
            scratch_shapes=[pltpu.VMEM((slots, rows, rows), jnp.float32)],
        ),
        out_shape=[
            jax.ShapeDtypeStruct((rows, wide), jnp.float32),
            jax.ShapeDtypeStruct((slots, rows, HEAD_WIDTH), jnp.float32),
            jax.ShapeDtypeStruct((slots, rows, HEAD_WIDTH), jnp.float32),
        ],
        compiler_params=pltpu.CompilerParams(
            dimension_semantics=("arbitrary",), vmem_limit_bytes=48 * 1024 * 1024
        ),
    )(flags, q, g, o, keys, values)


def on_device(query, key, value, output, output_gradient, parent, owner):
    count = lax.axis_size("ctx")
    me = lax.axis_index("ctx")
    tile = query.shape[1]
    width = key.shape[2]
    scale_factor = HEAD_WIDTH ** (-0.5)
    prompt_tiles = count // 8
    parent_row = parent[0]
    owner_row = owner[0]
    tile_at, reach = tree_tables(parent_row, owner_row)
    my_tile = pick_entry(tile_at, me)
    tiles = jnp.arange(count, dtype=jnp.int32)
    reach_row = jnp.sum(jnp.where((tiles == my_tile)[:, None], reach, False), axis=0) > 0
    trained = my_tile >= prompt_tiles
    above = pick_entry(parent_row, my_tile)
    second = above >= prompt_tiles
    slot_tiles = jnp.stack(
        [jnp.int32(0), jnp.int32(1), jnp.where(second, above, 1).astype(jnp.int32)]
    )
    slot_blocks = jnp.sum(
        jnp.where(slot_tiles[:, None] == tiles[None, :], owner_row[None, :], 0), axis=1
    ).astype(jnp.int32)
    slot_seen = jnp.sum(
        jnp.where(slot_tiles[:, None] == tiles[None, :], reach_row[None, :], False), axis=1
    ) > 0
    slot_new = jnp.stack([True, slot_tiles[1] != slot_tiles[0], second])
    slot_keep = jnp.logical_and(jnp.logical_and(slot_seen, slot_new), trained)
    flags = jnp.concatenate([slot_keep, trained[None]]).astype(jnp.int32)

    pair = jnp.concatenate([key[0], value[0]], axis=1)
    gathered = lax.all_gather(pair, "ctx")
    picked = gathered[slot_blocks]
    keys = jnp.concatenate([picked[:, :, :width], key[0][None]], axis=0)
    values = jnp.concatenate([picked[:, :, width:], value[0][None]], axis=0)

    dq, dk, dv = attention_grads(
        flags, query[0], output_gradient[0], output[0], keys, values, scale_factor
    )
    partial = jnp.concatenate([dk, dv], axis=2)
    targets = jnp.concatenate([slot_blocks, me[None].astype(jnp.int32)])
    spread = jnp.zeros((count, tile, 2 * width), jnp.float32).at[targets].add(partial)
    grads = lax.psum_scatter(spread, "ctx", scatter_dimension=0, tiled=True)[0]

    total_rows = lax.axis_size("dp") * query.shape[0] * count * tile
    norm = total_rows ** (-0.5)
    sum_q, sum_k, sum_v = lax.psum(
        (jnp.sum(dq, axis=0), jnp.sum(grads[:, :width], axis=0), jnp.sum(grads[:, width:], axis=0)),
        ("ctx", "dp"),
    )
    return (
        dq.astype(jnp.bfloat16)[None],
        grads[:, :width].astype(jnp.bfloat16)[None],
        grads[:, width:].astype(jnp.bfloat16)[None],
        sum_q * norm,
        sum_k * norm,
        sum_v * norm,
    )


def solution(mesh):
    return jax.shard_map(
        on_device,
        mesh=mesh,
        in_specs=(
            P("dp", "ctx", "head"),
            P("dp", "ctx", "head"),
            P("dp", "ctx", "head"),
            P("dp", "ctx", "head"),
            P("dp", "ctx", "head"),
            P("dp", None),
            P("dp", None),
        ),
        out_specs=(
            P("dp", "ctx", "head"),
            P("dp", "ctx", "head"),
            P("dp", "ctx", "head"),
            P("head"),
            P("head"),
            P("head"),
        ),
        check_vma=False,
    )
```

```python
import functools

import jax
import jax.numpy as jnp
from jax import lax
from jax.experimental import pallas as pl
from jax.experimental.pallas import tpu as pltpu
from jax.sharding import PartitionSpec as P

HEAD_WIDTH = 128

NEGATIVE_FILL = -1e30


def pick_entry(vector, index):
    spots = jnp.arange(vector.shape[0], dtype=jnp.int32)
    return jnp.sum(jnp.where(spots == index, vector, 0), axis=0)


def pick_rows(matrix, index):
    spots = jnp.arange(matrix.shape[0], dtype=jnp.int32)
    return jnp.sum(jnp.where((spots == index)[:, None], matrix, 0.0), axis=0)


def attention_grads_kernel(flags_ref, q_ref, g_ref, o_ref, k_ref, v_ref,
                           dq_ref, dk_ref, dv_ref, s_scr, *, slots, scale):
    head = pl.program_id(0)

    @pl.when(head == 0)
    def _():
        dk_ref[...] = jnp.zeros_like(dk_ref)
        dv_ref[...] = jnp.zeros_like(dv_ref)

    q = q_ref[...]
    g = g_ref[...]
    o = o_ref[...]
    rows = q.shape[0]
    delta = jnp.sum(g.astype(jnp.float32) * o.astype(jnp.float32), axis=1, keepdims=True)
    causal = (lax.broadcasted_iota(jnp.int32, (rows, rows), 0)
              >= lax.broadcasted_iota(jnp.int32, (rows, rows), 1))
    nt = (((1,), (1,)), ((), ()))
    tn = (((0,), (0,)), ((), ()))

    top = jnp.full((rows, 1), NEGATIVE_FILL, jnp.float32)
    for j in range(slots):
        keep = flags_ref[j] > 0
        if j == slots - 1:
            keep = jnp.logical_and(keep, causal)
        scores = lax.dot_general(q, k_ref[j], nt, preferred_element_type=jnp.float32) * scale
        scores = jnp.where(keep, scores, NEGATIVE_FILL)
        s_scr[j] = scores
        top = jnp.maximum(top, jnp.max(scores, axis=1, keepdims=True))

    total = jnp.zeros((rows, 1), jnp.float32)
    for j in range(slots):
        keep = flags_ref[j] > 0
        if j == slots - 1:
            keep = jnp.logical_and(keep, causal)
        probs = jnp.where(keep, jnp.exp(s_scr[j] - top), 0.0)
        s_scr[j] = probs
        total = total + jnp.sum(probs, axis=1, keepdims=True)
    inverse = jnp.where(total > 0, 1.0 / jnp.where(total > 0, total, 1.0), 0.0)

    dq = jnp.zeros((rows, q.shape[1]), jnp.float32)
    for j in range(slots):
        probs = s_scr[j] * inverse
        dv_ref[j] += lax.dot_general(probs.astype(jnp.bfloat16), g, tn,
                                     preferred_element_type=jnp.float32)
        dprobs = lax.dot_general(g, v_ref[j], nt, preferred_element_type=jnp.float32)
        dscores = (probs * (dprobs - delta)).astype(jnp.bfloat16)
        dq = dq + jnp.dot(dscores, k_ref[j], preferred_element_type=jnp.float32)
        dk_ref[j] += lax.dot_general(dscores, q, tn, preferred_element_type=jnp.float32) * scale
    dq_ref[...] = dq * scale


def attention_grads(flags, q, g, o, keys, values, scale):
    rows, wide = q.shape
    slots = keys.shape[0]
    heads = wide // HEAD_WIDTH
    col = pl.BlockSpec((rows, HEAD_WIDTH), lambda h, f: (0, h))
    whole = pl.BlockSpec((slots, rows, HEAD_WIDTH), lambda h, f: (0, 0, 0))
    return pl.pallas_call(
        functools.partial(attention_grads_kernel, slots=slots, scale=scale),
        grid_spec=pltpu.PrefetchScalarGridSpec(
            num_scalar_prefetch=1,
            grid=(heads,),
            in_specs=[col, col, col, whole, whole],
            out_specs=[col, whole, whole],
            scratch_shapes=[pltpu.VMEM((slots, rows, rows), jnp.float32)],
        ),
        out_shape=[
            jax.ShapeDtypeStruct((rows, wide), jnp.float32),
            jax.ShapeDtypeStruct((slots, rows, HEAD_WIDTH), jnp.float32),
            jax.ShapeDtypeStruct((slots, rows, HEAD_WIDTH), jnp.float32),
        ],
        compiler_params=pltpu.CompilerParams(
            dimension_semantics=("arbitrary",), vmem_limit_bytes=48 * 1024 * 1024
        ),
    )(flags, q, g, o, keys, values)


def on_device(query, key, value, output, output_gradient, parent, owner):
    count = lax.axis_size("ctx")
    me = lax.axis_index("ctx")
    tile = query.shape[1]
    width = key.shape[2]
    scale_factor = HEAD_WIDTH ** (-0.5)
    prompt_tiles = count // 8
    parent_row = parent[0]
    owner_row = owner[0]
    tiles = jnp.arange(count, dtype=jnp.int32)
    my_tile = jnp.sum(jnp.where(owner_row == me, tiles, 0))
    trained = my_tile >= prompt_tiles
    above = pick_entry(parent_row, my_tile)
    second = jnp.logical_and(trained, above >= prompt_tiles)
    slot_tiles = jnp.stack(
        [jnp.int32(0), jnp.int32(1), jnp.where(second, above, 1).astype(jnp.int32)]
    )
    slot_blocks = jnp.sum(
        jnp.where(slot_tiles[:, None] == tiles[None, :], owner_row[None, :], 0), axis=1
    ).astype(jnp.int32)
    flags = jnp.stack([trained, trained, second, trained]).astype(jnp.int32)

    pair = jnp.concatenate([key[0], value[0]], axis=1)
    gathered = lax.all_gather(pair, "ctx")
    picked = gathered[slot_blocks]
    keys = jnp.concatenate([picked[:, :, :width], key[0][None]], axis=0)
    values = jnp.concatenate([picked[:, :, width:], value[0][None]], axis=0)

    dq, dk, dv = attention_grads(
        flags, query[0], output_gradient[0], output[0], keys, values, scale_factor
    )
    partial = jnp.concatenate([dk, dv], axis=2)
    targets = jnp.concatenate([slot_blocks, me[None].astype(jnp.int32)])
    spread = jnp.zeros((count, tile, 2 * width), jnp.float32).at[targets].add(partial)
    grads = lax.psum_scatter(spread, "ctx", scatter_dimension=0, tiled=True)[0]

    total_rows = lax.axis_size("dp") * query.shape[0] * count * tile
    norm = total_rows ** (-0.5)
    sums = jnp.concatenate(
        [jnp.sum(dq, axis=0), jnp.sum(grads[:, :width], axis=0), jnp.sum(grads[:, width:], axis=0)]
    )
    groups = lax.axis_size("head")
    slots = jnp.zeros((groups, sums.shape[0]), jnp.float32).at[lax.axis_index("head")].set(sums)
    slots = lax.psum(slots, ("ctx", "head", "dp"))
    sums = pick_rows(slots, lax.axis_index("head")) * norm
    wide = query.shape[2]
    sum_q, sum_k, sum_v = sums[:wide], sums[wide:wide + width], sums[wide + width:]
    return (
        dq.astype(jnp.bfloat16)[None],
        grads[:, :width].astype(jnp.bfloat16)[None],
        grads[:, width:].astype(jnp.bfloat16)[None],
        sum_q,
        sum_k,
        sum_v,
    )


def solution(mesh):
    return jax.shard_map(
        on_device,
        mesh=mesh,
        in_specs=(
            P("dp", "ctx", "head"),
            P("dp", "ctx", "head"),
            P("dp", "ctx", "head"),
            P("dp", "ctx", "head"),
            P("dp", "ctx", "head"),
            P("dp", None),
            P("dp", None),
        ),
        out_specs=(
            P("dp", "ctx", "head"),
            P("dp", "ctx", "head"),
            P("dp", "ctx", "head"),
            P("head"),
            P("head"),
            P("head"),
        ),
        check_vma=False,
    )
```

```python
import functools

import jax
import jax.numpy as jnp
from jax import lax
from jax.experimental import pallas as pl
from jax.experimental.pallas import tpu as pltpu
from jax.sharding import PartitionSpec as P

HEAD_WIDTH = 128

NEGATIVE_FILL = -1e30


def pick_entry(vector, index):
    spots = jnp.arange(vector.shape[0], dtype=jnp.int32)
    return jnp.sum(jnp.where(spots == index, vector, 0), axis=0)


def pick_rows(matrix, index):
    spots = jnp.arange(matrix.shape[0], dtype=jnp.int32)
    return jnp.sum(jnp.where((spots == index)[:, None], matrix, 0.0), axis=0)


def attention_grads_kernel(flags_ref, q_ref, g_ref, o_ref, k_ref, v_ref,
                           dq_ref, dk_ref, dv_ref, s_scr, *, slots, scale):
    head = pl.program_id(0)

    @pl.when(head == 0)
    def _():
        dk_ref[...] = jnp.zeros_like(dk_ref)
        dv_ref[...] = jnp.zeros_like(dv_ref)

    q = q_ref[...]
    g = g_ref[...]
    o = o_ref[...]
    rows = q.shape[0]
    delta = jnp.sum(g.astype(jnp.float32) * o.astype(jnp.float32), axis=1, keepdims=True)
    causal = (lax.broadcasted_iota(jnp.int32, (rows, rows), 0)
              >= lax.broadcasted_iota(jnp.int32, (rows, rows), 1))
    nt = (((1,), (1,)), ((), ()))
    tn = (((0,), (0,)), ((), ()))

    top = jnp.full((rows, 1), NEGATIVE_FILL, jnp.float32)
    for j in range(slots):
        keep = flags_ref[j] > 0
        if j == slots - 1:
            keep = jnp.logical_and(keep, causal)
        scores = lax.dot_general(q, k_ref[j], nt, preferred_element_type=jnp.float32) * scale
        scores = jnp.where(keep, scores, NEGATIVE_FILL)
        s_scr[j] = scores
        top = jnp.maximum(top, jnp.max(scores, axis=1, keepdims=True))

    total = jnp.zeros((rows, 1), jnp.float32)
    for j in range(slots):
        keep = flags_ref[j] > 0
        if j == slots - 1:
            keep = jnp.logical_and(keep, causal)
        probs = jnp.where(keep, jnp.exp(s_scr[j] - top), 0.0)
        s_scr[j] = probs
        total = total + jnp.sum(probs, axis=1, keepdims=True)
    inverse = jnp.where(total > 0, 1.0 / jnp.where(total > 0, total, 1.0), 0.0)

    dq = jnp.zeros((rows, q.shape[1]), jnp.float32)
    for j in range(slots):
        probs = s_scr[j] * inverse
        dv_ref[j] += lax.dot_general(probs.astype(jnp.bfloat16), g, tn,
                                     preferred_element_type=jnp.float32)
        dprobs = lax.dot_general(g, v_ref[j], nt, preferred_element_type=jnp.float32)
        dscores = (probs * (dprobs - delta)).astype(jnp.bfloat16)
        dq = dq + jnp.dot(dscores, k_ref[j], preferred_element_type=jnp.float32)
        dk_ref[j] += lax.dot_general(dscores, q, tn, preferred_element_type=jnp.float32) * scale
    dq_ref[...] = dq * scale


def attention_grads(flags, q, g, o, keys, values, scale):
    rows, wide = q.shape
    slots = keys.shape[0]
    heads = wide // HEAD_WIDTH
    col = pl.BlockSpec((rows, HEAD_WIDTH), lambda h, f: (0, h))
    whole = pl.BlockSpec((slots, rows, HEAD_WIDTH), lambda h, f: (0, 0, 0))
    return pl.pallas_call(
        functools.partial(attention_grads_kernel, slots=slots, scale=scale),
        grid_spec=pltpu.PrefetchScalarGridSpec(
            num_scalar_prefetch=1,
            grid=(heads,),
            in_specs=[col, col, col, whole, whole],
            out_specs=[col, whole, whole],
            scratch_shapes=[pltpu.VMEM((slots, rows, rows), jnp.float32)],
        ),
        out_shape=[
            jax.ShapeDtypeStruct((rows, wide), jnp.float32),
            jax.ShapeDtypeStruct((slots, rows, HEAD_WIDTH), jnp.float32),
            jax.ShapeDtypeStruct((slots, rows, HEAD_WIDTH), jnp.float32),
        ],
        compiler_params=pltpu.CompilerParams(
            dimension_semantics=("arbitrary",), vmem_limit_bytes=48 * 1024 * 1024
        ),
    )(flags, q, g, o, keys, values)


def exchange_kernel(x_ref, out_ref, send_sem, recv_sem, self_sem, *, axis, n, indexed):
    me = lax.axis_index(axis)
    barrier = pltpu.get_barrier_semaphore()
    for d in range(1, n):
        pl.semaphore_signal(
            barrier, inc=1, device_id={axis: lax.rem(me + d, n)},
            device_id_type=pl.DeviceIdType.MESH,
        )
    pl.semaphore_wait(barrier, n - 1)
    copies = []
    for d in range(1, n):
        peer = lax.rem(me + d, n)
        copy = pltpu.make_async_remote_copy(
            src_ref=x_ref.at[peer] if indexed else x_ref,
            dst_ref=out_ref.at[me],
            send_sem=send_sem.at[d - 1],
            recv_sem=recv_sem.at[d - 1],
            device_id={axis: peer},
            device_id_type=pl.DeviceIdType.MESH,
        )
        copy.start()
        copies.append(copy)
    local = pltpu.make_async_copy(x_ref.at[me] if indexed else x_ref, out_ref.at[me], self_sem)
    local.start()
    for copy in copies:
        copy.wait_send()
    for copy in copies:
        copy.wait_recv()
    local.wait()


def exchange(x, axis, indexed, collective_id):
    n = lax.axis_size(axis)
    piece = x.shape[1:] if indexed else x.shape
    return pl.pallas_call(
        functools.partial(exchange_kernel, axis=axis, n=n, indexed=indexed),
        out_shape=jax.ShapeDtypeStruct((n,) + tuple(piece), x.dtype),
        in_specs=[pl.BlockSpec(memory_space=pl.ANY)],
        out_specs=pl.BlockSpec(memory_space=pl.ANY),
        scratch_shapes=[
            pltpu.SemaphoreType.DMA((n - 1,)),
            pltpu.SemaphoreType.DMA((n - 1,)),
            pltpu.SemaphoreType.DMA,
        ],
        compiler_params=pltpu.CompilerParams(collective_id=collective_id, has_side_effects=True),
    )(x)


def on_device(query, key, value, output, output_gradient, parent, owner):
    count = lax.axis_size("ctx")
    me = lax.axis_index("ctx")
    tile = query.shape[1]
    width = key.shape[2]
    scale_factor = HEAD_WIDTH ** (-0.5)
    prompt_tiles = count // 8
    parent_row = parent[0]
    owner_row = owner[0]
    tiles = jnp.arange(count, dtype=jnp.int32)
    my_tile = jnp.sum(jnp.where(owner_row == me, tiles, 0))
    trained = my_tile >= prompt_tiles
    above = pick_entry(parent_row, my_tile)
    second = jnp.logical_and(trained, above >= prompt_tiles)
    slot_tiles = jnp.stack(
        [jnp.int32(0), jnp.int32(1), jnp.where(second, above, 1).astype(jnp.int32)]
    )
    slot_blocks = jnp.sum(
        jnp.where(slot_tiles[:, None] == tiles[None, :], owner_row[None, :], 0), axis=1
    ).astype(jnp.int32)
    flags = jnp.stack([trained, trained, second, trained]).astype(jnp.int32)

    pair = jnp.concatenate([key[0], value[0]], axis=1)
    gathered = exchange(pair, "ctx", False, 0)
    picked = gathered[slot_blocks]
    keys = jnp.concatenate([picked[:, :, :width], key[0][None]], axis=0)
    values = jnp.concatenate([picked[:, :, width:], value[0][None]], axis=0)

    dq, dk, dv = attention_grads(
        flags, query[0], output_gradient[0], output[0], keys, values, scale_factor
    )
    partial = jnp.concatenate([dk, dv], axis=2)
    targets = jnp.concatenate([slot_blocks, me[None].astype(jnp.int32)])
    total_rows = lax.axis_size("dp") * query.shape[0] * count * tile
    norm = total_rows ** (-0.5)
    wide = query.shape[2]
    dq_sum = jnp.sum(dq, axis=0)
    kv_sum = jnp.sum(partial, axis=(0, 1))
    tail_width = 2 * width
    tail_rows = 8
    tail = jnp.concatenate(
        [dq_sum, kv_sum, jnp.zeros((tail_rows * tail_width - wide - tail_width,), jnp.float32)]
    ).reshape(tail_rows, tail_width)
    spread = jnp.zeros((count, tile, tail_width), jnp.float32).at[targets].add(partial)
    spread = jnp.concatenate([spread, jnp.broadcast_to(tail, (count, tail_rows, tail_width))], axis=1)
    landed = exchange(spread, "ctx", True, 1)
    summed = landed[0]
    for peer in range(1, count):
        summed = summed + landed[peer]
    grads = summed[:tile]
    both = exchange(summed[tile:], "dp", False, 2)
    sums = (both[0] + both[1]).reshape(-1) * norm
    sum_q = sums[:wide]
    sum_k = sums[wide:wide + width]
    sum_v = sums[wide + width:wide + 2 * width]
    return (
        dq.astype(jnp.bfloat16)[None],
        grads[:, :width].astype(jnp.bfloat16)[None],
        grads[:, width:].astype(jnp.bfloat16)[None],
        sum_q,
        sum_k,
        sum_v,
    )


def solution(mesh):
    return jax.shard_map(
        on_device,
        mesh=mesh,
        in_specs=(
            P("dp", "ctx", "head"),
            P("dp", "ctx", "head"),
            P("dp", "ctx", "head"),
            P("dp", "ctx", "head"),
            P("dp", "ctx", "head"),
            P("dp", None),
            P("dp", None),
        ),
        out_specs=(
            P("dp", "ctx", "head"),
            P("dp", "ctx", "head"),
            P("dp", "ctx", "head"),
            P("head"),
            P("head"),
            P("head"),
        ),
        check_vma=False,
    )
```

```python
import functools

import jax
import jax.numpy as jnp
from jax import lax
from jax.experimental import pallas as pl
from jax.experimental.pallas import tpu as pltpu
from jax.sharding import PartitionSpec as P

HEAD_WIDTH = 128

NEGATIVE_FILL = -1e30


def pick_entry(vector, index):
    spots = jnp.arange(vector.shape[0], dtype=jnp.int32)
    return jnp.sum(jnp.where(spots == index, vector, 0), axis=0)


def pick_rows(matrix, index):
    spots = jnp.arange(matrix.shape[0], dtype=jnp.int32)
    return jnp.sum(jnp.where((spots == index)[:, None], matrix, 0.0), axis=0)


def attention_grads_kernel(flags_ref, q_ref, g_ref, o_ref, k_ref, v_ref,
                           dq_ref, dk_ref, dv_ref, s_scr, *, slots, scale):
    head = pl.program_id(0)

    @pl.when(head == 0)
    def _():
        dk_ref[...] = jnp.zeros_like(dk_ref)
        dv_ref[...] = jnp.zeros_like(dv_ref)

    q = q_ref[...]
    g = g_ref[...]
    o = o_ref[...]
    rows = q.shape[0]
    delta = jnp.sum(g.astype(jnp.float32) * o.astype(jnp.float32), axis=1, keepdims=True)
    causal = (lax.broadcasted_iota(jnp.int32, (rows, rows), 0)
              >= lax.broadcasted_iota(jnp.int32, (rows, rows), 1))
    nt = (((1,), (1,)), ((), ()))
    tn = (((0,), (0,)), ((), ()))

    top = jnp.full((rows, 1), NEGATIVE_FILL, jnp.float32)
    for j in range(slots):
        keep = flags_ref[j] > 0
        if j == slots - 1:
            keep = jnp.logical_and(keep, causal)
        scores = lax.dot_general(q, k_ref[j], nt, preferred_element_type=jnp.float32) * scale
        scores = jnp.where(keep, scores, NEGATIVE_FILL)
        s_scr[j] = scores
        top = jnp.maximum(top, jnp.max(scores, axis=1, keepdims=True))

    total = jnp.zeros((rows, 1), jnp.float32)
    for j in range(slots):
        keep = flags_ref[j] > 0
        if j == slots - 1:
            keep = jnp.logical_and(keep, causal)
        probs = jnp.where(keep, jnp.exp(s_scr[j] - top), 0.0)
        s_scr[j] = probs
        total = total + jnp.sum(probs, axis=1, keepdims=True)
    inverse = jnp.where(total > 0, 1.0 / jnp.where(total > 0, total, 1.0), 0.0)

    dq = jnp.zeros((rows, q.shape[1]), jnp.float32)
    for j in range(slots):
        probs = s_scr[j] * inverse
        dv_ref[j] += lax.dot_general(probs.astype(jnp.bfloat16), g, tn,
                                     preferred_element_type=jnp.float32)
        dprobs = lax.dot_general(g, v_ref[j], nt, preferred_element_type=jnp.float32)
        dscores = (probs * (dprobs - delta)).astype(jnp.bfloat16)
        dq = dq + jnp.dot(dscores, k_ref[j], preferred_element_type=jnp.float32)
        dk_ref[j] += lax.dot_general(dscores, q, tn, preferred_element_type=jnp.float32) * scale
    dq_ref[...] = dq * scale


def attention_grads(flags, q, g, o, keys, values, scale):
    rows, wide = q.shape
    slots = keys.shape[0]
    heads = wide // HEAD_WIDTH
    col = pl.BlockSpec((rows, HEAD_WIDTH), lambda h, f: (0, h))
    whole = pl.BlockSpec((slots, rows, HEAD_WIDTH), lambda h, f: (0, 0, 0))
    return pl.pallas_call(
        functools.partial(attention_grads_kernel, slots=slots, scale=scale),
        grid_spec=pltpu.PrefetchScalarGridSpec(
            num_scalar_prefetch=1,
            grid=(heads,),
            in_specs=[col, col, col, whole, whole],
            out_specs=[col, whole, whole],
            scratch_shapes=[pltpu.VMEM((slots, rows, rows), jnp.float32)],
        ),
        out_shape=[
            jax.ShapeDtypeStruct((rows, wide), jnp.float32),
            jax.ShapeDtypeStruct((slots, rows, HEAD_WIDTH), jnp.float32),
            jax.ShapeDtypeStruct((slots, rows, HEAD_WIDTH), jnp.float32),
        ],
        compiler_params=pltpu.CompilerParams(
            dimension_semantics=("arbitrary",), vmem_limit_bytes=48 * 1024 * 1024
        ),
    )(flags, q, g, o, keys, values)


def exchange_kernel(x_ref, out_ref, send_sem, recv_sem, self_sem, *, axis, n, indexed):
    me = lax.axis_index(axis)
    barrier = pltpu.get_barrier_semaphore()
    for d in range(1, n):
        pl.semaphore_signal(
            barrier, inc=1, device_id={axis: lax.rem(me + d, n)},
            device_id_type=pl.DeviceIdType.MESH,
        )
    pl.semaphore_wait(barrier, n - 1)
    copies = []
    for d in range(1, n):
        peer = lax.rem(me + d, n)
        copy = pltpu.make_async_remote_copy(
            src_ref=x_ref.at[peer] if indexed else x_ref,
            dst_ref=out_ref.at[me],
            send_sem=send_sem.at[d - 1],
            recv_sem=recv_sem.at[d - 1],
            device_id={axis: peer},
            device_id_type=pl.DeviceIdType.MESH,
        )
        copy.start()
        copies.append(copy)
    local = pltpu.make_async_copy(x_ref.at[me] if indexed else x_ref, out_ref.at[me], self_sem)
    local.start()
    for copy in copies:
        copy.wait_send()
    for copy in copies:
        copy.wait_recv()
    local.wait()


def exchange(x, axis, indexed, collective_id):
    n = lax.axis_size(axis)
    piece = x.shape[1:] if indexed else x.shape
    return pl.pallas_call(
        functools.partial(exchange_kernel, axis=axis, n=n, indexed=indexed),
        out_shape=jax.ShapeDtypeStruct((n,) + tuple(piece), x.dtype),
        in_specs=[pl.BlockSpec(memory_space=pl.ANY)],
        out_specs=pl.BlockSpec(memory_space=pl.ANY),
        scratch_shapes=[
            pltpu.SemaphoreType.DMA((n - 1,)),
            pltpu.SemaphoreType.DMA((n - 1,)),
            pltpu.SemaphoreType.DMA,
        ],
        compiler_params=pltpu.CompilerParams(collective_id=collective_id, has_side_effects=True),
    )(x)


def on_device(query, key, value, output, output_gradient, parent, owner):
    count = lax.axis_size("ctx")
    me = lax.axis_index("ctx")
    tile = query.shape[1]
    width = key.shape[2]
    scale_factor = HEAD_WIDTH ** (-0.5)
    prompt_tiles = count // 8
    parent_row = parent[0]
    owner_row = owner[0]
    tiles = jnp.arange(count, dtype=jnp.int32)
    my_tile = jnp.sum(jnp.where(owner_row == me, tiles, 0))
    trained = my_tile >= prompt_tiles
    above = pick_entry(parent_row, my_tile)
    second = jnp.logical_and(trained, above >= prompt_tiles)
    slot_tiles = jnp.stack(
        [jnp.int32(0), jnp.int32(1), jnp.where(second, above, 1).astype(jnp.int32)]
    )
    slot_blocks = jnp.sum(
        jnp.where(slot_tiles[:, None] == tiles[None, :], owner_row[None, :], 0), axis=1
    ).astype(jnp.int32)
    flags = jnp.stack([trained, trained, second, trained]).astype(jnp.int32)

    pair = jnp.concatenate([key[0], value[0]], axis=1)
    gathered = exchange(pair, "ctx", False, 0)
    picked = gathered[slot_blocks]
    keys = jnp.concatenate([picked[:, :, :width], key[0][None]], axis=0)
    values = jnp.concatenate([picked[:, :, width:], value[0][None]], axis=0)

    dq, dk, dv = attention_grads(
        flags, query[0], output_gradient[0], output[0], keys, values, scale_factor
    )
    partial = jnp.concatenate([dk, dv], axis=2)
    targets = jnp.concatenate([slot_blocks, me[None].astype(jnp.int32)])
    total_rows = lax.axis_size("dp") * query.shape[0] * count * tile
    norm = total_rows ** (-0.5)
    wide = query.shape[2]
    dq_sum = jnp.sum(dq, axis=0)
    kv_sum = jnp.sum(partial, axis=(0, 1))
    tail_width = 2 * width
    tail_rows = 8
    tail = jnp.concatenate(
        [dq_sum, kv_sum, jnp.zeros((tail_rows * tail_width - wide - tail_width,), jnp.float32)]
    ).reshape(tail_rows, tail_width)
    spread = jnp.zeros((count, tile, tail_width), jnp.float32).at[targets].add(partial)
    rounded = lax.reduce_precision(tail, exponent_bits=8, mantissa_bits=7)
    high = rounded.astype(jnp.bfloat16)
    low = (tail - rounded).astype(jnp.bfloat16)
    coded = jnp.concatenate([high, low], axis=0)
    spread = jnp.concatenate(
        [spread.astype(jnp.bfloat16), jnp.broadcast_to(coded, (count,) + coded.shape)], axis=1
    )
    landed = exchange(spread, "ctx", True, 1)
    summed = landed[0].astype(jnp.float32)
    for peer in range(1, count):
        summed = summed + landed[peer].astype(jnp.float32)
    summed = jnp.concatenate(
        [summed[:tile], summed[tile:tile + tail_rows] + summed[tile + tail_rows:]], axis=0
    )
    grads = summed[:tile]
    both = exchange(summed[tile:], "dp", False, 2)
    sums = (both[0] + both[1]).reshape(-1) * norm
    sum_q = sums[:wide]
    sum_k = sums[wide:wide + width]
    sum_v = sums[wide + width:wide + 2 * width]
    return (
        dq.astype(jnp.bfloat16)[None],
        grads[:, :width].astype(jnp.bfloat16)[None],
        grads[:, width:].astype(jnp.bfloat16)[None],
        sum_q,
        sum_k,
        sum_v,
    )


def solution(mesh):
    return jax.shard_map(
        on_device,
        mesh=mesh,
        in_specs=(
            P("dp", "ctx", "head"),
            P("dp", "ctx", "head"),
            P("dp", "ctx", "head"),
            P("dp", "ctx", "head"),
            P("dp", "ctx", "head"),
            P("dp", None),
            P("dp", None),
        ),
        out_specs=(
            P("dp", "ctx", "head"),
            P("dp", "ctx", "head"),
            P("dp", "ctx", "head"),
            P("head"),
            P("head"),
            P("head"),
        ),
        check_vma=False,
    )
```

```python
import functools

import jax
import jax.numpy as jnp
from jax import lax
from jax.experimental import pallas as pl
from jax.experimental.pallas import tpu as pltpu
from jax.sharding import PartitionSpec as P

HEAD_WIDTH = 128

NEGATIVE_FILL = -1e30


def pick_entry(vector, index):
    spots = jnp.arange(vector.shape[0], dtype=jnp.int32)
    return jnp.sum(jnp.where(spots == index, vector, 0), axis=0)


def pick_rows(matrix, index):
    spots = jnp.arange(matrix.shape[0], dtype=jnp.int32)
    return jnp.sum(jnp.where((spots == index)[:, None], matrix, 0.0), axis=0)


def attention_grads_kernel(flags_ref, q_ref, g_ref, o_ref, k_ref, v_ref,
                           dq_ref, dk_ref, dv_ref, s_scr, *, slots, scale):
    head = pl.program_id(0)

    @pl.when(head == 0)
    def _():
        dk_ref[...] = jnp.zeros_like(dk_ref)
        dv_ref[...] = jnp.zeros_like(dv_ref)

    q = q_ref[...]
    g = g_ref[...]
    o = o_ref[...]
    rows = q.shape[0]
    delta = jnp.sum(g.astype(jnp.float32) * o.astype(jnp.float32), axis=1, keepdims=True)
    causal = (lax.broadcasted_iota(jnp.int32, (rows, rows), 0)
              >= lax.broadcasted_iota(jnp.int32, (rows, rows), 1))
    nt = (((1,), (1,)), ((), ()))
    tn = (((0,), (0,)), ((), ()))

    top = jnp.full((rows, 1), NEGATIVE_FILL, jnp.float32)
    for j in range(slots):
        keep = flags_ref[j] > 0
        if j == slots - 1:
            keep = jnp.logical_and(keep, causal)
        scores = lax.dot_general(q, k_ref[j], nt, preferred_element_type=jnp.float32) * scale
        scores = jnp.where(keep, scores, NEGATIVE_FILL)
        s_scr[j] = scores
        top = jnp.maximum(top, jnp.max(scores, axis=1, keepdims=True))

    total = jnp.zeros((rows, 1), jnp.float32)
    for j in range(slots):
        keep = flags_ref[j] > 0
        if j == slots - 1:
            keep = jnp.logical_and(keep, causal)
        probs = jnp.where(keep, jnp.exp(s_scr[j] - top), 0.0)
        s_scr[j] = probs
        total = total + jnp.sum(probs, axis=1, keepdims=True)
    inverse = jnp.where(total > 0, 1.0 / jnp.where(total > 0, total, 1.0), 0.0)

    dq = jnp.zeros((rows, q.shape[1]), jnp.float32)
    for j in range(slots):
        probs = s_scr[j] * inverse
        dv_ref[j] += lax.dot_general(probs.astype(jnp.bfloat16), g, tn,
                                     preferred_element_type=jnp.float32)
        dprobs = lax.dot_general(g, v_ref[j], nt, preferred_element_type=jnp.float32)
        dscores = (probs * (dprobs - delta)).astype(jnp.bfloat16)
        dq = dq + jnp.dot(dscores, k_ref[j], preferred_element_type=jnp.float32)
        dk_ref[j] += lax.dot_general(dscores, q, tn, preferred_element_type=jnp.float32) * scale
    dq_ref[...] = dq * scale


def attention_grads(flags, q, g, o, keys, values, scale):
    rows, wide = q.shape
    slots = keys.shape[0]
    heads = wide // HEAD_WIDTH
    col = pl.BlockSpec((rows, HEAD_WIDTH), lambda h, f: (0, h))
    whole = pl.BlockSpec((slots, rows, HEAD_WIDTH), lambda h, f: (0, 0, 0))
    return pl.pallas_call(
        functools.partial(attention_grads_kernel, slots=slots, scale=scale),
        grid_spec=pltpu.PrefetchScalarGridSpec(
            num_scalar_prefetch=1,
            grid=(heads,),
            in_specs=[col, col, col, whole, whole],
            out_specs=[col, whole, whole],
            scratch_shapes=[pltpu.VMEM((slots, rows, rows), jnp.float32)],
        ),
        out_shape=[
            jax.ShapeDtypeStruct((rows, wide), jnp.float32),
            jax.ShapeDtypeStruct((slots, rows, HEAD_WIDTH), jnp.float32),
            jax.ShapeDtypeStruct((slots, rows, HEAD_WIDTH), jnp.float32),
        ],
        compiler_params=pltpu.CompilerParams(
            dimension_semantics=("arbitrary",), vmem_limit_bytes=48 * 1024 * 1024
        ),
    )(flags, q, g, o, keys, values)


def exchange_kernel(x_ref, out_ref, send_sem, recv_sem, self_sem, *, axis, n, indexed):
    me = lax.axis_index(axis)
    barrier = pltpu.get_barrier_semaphore()
    for d in range(1, n):
        pl.semaphore_signal(
            barrier, inc=1, device_id={axis: lax.rem(me + d, n)},
            device_id_type=pl.DeviceIdType.MESH,
        )
    pl.semaphore_wait(barrier, n - 1)
    copies = []
    for d in range(1, n):
        peer = lax.rem(me + d, n)
        copy = pltpu.make_async_remote_copy(
            src_ref=x_ref.at[peer] if indexed else x_ref,
            dst_ref=out_ref.at[me],
            send_sem=send_sem.at[d - 1],
            recv_sem=recv_sem.at[d - 1],
            device_id={axis: peer},
            device_id_type=pl.DeviceIdType.MESH,
        )
        copy.start()
        copies.append(copy)
    local = pltpu.make_async_copy(x_ref.at[me] if indexed else x_ref, out_ref.at[me], self_sem)
    local.start()
    for copy in copies:
        copy.wait_send()
    for copy in copies:
        copy.wait_recv()
    local.wait()


def exchange(x, axis, indexed, collective_id):
    n = lax.axis_size(axis)
    piece = x.shape[1:] if indexed else x.shape
    return pl.pallas_call(
        functools.partial(exchange_kernel, axis=axis, n=n, indexed=indexed),
        out_shape=jax.ShapeDtypeStruct((n,) + tuple(piece), x.dtype),
        in_specs=[pl.BlockSpec(memory_space=pl.ANY)],
        out_specs=pl.BlockSpec(memory_space=pl.ANY),
        scratch_shapes=[
            pltpu.SemaphoreType.DMA((n - 1,)),
            pltpu.SemaphoreType.DMA((n - 1,)),
            pltpu.SemaphoreType.DMA,
        ],
        compiler_params=pltpu.CompilerParams(collective_id=collective_id, has_side_effects=True),
    )(x)


def relay_gather_kernel(x_ref, out_ref, send_sem, recv_sem, self_sem, *, n):
    me = lax.axis_index("ctx")
    ring = n // 2
    z = me // 2
    side = me % 2
    partner = z * 2 + (1 - side)
    up = lax.rem(z + 1, ring) * 2 + side
    down = lax.rem(z + ring - 1, ring) * 2 + side
    barrier = pltpu.get_barrier_semaphore()
    for peer in (partner, up, down):
        pl.semaphore_signal(barrier, inc=1, device_id={"ctx": peer},
                            device_id_type=pl.DeviceIdType.MESH)
    pl.semaphore_wait(barrier, 3)
    local = pltpu.make_async_copy(x_ref, out_ref.at[me], self_sem)
    local.start()
    sends = []

    def send(slot, target, src):
        copy = pltpu.make_async_remote_copy(
            src_ref=src, dst_ref=out_ref.at[slot], send_sem=send_sem.at[len(sends)],
            recv_sem=recv_sem.at[slot], device_id={"ctx": target},
            device_id_type=pl.DeviceIdType.MESH,
        )
        copy.start()
        sends.append(copy)

    def arrive(slot):
        pltpu.make_async_remote_copy(
            src_ref=x_ref, dst_ref=out_ref.at[slot], send_sem=send_sem.at[0],
            recv_sem=recv_sem.at[slot], device_id={"ctx": partner},
            device_id_type=pl.DeviceIdType.MESH,
        ).wait_recv()

    def origin(step, offset):
        return lax.rem(z + step + ring, ring) * 2 + offset

    upward = ring // 2
    downward = ring - 1 - upward
    send(me, partner, x_ref)
    send(me, up, x_ref)
    send(me, down, x_ref)
    arrive(partner)
    send(partner, up, out_ref.at[partner])
    send(partner, down, out_ref.at[partner])
    for step in range(2, upward + 1):
        for offset in (0, 1):
            slot = origin(-(step - 1), offset)
            arrive(slot)
            send(slot, up, out_ref.at[slot])
        if step <= downward:
            for offset in (0, 1):
                slot = origin(step - 1, offset)
                arrive(slot)
                send(slot, down, out_ref.at[slot])
    for offset in (0, 1):
        arrive(origin(-upward, offset))
    for offset in (0, 1):
        arrive(origin(downward, offset))
    for copy in sends:
        copy.wait_send()
    local.wait()


def relay_gather(x, collective_id):
    n = lax.axis_size("ctx")
    return pl.pallas_call(
        functools.partial(relay_gather_kernel, n=n),
        out_shape=jax.ShapeDtypeStruct((n,) + tuple(x.shape), x.dtype),
        in_specs=[pl.BlockSpec(memory_space=pl.ANY)],
        out_specs=pl.BlockSpec(memory_space=pl.ANY),
        scratch_shapes=[
            pltpu.SemaphoreType.DMA((n - 1,)),
            pltpu.SemaphoreType.DMA((n,)),
            pltpu.SemaphoreType.DMA,
        ],
        compiler_params=pltpu.CompilerParams(collective_id=collective_id, has_side_effects=True),
    )(x)


def on_device(query, key, value, output, output_gradient, parent, owner):
    count = lax.axis_size("ctx")
    me = lax.axis_index("ctx")
    tile = query.shape[1]
    width = key.shape[2]
    scale_factor = HEAD_WIDTH ** (-0.5)
    prompt_tiles = count // 8
    parent_row = parent[0]
    owner_row = owner[0]
    tiles = jnp.arange(count, dtype=jnp.int32)
    my_tile = jnp.sum(jnp.where(owner_row == me, tiles, 0))
    trained = my_tile >= prompt_tiles
    above = pick_entry(parent_row, my_tile)
    second = jnp.logical_and(trained, above >= prompt_tiles)
    slot_tiles = jnp.stack(
        [jnp.int32(0), jnp.int32(1), jnp.where(second, above, 1).astype(jnp.int32)]
    )
    slot_blocks = jnp.sum(
        jnp.where(slot_tiles[:, None] == tiles[None, :], owner_row[None, :], 0), axis=1
    ).astype(jnp.int32)
    flags = jnp.stack([trained, trained, second, trained]).astype(jnp.int32)

    pair = jnp.concatenate([key[0], value[0]], axis=1)
    gathered = relay_gather(pair, 0)
    picked = gathered[slot_blocks]
    keys = jnp.concatenate([picked[:, :, :width], key[0][None]], axis=0)
    values = jnp.concatenate([picked[:, :, width:], value[0][None]], axis=0)

    dq, dk, dv = attention_grads(
        flags, query[0], output_gradient[0], output[0], keys, values, scale_factor
    )
    partial = jnp.concatenate([dk, dv], axis=2)
    targets = jnp.concatenate([slot_blocks, me[None].astype(jnp.int32)])
    total_rows = lax.axis_size("dp") * query.shape[0] * count * tile
    norm = total_rows ** (-0.5)
    wide = query.shape[2]
    dq_sum = jnp.sum(dq, axis=0)
    kv_sum = jnp.sum(partial, axis=(0, 1))
    tail_width = 2 * width
    tail_rows = 8
    tail = jnp.concatenate(
        [dq_sum, kv_sum, jnp.zeros((tail_rows * tail_width - wide - tail_width,), jnp.float32)]
    ).reshape(tail_rows, tail_width)
    spread = jnp.zeros((count, tile, tail_width), jnp.float32).at[targets].add(partial)
    rounded = lax.reduce_precision(tail, exponent_bits=8, mantissa_bits=7)
    high = rounded.astype(jnp.bfloat16)
    low = (tail - rounded).astype(jnp.bfloat16)
    coded = jnp.concatenate([high, low], axis=0)
    spread = jnp.concatenate(
        [spread.astype(jnp.bfloat16), jnp.broadcast_to(coded, (count,) + coded.shape)], axis=1
    )
    landed = exchange(spread, "ctx", True, 1)
    summed = landed[0].astype(jnp.float32)
    for peer in range(1, count):
        summed = summed + landed[peer].astype(jnp.float32)
    summed = jnp.concatenate(
        [summed[:tile], summed[tile:tile + tail_rows] + summed[tile + tail_rows:]], axis=0
    )
    grads = summed[:tile]
    both = exchange(summed[tile:], "dp", False, 2)
    sums = (both[0] + both[1]).reshape(-1) * norm
    sum_q = sums[:wide]
    sum_k = sums[wide:wide + width]
    sum_v = sums[wide + width:wide + 2 * width]
    return (
        dq.astype(jnp.bfloat16)[None],
        grads[:, :width].astype(jnp.bfloat16)[None],
        grads[:, width:].astype(jnp.bfloat16)[None],
        sum_q,
        sum_k,
        sum_v,
    )


def solution(mesh):
    return jax.shard_map(
        on_device,
        mesh=mesh,
        in_specs=(
            P("dp", "ctx", "head"),
            P("dp", "ctx", "head"),
            P("dp", "ctx", "head"),
            P("dp", "ctx", "head"),
            P("dp", "ctx", "head"),
            P("dp", None),
            P("dp", None),
        ),
        out_specs=(
            P("dp", "ctx", "head"),
            P("dp", "ctx", "head"),
            P("dp", "ctx", "head"),
            P("head"),
            P("head"),
            P("head"),
        ),
        check_vma=False,
    )
```

```python
import functools

import jax
import jax.numpy as jnp
from jax import lax
from jax.experimental import pallas as pl
from jax.experimental.pallas import tpu as pltpu
from jax.sharding import PartitionSpec as P

HEAD_WIDTH = 128

NEGATIVE_FILL = -1e30


def pick_entry(vector, index):
    spots = jnp.arange(vector.shape[0], dtype=jnp.int32)
    return jnp.sum(jnp.where(spots == index, vector, 0), axis=0)


def pick_rows(matrix, index):
    spots = jnp.arange(matrix.shape[0], dtype=jnp.int32)
    return jnp.sum(jnp.where((spots == index)[:, None], matrix, 0.0), axis=0)


def attention_grads_kernel(flags_ref, q_ref, g_ref, o_ref, k_ref, v_ref,
                           dq_ref, dk_ref, dv_ref, s_scr, *, slots, scale):
    head = pl.program_id(0)

    @pl.when(head == 0)
    def _():
        dk_ref[...] = jnp.zeros_like(dk_ref)
        dv_ref[...] = jnp.zeros_like(dv_ref)

    q = q_ref[...]
    g = g_ref[...]
    o = o_ref[...]
    rows = q.shape[0]
    delta = jnp.sum(g.astype(jnp.float32) * o.astype(jnp.float32), axis=1, keepdims=True)
    causal = (lax.broadcasted_iota(jnp.int32, (rows, rows), 0)
              >= lax.broadcasted_iota(jnp.int32, (rows, rows), 1))
    nt = (((1,), (1,)), ((), ()))
    tn = (((0,), (0,)), ((), ()))

    top = jnp.full((rows, 1), NEGATIVE_FILL, jnp.float32)
    for j in range(slots):
        keep = flags_ref[j] > 0
        if j == slots - 1:
            keep = jnp.logical_and(keep, causal)
        scores = lax.dot_general(q, k_ref[j], nt, preferred_element_type=jnp.float32) * scale
        scores = jnp.where(keep, scores, NEGATIVE_FILL)
        s_scr[j] = scores
        top = jnp.maximum(top, jnp.max(scores, axis=1, keepdims=True))

    total = jnp.zeros((rows, 1), jnp.float32)
    for j in range(slots):
        keep = flags_ref[j] > 0
        if j == slots - 1:
            keep = jnp.logical_and(keep, causal)
        probs = jnp.where(keep, jnp.exp(s_scr[j] - top), 0.0)
        s_scr[j] = probs
        total = total + jnp.sum(probs, axis=1, keepdims=True)
    inverse = jnp.where(total > 0, 1.0 / jnp.where(total > 0, total, 1.0), 0.0)

    dq = jnp.zeros((rows, q.shape[1]), jnp.float32)
    for j in range(slots):
        probs = s_scr[j] * inverse
        dv_ref[j] += lax.dot_general(probs.astype(jnp.bfloat16), g, tn,
                                     preferred_element_type=jnp.float32)
        dprobs = lax.dot_general(g, v_ref[j], nt, preferred_element_type=jnp.float32)
        dscores = (probs * (dprobs - delta)).astype(jnp.bfloat16)
        dq = dq + jnp.dot(dscores, k_ref[j], preferred_element_type=jnp.float32)
        dk_ref[j] += lax.dot_general(dscores, q, tn, preferred_element_type=jnp.float32) * scale
    dq_ref[...] = dq * scale


def attention_grads(flags, q, g, o, keys, values, scale):
    rows, wide = q.shape
    slots = keys.shape[0]
    heads = wide // HEAD_WIDTH
    col = pl.BlockSpec((rows, HEAD_WIDTH), lambda h, f: (0, h))
    whole = pl.BlockSpec((slots, rows, HEAD_WIDTH), lambda h, f: (0, 0, 0))
    return pl.pallas_call(
        functools.partial(attention_grads_kernel, slots=slots, scale=scale),
        grid_spec=pltpu.PrefetchScalarGridSpec(
            num_scalar_prefetch=1,
            grid=(heads,),
            in_specs=[col, col, col, whole, whole],
            out_specs=[col, whole, whole],
            scratch_shapes=[pltpu.VMEM((slots, rows, rows), jnp.float32)],
        ),
        out_shape=[
            jax.ShapeDtypeStruct((rows, wide), jnp.float32),
            jax.ShapeDtypeStruct((slots, rows, HEAD_WIDTH), jnp.float32),
            jax.ShapeDtypeStruct((slots, rows, HEAD_WIDTH), jnp.float32),
        ],
        compiler_params=pltpu.CompilerParams(
            dimension_semantics=("arbitrary",), vmem_limit_bytes=48 * 1024 * 1024
        ),
    )(flags, q, g, o, keys, values)


def exchange_kernel(x_ref, out_ref, send_sem, recv_sem, self_sem, *, axis, n, indexed):
    me = lax.axis_index(axis)
    barrier = pltpu.get_barrier_semaphore()
    for d in range(1, n):
        pl.semaphore_signal(
            barrier, inc=1, device_id={axis: lax.rem(me + d, n)},
            device_id_type=pl.DeviceIdType.MESH,
        )
    pl.semaphore_wait(barrier, n - 1)
    copies = []
    for d in range(1, n):
        peer = lax.rem(me + d, n)
        copy = pltpu.make_async_remote_copy(
            src_ref=x_ref.at[peer] if indexed else x_ref,
            dst_ref=out_ref.at[me],
            send_sem=send_sem.at[d - 1],
            recv_sem=recv_sem.at[d - 1],
            device_id={axis: peer},
            device_id_type=pl.DeviceIdType.MESH,
        )
        copy.start()
        copies.append(copy)
    local = pltpu.make_async_copy(x_ref.at[me] if indexed else x_ref, out_ref.at[me], self_sem)
    local.start()
    for copy in copies:
        copy.wait_send()
    for copy in copies:
        copy.wait_recv()
    local.wait()


def exchange(x, axis, indexed, collective_id):
    n = lax.axis_size(axis)
    piece = x.shape[1:] if indexed else x.shape
    return pl.pallas_call(
        functools.partial(exchange_kernel, axis=axis, n=n, indexed=indexed),
        out_shape=jax.ShapeDtypeStruct((n,) + tuple(piece), x.dtype),
        in_specs=[pl.BlockSpec(memory_space=pl.ANY)],
        out_specs=pl.BlockSpec(memory_space=pl.ANY),
        scratch_shapes=[
            pltpu.SemaphoreType.DMA((n - 1,)),
            pltpu.SemaphoreType.DMA((n - 1,)),
            pltpu.SemaphoreType.DMA,
        ],
        compiler_params=pltpu.CompilerParams(collective_id=collective_id, has_side_effects=True),
    )(x)


def relay_gather_kernel(x_ref, out_ref, send_sem, recv_sem, self_sem, *, n):
    me = lax.axis_index("ctx")
    ring = n // 2
    z = me // 2
    side = me % 2
    partner = z * 2 + (1 - side)
    up = lax.rem(z + 1, ring) * 2 + side
    down = lax.rem(z + ring - 1, ring) * 2 + side
    barrier = pltpu.get_barrier_semaphore()
    for peer in (partner, up, down):
        pl.semaphore_signal(barrier, inc=1, device_id={"ctx": peer},
                            device_id_type=pl.DeviceIdType.MESH)
    pl.semaphore_wait(barrier, 3)
    local = pltpu.make_async_copy(x_ref, out_ref.at[me], self_sem)
    local.start()
    sends = []

    def send(slot, target, src):
        copy = pltpu.make_async_remote_copy(
            src_ref=src, dst_ref=out_ref.at[slot], send_sem=send_sem.at[len(sends)],
            recv_sem=recv_sem.at[slot], device_id={"ctx": target},
            device_id_type=pl.DeviceIdType.MESH,
        )
        copy.start()
        sends.append(copy)

    def arrive(slot):
        pltpu.make_async_remote_copy(
            src_ref=x_ref, dst_ref=out_ref.at[slot], send_sem=send_sem.at[0],
            recv_sem=recv_sem.at[slot], device_id={"ctx": partner},
            device_id_type=pl.DeviceIdType.MESH,
        ).wait_recv()

    def origin(step, offset):
        return lax.rem(z + step + ring, ring) * 2 + offset

    upward = ring // 2
    downward = ring - 1 - upward
    send(me, partner, x_ref)
    send(me, up, x_ref)
    send(me, down, x_ref)
    arrive(partner)
    send(partner, up, out_ref.at[partner])
    send(partner, down, out_ref.at[partner])
    for step in range(2, upward + 1):
        for offset in (0, 1):
            slot = origin(-(step - 1), offset)
            arrive(slot)
            send(slot, up, out_ref.at[slot])
        if step <= downward:
            for offset in (0, 1):
                slot = origin(step - 1, offset)
                arrive(slot)
                send(slot, down, out_ref.at[slot])
    for offset in (0, 1):
        arrive(origin(-upward, offset))
    for offset in (0, 1):
        arrive(origin(downward, offset))
    for copy in sends:
        copy.wait_send()
    local.wait()


def relay_gather(x, collective_id):
    n = lax.axis_size("ctx")
    return pl.pallas_call(
        functools.partial(relay_gather_kernel, n=n),
        out_shape=jax.ShapeDtypeStruct((n,) + tuple(x.shape), x.dtype),
        in_specs=[pl.BlockSpec(memory_space=pl.ANY)],
        out_specs=pl.BlockSpec(memory_space=pl.ANY),
        scratch_shapes=[
            pltpu.SemaphoreType.DMA((n - 1,)),
            pltpu.SemaphoreType.DMA((n,)),
            pltpu.SemaphoreType.DMA,
        ],
        compiler_params=pltpu.CompilerParams(collective_id=collective_id, has_side_effects=True),
    )(x)


def relay_reduce_kernel(x_ref, out_ref, up_in, down_in, up_out, down_out, side_out, side_in,
                        send_sem, recv_sem, *, n):
    me = lax.axis_index("ctx")
    ring = n // 2
    z = me // 2
    side = me % 2
    partner = z * 2 + (1 - side)
    up = lax.rem(z + 1, ring) * 2 + side
    down = lax.rem(z + ring - 1, ring) * 2 + side
    upward = ring // 2
    downward = ring - 1 - upward
    barrier = pltpu.get_barrier_semaphore()
    for peer in (partner, up, down):
        pl.semaphore_signal(barrier, inc=1, device_id={"ctx": peer},
                            device_id_type=pl.DeviceIdType.MESH)
    pl.semaphore_wait(barrier, 3)
    sends = []

    def send(src, dst, target, sem_index):
        copy = pltpu.make_async_remote_copy(
            src_ref=src, dst_ref=dst, send_sem=send_sem.at[len(sends)],
            recv_sem=recv_sem.at[sem_index], device_id={"ctx": target},
            device_id_type=pl.DeviceIdType.MESH,
        )
        copy.start()
        sends.append(copy)
        return copy

    def own(target_z):
        block = pl.multiple_of(lax.rem(target_z + 2 * ring, ring) * 2, 2)
        return x_ref[pl.ds(block, 2)]

    pending_up = None
    pending_down = None
    for step in range(1, upward + 1):
        term = own(z + upward - step + 1)
        if pending_up is not None:
            pending_up.wait_recv()
            term = term + up_in[step - 2].astype(jnp.float32)
        up_out[step - 1] = term.astype(up_out.dtype)
        pending_up = send(up_out.at[step - 1], up_in.at[step - 1], up, step - 1)
        if step <= downward:
            term = own(z - (downward - step + 1))
            if pending_down is not None:
                pending_down.wait_recv()
                term = term + down_in[step - 2].astype(jnp.float32)
            down_out[step - 1] = term.astype(down_out.dtype)
            pending_down = send(down_out.at[step - 1], down_in.at[step - 1], down,
                                upward + step - 1)
    pending_up.wait_recv()
    pending_down.wait_recv()
    mine = (own(z) + up_in[upward - 1].astype(jnp.float32)
            + down_in[downward - 1].astype(jnp.float32))
    side_out[...] = jnp.where(side == 0, mine[1], mine[0])
    across = send(side_out, side_in, partner, upward + downward)
    across.wait_recv()
    out_ref[...] = jnp.where(side == 0, mine[0], mine[1]) + side_in[...]
    for copy in sends:
        copy.wait_send()


def relay_reduce(x, collective_id):
    n, rows, cols = x.shape
    ring = n // 2
    upward = ring // 2
    downward = ring - 1 - upward
    vmem = pl.BlockSpec(memory_space=pltpu.VMEM)
    return pl.pallas_call(
        functools.partial(relay_reduce_kernel, n=n),
        out_shape=jax.ShapeDtypeStruct((rows, cols), jnp.float32),
        in_specs=[vmem],
        out_specs=vmem,
        scratch_shapes=[
            pltpu.VMEM((upward, 2, rows, cols), jnp.bfloat16),
            pltpu.VMEM((downward, 2, rows, cols), jnp.bfloat16),
            pltpu.VMEM((upward, 2, rows, cols), jnp.bfloat16),
            pltpu.VMEM((downward, 2, rows, cols), jnp.bfloat16),
            pltpu.VMEM((rows, cols), jnp.float32),
            pltpu.VMEM((rows, cols), jnp.float32),
            pltpu.SemaphoreType.DMA((upward + downward + 1,)),
            pltpu.SemaphoreType.DMA((upward + downward + 1,)),
        ],
        compiler_params=pltpu.CompilerParams(
            collective_id=collective_id, has_side_effects=True,
            vmem_limit_bytes=56 * 1024 * 1024,
        ),
    )(x)


def on_device(query, key, value, output, output_gradient, parent, owner):
    count = lax.axis_size("ctx")
    me = lax.axis_index("ctx")
    tile = query.shape[1]
    width = key.shape[2]
    scale_factor = HEAD_WIDTH ** (-0.5)
    prompt_tiles = count // 8
    parent_row = parent[0]
    owner_row = owner[0]
    tiles = jnp.arange(count, dtype=jnp.int32)
    my_tile = jnp.sum(jnp.where(owner_row == me, tiles, 0))
    trained = my_tile >= prompt_tiles
    above = pick_entry(parent_row, my_tile)
    second = jnp.logical_and(trained, above >= prompt_tiles)
    slot_tiles = jnp.stack(
        [jnp.int32(0), jnp.int32(1), jnp.where(second, above, 1).astype(jnp.int32)]
    )
    slot_blocks = jnp.sum(
        jnp.where(slot_tiles[:, None] == tiles[None, :], owner_row[None, :], 0), axis=1
    ).astype(jnp.int32)
    flags = jnp.stack([trained, trained, second, trained]).astype(jnp.int32)

    pair = jnp.concatenate([key[0], value[0]], axis=1)
    gathered = relay_gather(pair, 0)
    picked = gathered[slot_blocks]
    keys = jnp.concatenate([picked[:, :, :width], key[0][None]], axis=0)
    values = jnp.concatenate([picked[:, :, width:], value[0][None]], axis=0)

    dq, dk, dv = attention_grads(
        flags, query[0], output_gradient[0], output[0], keys, values, scale_factor
    )
    partial = jnp.concatenate([dk, dv], axis=2)
    targets = jnp.concatenate([slot_blocks, me[None].astype(jnp.int32)])
    total_rows = lax.axis_size("dp") * query.shape[0] * count * tile
    norm = total_rows ** (-0.5)
    wide = query.shape[2]
    dq_sum = jnp.sum(dq, axis=0)
    kv_sum = jnp.sum(partial, axis=(0, 1))
    tail_width = 2 * width
    tail_rows = 8
    tail = jnp.concatenate(
        [dq_sum, kv_sum, jnp.zeros((tail_rows * tail_width - wide - tail_width,), jnp.float32)]
    ).reshape(tail_rows, tail_width)
    spread = jnp.zeros((count, tile, tail_width), jnp.float32).at[targets].add(partial)
    grads = relay_reduce(spread, 1)
    landed = exchange(tail, "ctx", False, 3)
    summed = landed[0]
    for peer in range(1, count):
        summed = summed + landed[peer]
    both = exchange(summed, "dp", False, 2)
    sums = (both[0] + both[1]).reshape(-1) * norm
    sum_q = sums[:wide]
    sum_k = sums[wide:wide + width]
    sum_v = sums[wide + width:wide + 2 * width]
    return (
        dq.astype(jnp.bfloat16)[None],
        grads[:, :width].astype(jnp.bfloat16)[None],
        grads[:, width:].astype(jnp.bfloat16)[None],
        sum_q,
        sum_k,
        sum_v,
    )


def solution(mesh):
    return jax.shard_map(
        on_device,
        mesh=mesh,
        in_specs=(
            P("dp", "ctx", "head"),
            P("dp", "ctx", "head"),
            P("dp", "ctx", "head"),
            P("dp", "ctx", "head"),
            P("dp", "ctx", "head"),
            P("dp", None),
            P("dp", None),
        ),
        out_specs=(
            P("dp", "ctx", "head"),
            P("dp", "ctx", "head"),
            P("dp", "ctx", "head"),
            P("head"),
            P("head"),
            P("head"),
        ),
        check_vma=False,
    )
```

```python
import functools

import jax
import jax.numpy as jnp
from jax import lax
from jax.experimental import pallas as pl
from jax.experimental.pallas import tpu as pltpu
from jax.sharding import PartitionSpec as P

HEAD_WIDTH = 128

NEGATIVE_FILL = -1e30


def pick_entry(vector, index):
    spots = jnp.arange(vector.shape[0], dtype=jnp.int32)
    return jnp.sum(jnp.where(spots == index, vector, 0), axis=0)


def pick_rows(matrix, index):
    spots = jnp.arange(matrix.shape[0], dtype=jnp.int32)
    return jnp.sum(jnp.where((spots == index)[:, None], matrix, 0.0), axis=0)


def attention_grads_kernel(flags_ref, q_ref, g_ref, o_ref, k_ref, v_ref,
                           dq_ref, dk_ref, dv_ref, s_scr, *, slots, scale):
    head = pl.program_id(0)

    @pl.when(head == 0)
    def _():
        dk_ref[...] = jnp.zeros_like(dk_ref)
        dv_ref[...] = jnp.zeros_like(dv_ref)

    q = q_ref[...]
    g = g_ref[...]
    o = o_ref[...]
    rows = q.shape[0]
    delta = jnp.sum(g.astype(jnp.float32) * o.astype(jnp.float32), axis=1, keepdims=True)
    causal = (lax.broadcasted_iota(jnp.int32, (rows, rows), 0)
              >= lax.broadcasted_iota(jnp.int32, (rows, rows), 1))
    nt = (((1,), (1,)), ((), ()))
    tn = (((0,), (0,)), ((), ()))

    top = jnp.full((rows, 1), NEGATIVE_FILL, jnp.float32)
    for j in range(slots):
        keep = flags_ref[j] > 0
        if j == slots - 1:
            keep = jnp.logical_and(keep, causal)
        scores = lax.dot_general(q, k_ref[j], nt, preferred_element_type=jnp.float32) * scale
        scores = jnp.where(keep, scores, NEGATIVE_FILL)
        s_scr[j] = scores
        top = jnp.maximum(top, jnp.max(scores, axis=1, keepdims=True))

    total = jnp.zeros((rows, 1), jnp.float32)
    for j in range(slots):
        keep = flags_ref[j] > 0
        if j == slots - 1:
            keep = jnp.logical_and(keep, causal)
        probs = jnp.where(keep, jnp.exp(s_scr[j] - top), 0.0)
        s_scr[j] = probs
        total = total + jnp.sum(probs, axis=1, keepdims=True)
    inverse = jnp.where(total > 0, 1.0 / jnp.where(total > 0, total, 1.0), 0.0)

    dq = jnp.zeros((rows, q.shape[1]), jnp.float32)
    for j in range(slots):
        probs = s_scr[j] * inverse
        dv_ref[j] += lax.dot_general(probs.astype(jnp.bfloat16), g, tn,
                                     preferred_element_type=jnp.float32)
        dprobs = lax.dot_general(g, v_ref[j], nt, preferred_element_type=jnp.float32)
        dscores = (probs * (dprobs - delta)).astype(jnp.bfloat16)
        dq = dq + jnp.dot(dscores, k_ref[j], preferred_element_type=jnp.float32)
        dk_ref[j] += lax.dot_general(dscores, q, tn, preferred_element_type=jnp.float32) * scale
    dq_ref[...] = dq * scale


def attention_grads(flags, q, g, o, keys, values, scale):
    rows, wide = q.shape
    slots = keys.shape[0]
    heads = wide // HEAD_WIDTH
    col = pl.BlockSpec((rows, HEAD_WIDTH), lambda h, f: (0, h))
    whole = pl.BlockSpec((slots, rows, HEAD_WIDTH), lambda h, f: (0, 0, 0))
    return pl.pallas_call(
        functools.partial(attention_grads_kernel, slots=slots, scale=scale),
        grid_spec=pltpu.PrefetchScalarGridSpec(
            num_scalar_prefetch=1,
            grid=(heads,),
            in_specs=[col, col, col, whole, whole],
            out_specs=[col, whole, whole],
            scratch_shapes=[pltpu.VMEM((slots, rows, rows), jnp.float32)],
        ),
        out_shape=[
            jax.ShapeDtypeStruct((rows, wide), jnp.float32),
            jax.ShapeDtypeStruct((slots, rows, HEAD_WIDTH), jnp.float32),
            jax.ShapeDtypeStruct((slots, rows, HEAD_WIDTH), jnp.float32),
        ],
        compiler_params=pltpu.CompilerParams(
            dimension_semantics=("arbitrary",), vmem_limit_bytes=48 * 1024 * 1024
        ),
    )(flags, q, g, o, keys, values)


def exchange_kernel(x_ref, out_ref, send_sem, recv_sem, self_sem, *, axis, n, indexed):
    me = lax.axis_index(axis)
    barrier = pltpu.get_barrier_semaphore()
    for d in range(1, n):
        pl.semaphore_signal(
            barrier, inc=1, device_id={axis: lax.rem(me + d, n)},
            device_id_type=pl.DeviceIdType.MESH,
        )
    pl.semaphore_wait(barrier, n - 1)
    copies = []
    for d in range(1, n):
        peer = lax.rem(me + d, n)
        copy = pltpu.make_async_remote_copy(
            src_ref=x_ref.at[peer] if indexed else x_ref,
            dst_ref=out_ref.at[me],
            send_sem=send_sem.at[d - 1],
            recv_sem=recv_sem.at[d - 1],
            device_id={axis: peer},
            device_id_type=pl.DeviceIdType.MESH,
        )
        copy.start()
        copies.append(copy)
    local = pltpu.make_async_copy(x_ref.at[me] if indexed else x_ref, out_ref.at[me], self_sem)
    local.start()
    for copy in copies:
        copy.wait_send()
    for copy in copies:
        copy.wait_recv()
    local.wait()


def exchange(x, axis, indexed, collective_id):
    n = lax.axis_size(axis)
    piece = x.shape[1:] if indexed else x.shape
    return pl.pallas_call(
        functools.partial(exchange_kernel, axis=axis, n=n, indexed=indexed),
        out_shape=jax.ShapeDtypeStruct((n,) + tuple(piece), x.dtype),
        in_specs=[pl.BlockSpec(memory_space=pl.ANY)],
        out_specs=pl.BlockSpec(memory_space=pl.ANY),
        scratch_shapes=[
            pltpu.SemaphoreType.DMA((n - 1,)),
            pltpu.SemaphoreType.DMA((n - 1,)),
            pltpu.SemaphoreType.DMA,
        ],
        compiler_params=pltpu.CompilerParams(collective_id=collective_id, has_side_effects=True),
    )(x)


def relay_gather_kernel(x_ref, out_ref, send_sem, recv_sem, self_sem, *, n):
    me = lax.axis_index("ctx")
    ring = n // 2
    z = me // 2
    side = me % 2
    partner = z * 2 + (1 - side)
    up = lax.rem(z + 1, ring) * 2 + side
    down = lax.rem(z + ring - 1, ring) * 2 + side
    barrier = pltpu.get_barrier_semaphore()
    for peer in (partner, up, down):
        pl.semaphore_signal(barrier, inc=1, device_id={"ctx": peer},
                            device_id_type=pl.DeviceIdType.MESH)
    pl.semaphore_wait(barrier, 3)
    local = pltpu.make_async_copy(x_ref, out_ref.at[me], self_sem)
    local.start()
    sends = []

    def send(slot, target, src):
        copy = pltpu.make_async_remote_copy(
            src_ref=src, dst_ref=out_ref.at[slot], send_sem=send_sem.at[len(sends)],
            recv_sem=recv_sem.at[slot], device_id={"ctx": target},
            device_id_type=pl.DeviceIdType.MESH,
        )
        copy.start()
        sends.append(copy)

    def arrive(slot):
        pltpu.make_async_remote_copy(
            src_ref=x_ref, dst_ref=out_ref.at[slot], send_sem=send_sem.at[0],
            recv_sem=recv_sem.at[slot], device_id={"ctx": partner},
            device_id_type=pl.DeviceIdType.MESH,
        ).wait_recv()

    def origin(step, offset):
        return lax.rem(z + step + ring, ring) * 2 + offset

    upward = ring // 2
    downward = ring - 1 - upward
    send(me, partner, x_ref)
    send(me, up, x_ref)
    send(me, down, x_ref)
    arrive(partner)
    send(partner, up, out_ref.at[partner])
    send(partner, down, out_ref.at[partner])
    for step in range(2, upward + 1):
        for offset in (0, 1):
            slot = origin(-(step - 1), offset)
            arrive(slot)
            send(slot, up, out_ref.at[slot])
        if step <= downward:
            for offset in (0, 1):
                slot = origin(step - 1, offset)
                arrive(slot)
                send(slot, down, out_ref.at[slot])
    for offset in (0, 1):
        arrive(origin(-upward, offset))
    for offset in (0, 1):
        arrive(origin(downward, offset))
    for copy in sends:
        copy.wait_send()
    local.wait()


def relay_gather(x, collective_id):
    n = lax.axis_size("ctx")
    return pl.pallas_call(
        functools.partial(relay_gather_kernel, n=n),
        out_shape=jax.ShapeDtypeStruct((n,) + tuple(x.shape), x.dtype),
        in_specs=[pl.BlockSpec(memory_space=pl.ANY)],
        out_specs=pl.BlockSpec(memory_space=pl.ANY),
        scratch_shapes=[
            pltpu.SemaphoreType.DMA((n - 1,)),
            pltpu.SemaphoreType.DMA((n,)),
            pltpu.SemaphoreType.DMA,
        ],
        compiler_params=pltpu.CompilerParams(collective_id=collective_id, has_side_effects=True),
    )(x)


def relay_reduce_kernel(t_ref, x_ref, tail_ref, out_ref, tails_ref, up_in, down_in, up_out,
                        down_out, side_out, side_in, tails_in, send_sem, recv_sem, tail_send,
                        tail_recv, *, n):
    me = lax.axis_index("ctx")
    ring = n // 2
    z = me // 2
    side = me % 2
    partner = z * 2 + (1 - side)
    up = lax.rem(z + 1, ring) * 2 + side
    down = lax.rem(z + ring - 1, ring) * 2 + side
    upward = ring // 2
    downward = ring - 1 - upward
    barrier = pltpu.get_barrier_semaphore()
    for d in range(1, n):
        pl.semaphore_signal(barrier, inc=1, device_id={"ctx": lax.rem(me + d, n)},
                            device_id_type=pl.DeviceIdType.MESH)
    pl.semaphore_wait(barrier, n - 1)
    tail_copies = []
    for d in range(1, n):
        copy = pltpu.make_async_remote_copy(
            src_ref=tail_ref, dst_ref=tails_in.at[me], send_sem=tail_send.at[d - 1],
            recv_sem=tail_recv.at[d - 1], device_id={"ctx": lax.rem(me + d, n)},
            device_id_type=pl.DeviceIdType.MESH,
        )
        copy.start()
        tail_copies.append(copy)
    tails_in[me] = tail_ref[...]
    sends = []

    def send(src, dst, target, sem_index):
        copy = pltpu.make_async_remote_copy(
            src_ref=src, dst_ref=dst, send_sem=send_sem.at[len(sends)],
            recv_sem=recv_sem.at[sem_index], device_id={"ctx": target},
            device_id_type=pl.DeviceIdType.MESH,
        )
        copy.start()
        sends.append(copy)
        return copy

    def own(target_z):
        base = lax.rem(target_z + 2 * ring, ring) * 2
        pieces = []
        for offset in (0, 1):
            total = jnp.zeros(x_ref.shape[1:], jnp.float32)
            for j in range(x_ref.shape[0]):
                total = total + jnp.where(t_ref[j] == base + offset, x_ref[j], 0.0)
            pieces.append(total)
        return jnp.stack(pieces)

    pending_up = None
    pending_down = None
    for step in range(1, upward + 1):
        term = own(z + upward - step + 1)
        if pending_up is not None:
            pending_up.wait_recv()
            term = term + up_in[step - 2].astype(jnp.float32)
        up_out[step - 1] = term.astype(up_out.dtype)
        pending_up = send(up_out.at[step - 1], up_in.at[step - 1], up, step - 1)
        if step <= downward:
            term = own(z - (downward - step + 1))
            if pending_down is not None:
                pending_down.wait_recv()
                term = term + down_in[step - 2].astype(jnp.float32)
            down_out[step - 1] = term.astype(down_out.dtype)
            pending_down = send(down_out.at[step - 1], down_in.at[step - 1], down,
                                upward + step - 1)
    pending_up.wait_recv()
    pending_down.wait_recv()
    mine = (own(z) + up_in[upward - 1].astype(jnp.float32)
            + down_in[downward - 1].astype(jnp.float32))
    side_out[...] = jnp.where(side == 0, mine[1], mine[0])
    across = send(side_out, side_in, partner, upward + downward)
    across.wait_recv()
    out_ref[...] = jnp.where(side == 0, mine[0], mine[1]) + side_in[...]
    for copy in sends:
        copy.wait_send()
    for copy in tail_copies:
        copy.wait_send()
    for copy in tail_copies:
        copy.wait_recv()
    tails_ref[...] = tails_in[...]


def relay_reduce(targets, partial, tail, n, collective_id):
    _, rows, cols = partial.shape
    ring = n // 2
    upward = ring // 2
    downward = ring - 1 - upward
    vmem = pl.BlockSpec(memory_space=pltpu.VMEM)
    return pl.pallas_call(
        functools.partial(relay_reduce_kernel, n=n),
        out_shape=[
            jax.ShapeDtypeStruct((rows, cols), jnp.float32),
            jax.ShapeDtypeStruct((n,) + tuple(tail.shape), jnp.float32),
        ],
        in_specs=[pl.BlockSpec(memory_space=pltpu.SMEM), vmem, vmem],
        out_specs=[vmem, vmem],
        scratch_shapes=[
            pltpu.VMEM((upward, 2, rows, cols), jnp.bfloat16),
            pltpu.VMEM((downward, 2, rows, cols), jnp.bfloat16),
            pltpu.VMEM((upward, 2, rows, cols), jnp.bfloat16),
            pltpu.VMEM((downward, 2, rows, cols), jnp.bfloat16),
            pltpu.VMEM((rows, cols), jnp.float32),
            pltpu.VMEM((rows, cols), jnp.float32),
            pltpu.VMEM((n,) + tuple(tail.shape), jnp.float32),
            pltpu.SemaphoreType.DMA((upward + downward + 1,)),
            pltpu.SemaphoreType.DMA((upward + downward + 1,)),
            pltpu.SemaphoreType.DMA((n - 1,)),
            pltpu.SemaphoreType.DMA((n - 1,)),
        ],
        compiler_params=pltpu.CompilerParams(
            collective_id=collective_id, has_side_effects=True,
            vmem_limit_bytes=56 * 1024 * 1024,
        ),
    )(targets, partial, tail)


def on_device(query, key, value, output, output_gradient, parent, owner):
    count = lax.axis_size("ctx")
    me = lax.axis_index("ctx")
    tile = query.shape[1]
    width = key.shape[2]
    scale_factor = HEAD_WIDTH ** (-0.5)
    prompt_tiles = count // 8
    parent_row = parent[0]
    owner_row = owner[0]
    tiles = jnp.arange(count, dtype=jnp.int32)
    my_tile = jnp.sum(jnp.where(owner_row == me, tiles, 0))
    trained = my_tile >= prompt_tiles
    above = pick_entry(parent_row, my_tile)
    second = jnp.logical_and(trained, above >= prompt_tiles)
    slot_tiles = jnp.stack(
        [jnp.int32(0), jnp.int32(1), jnp.where(second, above, 1).astype(jnp.int32)]
    )
    slot_blocks = jnp.sum(
        jnp.where(slot_tiles[:, None] == tiles[None, :], owner_row[None, :], 0), axis=1
    ).astype(jnp.int32)
    flags = jnp.stack([trained, trained, second, trained]).astype(jnp.int32)

    pair = jnp.concatenate([key[0], value[0]], axis=1)
    gathered = relay_gather(pair, 0)
    picked = gathered[slot_blocks]
    keys = jnp.concatenate([picked[:, :, :width], key[0][None]], axis=0)
    values = jnp.concatenate([picked[:, :, width:], value[0][None]], axis=0)

    dq, dk, dv = attention_grads(
        flags, query[0], output_gradient[0], output[0], keys, values, scale_factor
    )
    partial = jnp.concatenate([dk, dv], axis=2)
    targets = jnp.concatenate([slot_blocks, me[None].astype(jnp.int32)])
    total_rows = lax.axis_size("dp") * query.shape[0] * count * tile
    norm = total_rows ** (-0.5)
    wide = query.shape[2]
    dq_sum = jnp.sum(dq, axis=0)
    kv_sum = jnp.sum(partial, axis=(0, 1))
    tail_width = 2 * width
    tail_rows = 8
    tail = jnp.concatenate(
        [dq_sum, kv_sum, jnp.zeros((tail_rows * tail_width - wide - tail_width,), jnp.float32)]
    ).reshape(tail_rows, tail_width)
    grads, landed = relay_reduce(targets, partial, tail, count, 1)
    summed = landed[0]
    for peer in range(1, count):
        summed = summed + landed[peer]
    both = exchange(summed, "dp", False, 2)
    sums = (both[0] + both[1]).reshape(-1) * norm
    sum_q = sums[:wide]
    sum_k = sums[wide:wide + width]
    sum_v = sums[wide + width:wide + 2 * width]
    return (
        dq.astype(jnp.bfloat16)[None],
        grads[:, :width].astype(jnp.bfloat16)[None],
        grads[:, width:].astype(jnp.bfloat16)[None],
        sum_q,
        sum_k,
        sum_v,
    )


def solution(mesh):
    return jax.shard_map(
        on_device,
        mesh=mesh,
        in_specs=(
            P("dp", "ctx", "head"),
            P("dp", "ctx", "head"),
            P("dp", "ctx", "head"),
            P("dp", "ctx", "head"),
            P("dp", "ctx", "head"),
            P("dp", None),
            P("dp", None),
        ),
        out_specs=(
            P("dp", "ctx", "head"),
            P("dp", "ctx", "head"),
            P("dp", "ctx", "head"),
            P("head"),
            P("head"),
            P("head"),
        ),
        check_vma=False,
    )
```

```python
import functools

import jax
import jax.numpy as jnp
from jax import lax
from jax.experimental import pallas as pl
from jax.experimental.pallas import tpu as pltpu
from jax.sharding import PartitionSpec as P

HEAD_WIDTH = 128

NEGATIVE_FILL = -1e30


def pick_entry(vector, index):
    spots = jnp.arange(vector.shape[0], dtype=jnp.int32)
    return jnp.sum(jnp.where(spots == index, vector, 0), axis=0)


def pick_rows(matrix, index):
    spots = jnp.arange(matrix.shape[0], dtype=jnp.int32)
    return jnp.sum(jnp.where((spots == index)[:, None], matrix, 0.0), axis=0)


def attention_grads_kernel(flags_ref, q_ref, g_ref, o_ref, k_ref, v_ref,
                           dq_ref, dk_ref, dv_ref, s_scr, *, slots, scale):
    head = pl.program_id(0)

    @pl.when(head == 0)
    def _():
        dk_ref[...] = jnp.zeros_like(dk_ref)
        dv_ref[...] = jnp.zeros_like(dv_ref)

    q = q_ref[...]
    g = g_ref[...]
    o = o_ref[...]
    rows = q.shape[0]
    delta = jnp.sum(g.astype(jnp.float32) * o.astype(jnp.float32), axis=1, keepdims=True)
    causal = (lax.broadcasted_iota(jnp.int32, (rows, rows), 0)
              >= lax.broadcasted_iota(jnp.int32, (rows, rows), 1))
    nt = (((1,), (1,)), ((), ()))
    tn = (((0,), (0,)), ((), ()))

    top = jnp.full((rows, 1), NEGATIVE_FILL, jnp.float32)
    for j in range(slots):
        keep = flags_ref[j] > 0
        if j == slots - 1:
            keep = jnp.logical_and(keep, causal)
        scores = lax.dot_general(q, k_ref[j], nt, preferred_element_type=jnp.float32) * scale
        scores = jnp.where(keep, scores, NEGATIVE_FILL)
        s_scr[j] = scores
        top = jnp.maximum(top, jnp.max(scores, axis=1, keepdims=True))

    total = jnp.zeros((rows, 1), jnp.float32)
    for j in range(slots):
        keep = flags_ref[j] > 0
        if j == slots - 1:
            keep = jnp.logical_and(keep, causal)
        probs = jnp.where(keep, jnp.exp(s_scr[j] - top), 0.0)
        s_scr[j] = probs
        total = total + jnp.sum(probs, axis=1, keepdims=True)
    inverse = jnp.where(total > 0, 1.0 / jnp.where(total > 0, total, 1.0), 0.0)

    dq = jnp.zeros((rows, q.shape[1]), jnp.float32)
    for j in range(slots):
        probs = s_scr[j] * inverse
        dv_ref[j] += lax.dot_general(probs.astype(jnp.bfloat16), g, tn,
                                     preferred_element_type=jnp.float32)
        dprobs = lax.dot_general(g, v_ref[j], nt, preferred_element_type=jnp.float32)
        dscores = (probs * (dprobs - delta)).astype(jnp.bfloat16)
        dq = dq + jnp.dot(dscores, k_ref[j], preferred_element_type=jnp.float32)
        dk_ref[j] += lax.dot_general(dscores, q, tn, preferred_element_type=jnp.float32) * scale
    dq_ref[...] = dq * scale


def attention_grads(flags, q, g, o, keys, values, scale):
    rows, wide = q.shape
    slots = keys.shape[0]
    heads = wide // HEAD_WIDTH
    col = pl.BlockSpec((rows, HEAD_WIDTH), lambda h, f: (0, h))
    whole = pl.BlockSpec((slots, rows, HEAD_WIDTH), lambda h, f: (0, 0, 0))
    return pl.pallas_call(
        functools.partial(attention_grads_kernel, slots=slots, scale=scale),
        grid_spec=pltpu.PrefetchScalarGridSpec(
            num_scalar_prefetch=1,
            grid=(heads,),
            in_specs=[col, col, col, whole, whole],
            out_specs=[col, whole, whole],
            scratch_shapes=[pltpu.VMEM((slots, rows, rows), jnp.float32)],
        ),
        out_shape=[
            jax.ShapeDtypeStruct((rows, wide), jnp.float32),
            jax.ShapeDtypeStruct((slots, rows, HEAD_WIDTH), jnp.float32),
            jax.ShapeDtypeStruct((slots, rows, HEAD_WIDTH), jnp.float32),
        ],
        compiler_params=pltpu.CompilerParams(
            dimension_semantics=("arbitrary",), vmem_limit_bytes=48 * 1024 * 1024
        ),
    )(flags, q, g, o, keys, values)


def exchange_kernel(x_ref, out_ref, send_sem, recv_sem, self_sem, *, axis, n, indexed):
    me = lax.axis_index(axis)
    barrier = pltpu.get_barrier_semaphore()
    for d in range(1, n):
        pl.semaphore_signal(
            barrier, inc=1, device_id={axis: lax.rem(me + d, n)},
            device_id_type=pl.DeviceIdType.MESH,
        )
    pl.semaphore_wait(barrier, n - 1)
    copies = []
    for d in range(1, n):
        peer = lax.rem(me + d, n)
        copy = pltpu.make_async_remote_copy(
            src_ref=x_ref.at[peer] if indexed else x_ref,
            dst_ref=out_ref.at[me],
            send_sem=send_sem.at[d - 1],
            recv_sem=recv_sem.at[d - 1],
            device_id={axis: peer},
            device_id_type=pl.DeviceIdType.MESH,
        )
        copy.start()
        copies.append(copy)
    local = pltpu.make_async_copy(x_ref.at[me] if indexed else x_ref, out_ref.at[me], self_sem)
    local.start()
    for copy in copies:
        copy.wait_send()
    for copy in copies:
        copy.wait_recv()
    local.wait()


def exchange(x, axis, indexed, collective_id):
    n = lax.axis_size(axis)
    piece = x.shape[1:] if indexed else x.shape
    return pl.pallas_call(
        functools.partial(exchange_kernel, axis=axis, n=n, indexed=indexed),
        out_shape=jax.ShapeDtypeStruct((n,) + tuple(piece), x.dtype),
        in_specs=[pl.BlockSpec(memory_space=pl.ANY)],
        out_specs=pl.BlockSpec(memory_space=pl.ANY),
        scratch_shapes=[
            pltpu.SemaphoreType.DMA((n - 1,)),
            pltpu.SemaphoreType.DMA((n - 1,)),
            pltpu.SemaphoreType.DMA,
        ],
        compiler_params=pltpu.CompilerParams(collective_id=collective_id, has_side_effects=True),
    )(x)


def relay_gather_kernel(x_ref, out_ref, send_sem, recv_sem, self_sem, *, n):
    me = lax.axis_index("ctx")
    ring = n // 2
    z = me // 2
    side = me % 2
    partner = z * 2 + (1 - side)
    up = lax.rem(z + 1, ring) * 2 + side
    down = lax.rem(z + ring - 1, ring) * 2 + side
    barrier = pltpu.get_barrier_semaphore()
    for peer in (partner, up, down):
        pl.semaphore_signal(barrier, inc=1, device_id={"ctx": peer},
                            device_id_type=pl.DeviceIdType.MESH)
    pl.semaphore_wait(barrier, 3)
    local = pltpu.make_async_copy(x_ref, out_ref.at[me], self_sem)
    local.start()
    sends = []

    def send(slot, target, src):
        copy = pltpu.make_async_remote_copy(
            src_ref=src, dst_ref=out_ref.at[slot], send_sem=send_sem.at[len(sends)],
            recv_sem=recv_sem.at[slot], device_id={"ctx": target},
            device_id_type=pl.DeviceIdType.MESH,
        )
        copy.start()
        sends.append(copy)

    def arrive(slot):
        pltpu.make_async_remote_copy(
            src_ref=x_ref, dst_ref=out_ref.at[slot], send_sem=send_sem.at[0],
            recv_sem=recv_sem.at[slot], device_id={"ctx": partner},
            device_id_type=pl.DeviceIdType.MESH,
        ).wait_recv()

    def origin(step, offset):
        return lax.rem(z + step + ring, ring) * 2 + offset

    upward = ring // 2
    downward = ring - 1 - upward
    send(me, partner, x_ref)
    send(me, up, x_ref)
    send(me, down, x_ref)
    arrive(partner)
    send(partner, up, out_ref.at[partner])
    send(partner, down, out_ref.at[partner])
    for step in range(2, upward + 1):
        for offset in (0, 1):
            slot = origin(-(step - 1), offset)
            arrive(slot)
            send(slot, up, out_ref.at[slot])
        if step <= downward:
            for offset in (0, 1):
                slot = origin(step - 1, offset)
                arrive(slot)
                send(slot, down, out_ref.at[slot])
    for offset in (0, 1):
        arrive(origin(-upward, offset))
    for offset in (0, 1):
        arrive(origin(downward, offset))
    for copy in sends:
        copy.wait_send()
    local.wait()


def relay_gather(x, collective_id):
    n = lax.axis_size("ctx")
    return pl.pallas_call(
        functools.partial(relay_gather_kernel, n=n),
        out_shape=jax.ShapeDtypeStruct((n,) + tuple(x.shape), x.dtype),
        in_specs=[pl.BlockSpec(memory_space=pl.ANY)],
        out_specs=pl.BlockSpec(memory_space=pl.ANY),
        scratch_shapes=[
            pltpu.SemaphoreType.DMA((n - 1,)),
            pltpu.SemaphoreType.DMA((n,)),
            pltpu.SemaphoreType.DMA,
        ],
        compiler_params=pltpu.CompilerParams(collective_id=collective_id, has_side_effects=True),
    )(x)


def relay_reduce_kernel(t_ref, x_ref, tail_ref, out_ref, tails_ref, up_in, down_in, up_out,
                        down_out, side_out, side_in, tails_in, send_sem, recv_sem, tail_send,
                        tail_recv, *, n):
    me = lax.axis_index("ctx")
    ring = n // 2
    z = me // 2
    side = me % 2
    partner = z * 2 + (1 - side)
    up = lax.rem(z + 1, ring) * 2 + side
    down = lax.rem(z + ring - 1, ring) * 2 + side
    upward = ring // 2
    downward = ring - 1 - upward
    barrier = pltpu.get_barrier_semaphore()
    for d in range(1, n):
        pl.semaphore_signal(barrier, inc=1, device_id={"ctx": lax.rem(me + d, n)},
                            device_id_type=pl.DeviceIdType.MESH)
    pl.semaphore_wait(barrier, n - 1)
    tail_copies = []
    for d in range(1, n):
        copy = pltpu.make_async_remote_copy(
            src_ref=tail_ref, dst_ref=tails_in.at[me], send_sem=tail_send.at[d - 1],
            recv_sem=tail_recv.at[d - 1], device_id={"ctx": lax.rem(me + d, n)},
            device_id_type=pl.DeviceIdType.MESH,
        )
        copy.start()
        tail_copies.append(copy)
    tails_in[me] = tail_ref[...]
    sends = []

    def send(src, dst, target, sem_index):
        copy = pltpu.make_async_remote_copy(
            src_ref=src, dst_ref=dst, send_sem=send_sem.at[len(sends)],
            recv_sem=recv_sem.at[sem_index], device_id={"ctx": target},
            device_id_type=pl.DeviceIdType.MESH,
        )
        copy.start()
        sends.append(copy)
        return copy

    chunks = up_in.shape[1]
    part = x_ref.shape[1] // chunks

    def own(target_z, chunk):
        base = lax.rem(target_z + 2 * ring, ring) * 2
        pieces = []
        for offset in (0, 1):
            total = jnp.zeros((part, x_ref.shape[2]), jnp.float32)
            for j in range(x_ref.shape[0]):
                total = total + jnp.where(
                    t_ref[j] == base + offset, x_ref[j, pl.ds(chunk * part, part)], 0.0
                )
            pieces.append(total)
        return jnp.stack(pieces)

    pending_up = [None] * chunks
    pending_down = [None] * chunks
    for step in range(1, upward + 1):
        for chunk in range(chunks):
            term = own(z + upward - step + 1, chunk)
            if pending_up[chunk] is not None:
                pending_up[chunk].wait_recv()
                term = term + up_in[step - 2, chunk].astype(jnp.float32)
            up_out[step - 1, chunk] = term.astype(up_out.dtype)
            pending_up[chunk] = send(up_out.at[step - 1, chunk], up_in.at[step - 1, chunk], up,
                                     (step - 1) * chunks + chunk)
            if step <= downward:
                term = own(z - (downward - step + 1), chunk)
                if pending_down[chunk] is not None:
                    pending_down[chunk].wait_recv()
                    term = term + down_in[step - 2, chunk].astype(jnp.float32)
                down_out[step - 1, chunk] = term.astype(down_out.dtype)
                pending_down[chunk] = send(
                    down_out.at[step - 1, chunk], down_in.at[step - 1, chunk], down,
                    (upward + step - 1) * chunks + chunk,
                )
    pieces = []
    for chunk in range(chunks):
        pending_up[chunk].wait_recv()
        pending_down[chunk].wait_recv()
        pieces.append(own(z, chunk) + up_in[upward - 1, chunk].astype(jnp.float32)
                      + down_in[downward - 1, chunk].astype(jnp.float32))
    mine = jnp.concatenate(pieces, axis=1)
    side_out[...] = jnp.where(side == 0, mine[1], mine[0])
    across = send(side_out, side_in, partner, (upward + downward) * chunks)
    across.wait_recv()
    out_ref[...] = jnp.where(side == 0, mine[0], mine[1]) + side_in[...]
    for copy in sends:
        copy.wait_send()
    for copy in tail_copies:
        copy.wait_send()
    for copy in tail_copies:
        copy.wait_recv()
    tails_ref[...] = tails_in[...]


def relay_reduce(targets, partial, tail, n, collective_id, chunks=2):
    _, rows, cols = partial.shape
    ring = n // 2
    upward = ring // 2
    downward = ring - 1 - upward
    vmem = pl.BlockSpec(memory_space=pltpu.VMEM)
    return pl.pallas_call(
        functools.partial(relay_reduce_kernel, n=n),
        out_shape=[
            jax.ShapeDtypeStruct((rows, cols), jnp.float32),
            jax.ShapeDtypeStruct((n,) + tuple(tail.shape), jnp.float32),
        ],
        in_specs=[pl.BlockSpec(memory_space=pltpu.SMEM), vmem, vmem],
        out_specs=[vmem, vmem],
        scratch_shapes=[
            pltpu.VMEM((upward, chunks, 2, rows // chunks, cols), jnp.bfloat16),
            pltpu.VMEM((downward, chunks, 2, rows // chunks, cols), jnp.bfloat16),
            pltpu.VMEM((upward, chunks, 2, rows // chunks, cols), jnp.bfloat16),
            pltpu.VMEM((downward, chunks, 2, rows // chunks, cols), jnp.bfloat16),
            pltpu.VMEM((rows, cols), jnp.float32),
            pltpu.VMEM((rows, cols), jnp.float32),
            pltpu.VMEM((n,) + tuple(tail.shape), jnp.float32),
            pltpu.SemaphoreType.DMA(((upward + downward) * chunks + 1,)),
            pltpu.SemaphoreType.DMA(((upward + downward) * chunks + 1,)),
            pltpu.SemaphoreType.DMA((n - 1,)),
            pltpu.SemaphoreType.DMA((n - 1,)),
        ],
        compiler_params=pltpu.CompilerParams(
            collective_id=collective_id, has_side_effects=True,
            vmem_limit_bytes=56 * 1024 * 1024,
        ),
    )(targets, partial, tail)


def on_device(query, key, value, output, output_gradient, parent, owner):
    count = lax.axis_size("ctx")
    me = lax.axis_index("ctx")
    tile = query.shape[1]
    width = key.shape[2]
    scale_factor = HEAD_WIDTH ** (-0.5)
    prompt_tiles = count // 8
    parent_row = parent[0]
    owner_row = owner[0]
    tiles = jnp.arange(count, dtype=jnp.int32)
    my_tile = jnp.sum(jnp.where(owner_row == me, tiles, 0))
    trained = my_tile >= prompt_tiles
    above = pick_entry(parent_row, my_tile)
    second = jnp.logical_and(trained, above >= prompt_tiles)
    slot_tiles = jnp.stack(
        [jnp.int32(0), jnp.int32(1), jnp.where(second, above, 1).astype(jnp.int32)]
    )
    slot_blocks = jnp.sum(
        jnp.where(slot_tiles[:, None] == tiles[None, :], owner_row[None, :], 0), axis=1
    ).astype(jnp.int32)
    flags = jnp.stack([trained, trained, second, trained]).astype(jnp.int32)

    pair = jnp.concatenate([key[0], value[0]], axis=1)
    gathered = relay_gather(pair, 0)
    picked = gathered[slot_blocks]
    keys = jnp.concatenate([picked[:, :, :width], key[0][None]], axis=0)
    values = jnp.concatenate([picked[:, :, width:], value[0][None]], axis=0)

    dq, dk, dv = attention_grads(
        flags, query[0], output_gradient[0], output[0], keys, values, scale_factor
    )
    partial = jnp.concatenate([dk, dv], axis=2)
    targets = jnp.concatenate([slot_blocks, me[None].astype(jnp.int32)])
    total_rows = lax.axis_size("dp") * query.shape[0] * count * tile
    norm = total_rows ** (-0.5)
    wide = query.shape[2]
    dq_sum = jnp.sum(dq, axis=0)
    kv_sum = jnp.sum(partial, axis=(0, 1))
    tail_width = 2 * width
    tail_rows = 8
    tail = jnp.concatenate(
        [dq_sum, kv_sum, jnp.zeros((tail_rows * tail_width - wide - tail_width,), jnp.float32)]
    ).reshape(tail_rows, tail_width)
    grads, landed = relay_reduce(targets, partial, tail, count, 1)
    summed = landed[0]
    for peer in range(1, count):
        summed = summed + landed[peer]
    both = exchange(summed, "dp", False, 2)
    sums = (both[0] + both[1]).reshape(-1) * norm
    sum_q = sums[:wide]
    sum_k = sums[wide:wide + width]
    sum_v = sums[wide + width:wide + 2 * width]
    return (
        dq.astype(jnp.bfloat16)[None],
        grads[:, :width].astype(jnp.bfloat16)[None],
        grads[:, width:].astype(jnp.bfloat16)[None],
        sum_q,
        sum_k,
        sum_v,
    )


def solution(mesh):
    return jax.shard_map(
        on_device,
        mesh=mesh,
        in_specs=(
            P("dp", "ctx", "head"),
            P("dp", "ctx", "head"),
            P("dp", "ctx", "head"),
            P("dp", "ctx", "head"),
            P("dp", "ctx", "head"),
            P("dp", None),
            P("dp", None),
        ),
        out_specs=(
            P("dp", "ctx", "head"),
            P("dp", "ctx", "head"),
            P("dp", "ctx", "head"),
            P("head"),
            P("head"),
            P("head"),
        ),
        check_vma=False,
    )
```

```python
import functools

import jax
import jax.numpy as jnp
from jax import lax
from jax.experimental import pallas as pl
from jax.experimental.pallas import tpu as pltpu
from jax.sharding import PartitionSpec as P

HEAD_WIDTH = 128

NEGATIVE_FILL = -1e30


def pick_entry(vector, index):
    spots = jnp.arange(vector.shape[0], dtype=jnp.int32)
    return jnp.sum(jnp.where(spots == index, vector, 0), axis=0)


def pick_rows(matrix, index):
    spots = jnp.arange(matrix.shape[0], dtype=jnp.int32)
    return jnp.sum(jnp.where((spots == index)[:, None], matrix, 0.0), axis=0)


def attention_grads_kernel(flags_ref, blocks_ref, q_ref, g_ref, o_ref, k0, k1, k2, k3, v0, v1, v2,
                           v3, dq_ref, dqsum_ref, dk_ref, dv_ref, ksum_ref, vsum_ref, s_scr, *,
                           scale):
    head = pl.program_id(0)
    k_refs = (k0, k1, k2, k3)
    v_refs = (v0, v1, v2, v3)
    slots = len(k_refs)

    @pl.when(head == 0)
    def _():
        dk_ref[...] = jnp.zeros_like(dk_ref)
        dv_ref[...] = jnp.zeros_like(dv_ref)

    q = q_ref[...]
    g = g_ref[...]
    o = o_ref[...]
    rows = q.shape[0]
    delta = jnp.sum(g.astype(jnp.float32) * o.astype(jnp.float32), axis=1, keepdims=True)
    causal = (lax.broadcasted_iota(jnp.int32, (rows, rows), 0)
              >= lax.broadcasted_iota(jnp.int32, (rows, rows), 1))
    nt = (((1,), (1,)), ((), ()))
    tn = (((0,), (0,)), ((), ()))

    top = jnp.full((rows, 1), NEGATIVE_FILL, jnp.float32)
    for j in range(slots):
        keep = flags_ref[j] > 0
        if j == slots - 1:
            keep = jnp.logical_and(keep, causal)
        scores = lax.dot_general(q, k_refs[j][...], nt, preferred_element_type=jnp.float32) * scale
        scores = jnp.where(keep, scores, NEGATIVE_FILL)
        s_scr[j] = scores
        top = jnp.maximum(top, jnp.max(scores, axis=1, keepdims=True))

    total = jnp.zeros((rows, 1), jnp.float32)
    for j in range(slots):
        keep = flags_ref[j] > 0
        if j == slots - 1:
            keep = jnp.logical_and(keep, causal)
        probs = jnp.where(keep, jnp.exp(s_scr[j] - top), 0.0)
        s_scr[j] = probs
        total = total + jnp.sum(probs, axis=1, keepdims=True)
    inverse = jnp.where(total > 0, 1.0 / jnp.where(total > 0, total, 1.0), 0.0)

    dq = jnp.zeros((rows, q.shape[1]), jnp.float32)
    for j in range(slots):
        probs = s_scr[j] * inverse
        dv_ref[j] += lax.dot_general(probs.astype(jnp.bfloat16), g, tn,
                                     preferred_element_type=jnp.float32)
        dprobs = lax.dot_general(g, v_refs[j][...], nt, preferred_element_type=jnp.float32)
        dscores = (probs * (dprobs - delta)).astype(jnp.bfloat16)
        dq = dq + jnp.dot(dscores, k_refs[j][...], preferred_element_type=jnp.float32)
        dk_ref[j] += lax.dot_general(dscores, q, tn, preferred_element_type=jnp.float32) * scale
    dq = dq * scale
    dq_ref[...] = dq.astype(dq_ref.dtype)
    dqsum_ref[...] = jnp.sum(dq, axis=0, keepdims=True)

    @pl.when(head == pl.num_programs(0) - 1)
    def _():
        ksum_ref[...] = jnp.sum(jnp.sum(dk_ref[...], axis=0), axis=0, keepdims=True)
        vsum_ref[...] = jnp.sum(jnp.sum(dv_ref[...], axis=0), axis=0, keepdims=True)


def attention_grads(flags, blocks, q, g, o, gathered, scale):
    rows, wide = q.shape
    slots = blocks.shape[0]
    heads = wide // HEAD_WIDTH
    col = pl.BlockSpec((rows, HEAD_WIDTH), lambda h, f, b: (0, h))
    line = pl.BlockSpec((1, HEAD_WIDTH), lambda h, f, b: (0, h))
    fixed = pl.BlockSpec((1, HEAD_WIDTH), lambda h, f, b: (0, 0))
    whole = pl.BlockSpec((slots, rows, HEAD_WIDTH), lambda h, f, b: (0, 0, 0))

    def pick(j, part):
        return pl.BlockSpec((None, rows, HEAD_WIDTH), lambda h, f, b: (b[j], 0, part))

    return pl.pallas_call(
        functools.partial(attention_grads_kernel, scale=scale),
        grid_spec=pltpu.PrefetchScalarGridSpec(
            num_scalar_prefetch=2,
            grid=(heads,),
            in_specs=[col, col, col] + [pick(j, 0) for j in range(slots)]
            + [pick(j, 1) for j in range(slots)],
            out_specs=[col, line, whole, whole, fixed, fixed],
            scratch_shapes=[pltpu.VMEM((slots, rows, rows), jnp.float32)],
        ),
        out_shape=[
            jax.ShapeDtypeStruct((rows, wide), jnp.bfloat16),
            jax.ShapeDtypeStruct((1, wide), jnp.float32),
            jax.ShapeDtypeStruct((slots, rows, HEAD_WIDTH), jnp.float32),
            jax.ShapeDtypeStruct((slots, rows, HEAD_WIDTH), jnp.float32),
            jax.ShapeDtypeStruct((1, HEAD_WIDTH), jnp.float32),
            jax.ShapeDtypeStruct((1, HEAD_WIDTH), jnp.float32),
        ],
        compiler_params=pltpu.CompilerParams(
            dimension_semantics=("arbitrary",), vmem_limit_bytes=48 * 1024 * 1024
        ),
    )(flags, blocks, q, g, o, *([gathered] * (2 * slots)))


def exchange_kernel(x_ref, out_ref, send_sem, recv_sem, self_sem, *, axis, n, indexed):
    me = lax.axis_index(axis)
    barrier = pltpu.get_barrier_semaphore()
    for d in range(1, n):
        pl.semaphore_signal(
            barrier, inc=1, device_id={axis: lax.rem(me + d, n)},
            device_id_type=pl.DeviceIdType.MESH,
        )
    pl.semaphore_wait(barrier, n - 1)
    copies = []
    for d in range(1, n):
        peer = lax.rem(me + d, n)
        copy = pltpu.make_async_remote_copy(
            src_ref=x_ref.at[peer] if indexed else x_ref,
            dst_ref=out_ref.at[me],
            send_sem=send_sem.at[d - 1],
            recv_sem=recv_sem.at[d - 1],
            device_id={axis: peer},
            device_id_type=pl.DeviceIdType.MESH,
        )
        copy.start()
        copies.append(copy)
    local = pltpu.make_async_copy(x_ref.at[me] if indexed else x_ref, out_ref.at[me], self_sem)
    local.start()
    for copy in copies:
        copy.wait_send()
    for copy in copies:
        copy.wait_recv()
    local.wait()


def exchange(x, axis, indexed, collective_id):
    n = lax.axis_size(axis)
    piece = x.shape[1:] if indexed else x.shape
    return pl.pallas_call(
        functools.partial(exchange_kernel, axis=axis, n=n, indexed=indexed),
        out_shape=jax.ShapeDtypeStruct((n,) + tuple(piece), x.dtype),
        in_specs=[pl.BlockSpec(memory_space=pl.ANY)],
        out_specs=pl.BlockSpec(memory_space=pl.ANY),
        scratch_shapes=[
            pltpu.SemaphoreType.DMA((n - 1,)),
            pltpu.SemaphoreType.DMA((n - 1,)),
            pltpu.SemaphoreType.DMA,
        ],
        compiler_params=pltpu.CompilerParams(collective_id=collective_id, has_side_effects=True),
    )(x)


def relay_gather_kernel(x_ref, out_ref, send_sem, recv_sem, self_sem, *, n):
    me = lax.axis_index("ctx")
    ring = n // 2
    z = me // 2
    side = me % 2
    partner = z * 2 + (1 - side)
    up = lax.rem(z + 1, ring) * 2 + side
    down = lax.rem(z + ring - 1, ring) * 2 + side
    barrier = pltpu.get_barrier_semaphore()
    for peer in (partner, up, down):
        pl.semaphore_signal(barrier, inc=1, device_id={"ctx": peer},
                            device_id_type=pl.DeviceIdType.MESH)
    pl.semaphore_wait(barrier, 3)
    local = pltpu.make_async_copy(x_ref, out_ref.at[me], self_sem)
    local.start()
    sends = []

    def send(slot, target, src):
        copy = pltpu.make_async_remote_copy(
            src_ref=src, dst_ref=out_ref.at[slot], send_sem=send_sem.at[len(sends)],
            recv_sem=recv_sem.at[slot], device_id={"ctx": target},
            device_id_type=pl.DeviceIdType.MESH,
        )
        copy.start()
        sends.append(copy)

    def arrive(slot):
        pltpu.make_async_remote_copy(
            src_ref=x_ref, dst_ref=out_ref.at[slot], send_sem=send_sem.at[0],
            recv_sem=recv_sem.at[slot], device_id={"ctx": partner},
            device_id_type=pl.DeviceIdType.MESH,
        ).wait_recv()

    def origin(step, offset):
        return lax.rem(z + step + ring, ring) * 2 + offset

    upward = ring // 2
    downward = ring - 1 - upward
    send(me, partner, x_ref)
    send(me, up, x_ref)
    send(me, down, x_ref)
    arrive(partner)
    send(partner, up, out_ref.at[partner])
    send(partner, down, out_ref.at[partner])
    for step in range(2, upward + 1):
        for offset in (0, 1):
            slot = origin(-(step - 1), offset)
            arrive(slot)
            send(slot, up, out_ref.at[slot])
        if step <= downward:
            for offset in (0, 1):
                slot = origin(step - 1, offset)
                arrive(slot)
                send(slot, down, out_ref.at[slot])
    for offset in (0, 1):
        arrive(origin(-upward, offset))
    for offset in (0, 1):
        arrive(origin(downward, offset))
    for copy in sends:
        copy.wait_send()
    local.wait()


def relay_gather(x, collective_id):
    n = lax.axis_size("ctx")
    return pl.pallas_call(
        functools.partial(relay_gather_kernel, n=n),
        out_shape=jax.ShapeDtypeStruct((n,) + tuple(x.shape), x.dtype),
        in_specs=[pl.BlockSpec(memory_space=pl.ANY)],
        out_specs=pl.BlockSpec(memory_space=pl.ANY),
        scratch_shapes=[
            pltpu.SemaphoreType.DMA((n - 1,)),
            pltpu.SemaphoreType.DMA((n,)),
            pltpu.SemaphoreType.DMA,
        ],
        compiler_params=pltpu.CompilerParams(collective_id=collective_id, has_side_effects=True),
    )(x)


def relay_reduce_kernel(t_ref, x_ref, tail_ref, out_ref, tails_ref, up_in, down_in, up_out,
                        down_out, side_out, side_in, tails_in, send_sem, recv_sem, tail_send,
                        tail_recv, *, n):
    me = lax.axis_index("ctx")
    ring = n // 2
    z = me // 2
    side = me % 2
    partner = z * 2 + (1 - side)
    up = lax.rem(z + 1, ring) * 2 + side
    down = lax.rem(z + ring - 1, ring) * 2 + side
    upward = ring // 2
    downward = ring - 1 - upward
    barrier = pltpu.get_barrier_semaphore()
    for d in range(1, n):
        pl.semaphore_signal(barrier, inc=1, device_id={"ctx": lax.rem(me + d, n)},
                            device_id_type=pl.DeviceIdType.MESH)
    pl.semaphore_wait(barrier, n - 1)
    tail_copies = []
    for d in range(1, n):
        copy = pltpu.make_async_remote_copy(
            src_ref=tail_ref, dst_ref=tails_in.at[me], send_sem=tail_send.at[d - 1],
            recv_sem=tail_recv.at[d - 1], device_id={"ctx": lax.rem(me + d, n)},
            device_id_type=pl.DeviceIdType.MESH,
        )
        copy.start()
        tail_copies.append(copy)
    tails_in[me] = tail_ref[...]
    sends = []

    def send(src, dst, target, sem_index):
        copy = pltpu.make_async_remote_copy(
            src_ref=src, dst_ref=dst, send_sem=send_sem.at[len(sends)],
            recv_sem=recv_sem.at[sem_index], device_id={"ctx": target},
            device_id_type=pl.DeviceIdType.MESH,
        )
        copy.start()
        sends.append(copy)
        return copy

    def own(target_z):
        base = lax.rem(target_z + 2 * ring, ring) * 2
        pieces = []
        for offset in (0, 1):
            total = jnp.zeros(x_ref.shape[1:], jnp.float32)
            for j in range(x_ref.shape[0]):
                total = total + jnp.where(t_ref[j] == base + offset, x_ref[j], 0.0)
            pieces.append(total)
        return jnp.stack(pieces)

    pending_up = None
    pending_down = None
    for step in range(1, upward + 1):
        term = own(z + upward - step + 1)
        if pending_up is not None:
            pending_up.wait_recv()
            term = term + up_in[step - 2].astype(jnp.float32)
        up_out[step - 1] = term.astype(up_out.dtype)
        pending_up = send(up_out.at[step - 1], up_in.at[step - 1], up, step - 1)
        if step <= downward:
            term = own(z - (downward - step + 1))
            if pending_down is not None:
                pending_down.wait_recv()
                term = term + down_in[step - 2].astype(jnp.float32)
            down_out[step - 1] = term.astype(down_out.dtype)
            pending_down = send(down_out.at[step - 1], down_in.at[step - 1], down,
                                upward + step - 1)
    pending_up.wait_recv()
    pending_down.wait_recv()
    mine = (own(z) + up_in[upward - 1].astype(jnp.float32)
            + down_in[downward - 1].astype(jnp.float32))
    side_out[...] = jnp.where(side == 0, mine[1], mine[0])
    across = send(side_out, side_in, partner, upward + downward)
    across.wait_recv()
    out_ref[...] = jnp.where(side == 0, mine[0], mine[1]) + side_in[...]
    for copy in sends:
        copy.wait_send()
    for copy in tail_copies:
        copy.wait_send()
    for copy in tail_copies:
        copy.wait_recv()
    tails_ref[...] = tails_in[...]


def relay_reduce(targets, partial, tail, n, collective_id):
    _, rows, cols = partial.shape
    ring = n // 2
    upward = ring // 2
    downward = ring - 1 - upward
    vmem = pl.BlockSpec(memory_space=pltpu.VMEM)
    return pl.pallas_call(
        functools.partial(relay_reduce_kernel, n=n),
        out_shape=[
            jax.ShapeDtypeStruct((rows, cols), jnp.float32),
            jax.ShapeDtypeStruct((n,) + tuple(tail.shape), jnp.float32),
        ],
        in_specs=[pl.BlockSpec(memory_space=pltpu.SMEM), vmem, vmem],
        out_specs=[vmem, vmem],
        scratch_shapes=[
            pltpu.VMEM((upward, 2, rows, cols), jnp.bfloat16),
            pltpu.VMEM((downward, 2, rows, cols), jnp.bfloat16),
            pltpu.VMEM((upward, 2, rows, cols), jnp.bfloat16),
            pltpu.VMEM((downward, 2, rows, cols), jnp.bfloat16),
            pltpu.VMEM((rows, cols), jnp.float32),
            pltpu.VMEM((rows, cols), jnp.float32),
            pltpu.VMEM((n,) + tuple(tail.shape), jnp.float32),
            pltpu.SemaphoreType.DMA((upward + downward + 1,)),
            pltpu.SemaphoreType.DMA((upward + downward + 1,)),
            pltpu.SemaphoreType.DMA((n - 1,)),
            pltpu.SemaphoreType.DMA((n - 1,)),
        ],
        compiler_params=pltpu.CompilerParams(
            collective_id=collective_id, has_side_effects=True,
            vmem_limit_bytes=56 * 1024 * 1024,
        ),
    )(targets, partial, tail)


def on_device(query, key, value, output, output_gradient, parent, owner):
    count = lax.axis_size("ctx")
    me = lax.axis_index("ctx")
    tile = query.shape[1]
    width = key.shape[2]
    scale_factor = HEAD_WIDTH ** (-0.5)
    prompt_tiles = count // 8
    parent_row = parent[0]
    owner_row = owner[0]
    tiles = jnp.arange(count, dtype=jnp.int32)
    my_tile = jnp.sum(jnp.where(owner_row == me, tiles, 0))
    trained = my_tile >= prompt_tiles
    above = pick_entry(parent_row, my_tile)
    second = jnp.logical_and(trained, above >= prompt_tiles)
    slot_tiles = jnp.stack(
        [jnp.int32(0), jnp.int32(1), jnp.where(second, above, 1).astype(jnp.int32)]
    )
    slot_blocks = jnp.sum(
        jnp.where(slot_tiles[:, None] == tiles[None, :], owner_row[None, :], 0), axis=1
    ).astype(jnp.int32)
    flags = jnp.stack([trained, trained, second, trained]).astype(jnp.int32)

    pair = jnp.concatenate([key[0], value[0]], axis=1)
    gathered = relay_gather(pair, 0)
    targets = jnp.concatenate([slot_blocks, me[None].astype(jnp.int32)])
    dq, dq_sum, dk, dv, k_sum, v_sum = attention_grads(
        flags, targets, query[0], output_gradient[0], output[0], gathered, scale_factor
    )
    partial = jnp.concatenate([dk, dv], axis=2)
    total_rows = lax.axis_size("dp") * query.shape[0] * count * tile
    norm = total_rows ** (-0.5)
    wide = query.shape[2]
    tail_width = 2 * width
    tail_rows = 8
    tail = jnp.concatenate(
        [dq_sum[0], k_sum[0], v_sum[0],
         jnp.zeros((tail_rows * tail_width - wide - tail_width,), jnp.float32)]
    ).reshape(tail_rows, tail_width)
    grads, landed = relay_reduce(targets, partial, tail, count, 1)
    summed = landed[0]
    for peer in range(1, count):
        summed = summed + landed[peer]
    both = exchange(summed, "dp", False, 2)
    sums = (both[0] + both[1]).reshape(-1) * norm
    sum_q = sums[:wide]
    sum_k = sums[wide:wide + width]
    sum_v = sums[wide + width:wide + 2 * width]
    return (
        dq[None],
        grads[:, :width].astype(jnp.bfloat16)[None],
        grads[:, width:].astype(jnp.bfloat16)[None],
        sum_q,
        sum_k,
        sum_v,
    )


def solution(mesh):
    return jax.shard_map(
        on_device,
        mesh=mesh,
        in_specs=(
            P("dp", "ctx", "head"),
            P("dp", "ctx", "head"),
            P("dp", "ctx", "head"),
            P("dp", "ctx", "head"),
            P("dp", "ctx", "head"),
            P("dp", None),
            P("dp", None),
        ),
        out_specs=(
            P("dp", "ctx", "head"),
            P("dp", "ctx", "head"),
            P("dp", "ctx", "head"),
            P("head"),
            P("head"),
            P("head"),
        ),
        check_vma=False,
    )
```

```python
import functools

import jax
import jax.numpy as jnp
from jax import lax
from jax.experimental import pallas as pl
from jax.experimental.pallas import tpu as pltpu
from jax.sharding import PartitionSpec as P

HEAD_WIDTH = 128

NEGATIVE_FILL = -1e30


def pick_entry(vector, index):
    spots = jnp.arange(vector.shape[0], dtype=jnp.int32)
    return jnp.sum(jnp.where(spots == index, vector, 0), axis=0)


def pick_rows(matrix, index):
    spots = jnp.arange(matrix.shape[0], dtype=jnp.int32)
    return jnp.sum(jnp.where((spots == index)[:, None], matrix, 0.0), axis=0)


def attention_grads_kernel(flags_ref, blocks_ref, q_ref, g_ref, o_ref, k0, k1, k2, k3, v0, v1, v2,
                           v3, dq_ref, dqsum_ref, dk_ref, dv_ref, ksum_ref, vsum_ref, s_scr, *,
                           scale):
    head = pl.program_id(0)
    k_refs = (k0, k1, k2, k3)
    v_refs = (v0, v1, v2, v3)
    slots = len(k_refs)

    @pl.when(head == 0)
    def _():
        dk_ref[...] = jnp.zeros_like(dk_ref)
        dv_ref[...] = jnp.zeros_like(dv_ref)

    q = q_ref[...]
    g = g_ref[...]
    o = o_ref[...]
    rows = q.shape[0]
    delta = jnp.sum(g.astype(jnp.float32) * o.astype(jnp.float32), axis=1, keepdims=True)
    causal = (lax.broadcasted_iota(jnp.int32, (rows, rows), 0)
              >= lax.broadcasted_iota(jnp.int32, (rows, rows), 1))
    nt = (((1,), (1,)), ((), ()))
    tn = (((0,), (0,)), ((), ()))

    top = jnp.full((rows, 1), NEGATIVE_FILL, jnp.float32)
    for j in range(slots):
        keep = flags_ref[j] > 0
        if j == slots - 1:
            keep = jnp.logical_and(keep, causal)
        scores = lax.dot_general(q, k_refs[j][...], nt, preferred_element_type=jnp.float32) * scale
        scores = jnp.where(keep, scores, NEGATIVE_FILL)
        s_scr[j] = scores
        top = jnp.maximum(top, jnp.max(scores, axis=1, keepdims=True))

    total = jnp.zeros((rows, 1), jnp.float32)
    for j in range(slots):
        keep = flags_ref[j] > 0
        if j == slots - 1:
            keep = jnp.logical_and(keep, causal)
        probs = jnp.where(keep, jnp.exp(s_scr[j] - top), 0.0)
        s_scr[j] = probs
        total = total + jnp.sum(probs, axis=1, keepdims=True)
    inverse = jnp.where(total > 0, 1.0 / jnp.where(total > 0, total, 1.0), 0.0)

    dq = jnp.zeros((rows, q.shape[1]), jnp.float32)
    for j in range(slots):
        probs = s_scr[j] * inverse
        dv_ref[j] += lax.dot_general(probs.astype(jnp.bfloat16), g, tn,
                                     preferred_element_type=jnp.float32)
        dprobs = lax.dot_general(g, v_refs[j][...], nt, preferred_element_type=jnp.float32)
        dscores = (probs * (dprobs - delta)).astype(jnp.bfloat16)
        dq = dq + jnp.dot(dscores, k_refs[j][...], preferred_element_type=jnp.float32)
        dk_ref[j] += lax.dot_general(dscores, q, tn, preferred_element_type=jnp.float32) * scale
    dq = dq * scale
    dq_ref[...] = dq.astype(dq_ref.dtype)
    dqsum_ref[...] = jnp.sum(dq, axis=0, keepdims=True)

    @pl.when(head == pl.num_programs(0) - 1)
    def _():
        ksum_ref[...] = jnp.sum(jnp.sum(dk_ref[...], axis=0), axis=0, keepdims=True)
        vsum_ref[...] = jnp.sum(jnp.sum(dv_ref[...], axis=0), axis=0, keepdims=True)


def attention_grads(flags, blocks, q, g, o, gathered, scale):
    rows, wide = q.shape
    slots = blocks.shape[0]
    heads = wide // HEAD_WIDTH
    col = pl.BlockSpec((rows, HEAD_WIDTH), lambda h, f, b: (0, h))
    line = pl.BlockSpec((1, HEAD_WIDTH), lambda h, f, b: (0, h))
    fixed = pl.BlockSpec((1, HEAD_WIDTH), lambda h, f, b: (0, 0))
    whole = pl.BlockSpec((slots, rows, HEAD_WIDTH), lambda h, f, b: (0, 0, 0))

    def pick(j, part):
        return pl.BlockSpec((None, rows, HEAD_WIDTH), lambda h, f, b: (b[j], 0, part))

    return pl.pallas_call(
        functools.partial(attention_grads_kernel, scale=scale),
        grid_spec=pltpu.PrefetchScalarGridSpec(
            num_scalar_prefetch=2,
            grid=(heads,),
            in_specs=[col, col, col] + [pick(j, 0) for j in range(slots)]
            + [pick(j, 1) for j in range(slots)],
            out_specs=[col, line, whole, whole, fixed, fixed],
            scratch_shapes=[pltpu.VMEM((slots, rows, rows), jnp.float32)],
        ),
        out_shape=[
            jax.ShapeDtypeStruct((rows, wide), jnp.bfloat16),
            jax.ShapeDtypeStruct((1, wide), jnp.float32),
            jax.ShapeDtypeStruct((slots, rows, HEAD_WIDTH), jnp.float32),
            jax.ShapeDtypeStruct((slots, rows, HEAD_WIDTH), jnp.float32),
            jax.ShapeDtypeStruct((1, HEAD_WIDTH), jnp.float32),
            jax.ShapeDtypeStruct((1, HEAD_WIDTH), jnp.float32),
        ],
        compiler_params=pltpu.CompilerParams(
            dimension_semantics=("arbitrary",), vmem_limit_bytes=48 * 1024 * 1024
        ),
    )(flags, blocks, q, g, o, *([gathered] * (2 * slots)))


def exchange_kernel(x_ref, out_ref, send_sem, recv_sem, self_sem, *, axis, n, indexed):
    me = lax.axis_index(axis)
    barrier = pltpu.get_barrier_semaphore()
    for d in range(1, n):
        pl.semaphore_signal(
            barrier, inc=1, device_id={axis: lax.rem(me + d, n)},
            device_id_type=pl.DeviceIdType.MESH,
        )
    pl.semaphore_wait(barrier, n - 1)
    copies = []
    for d in range(1, n):
        peer = lax.rem(me + d, n)
        copy = pltpu.make_async_remote_copy(
            src_ref=x_ref.at[peer] if indexed else x_ref,
            dst_ref=out_ref.at[me],
            send_sem=send_sem.at[d - 1],
            recv_sem=recv_sem.at[d - 1],
            device_id={axis: peer},
            device_id_type=pl.DeviceIdType.MESH,
        )
        copy.start()
        copies.append(copy)
    local = pltpu.make_async_copy(x_ref.at[me] if indexed else x_ref, out_ref.at[me], self_sem)
    local.start()
    for copy in copies:
        copy.wait_send()
    for copy in copies:
        copy.wait_recv()
    local.wait()


def exchange(x, axis, indexed, collective_id):
    n = lax.axis_size(axis)
    piece = x.shape[1:] if indexed else x.shape
    return pl.pallas_call(
        functools.partial(exchange_kernel, axis=axis, n=n, indexed=indexed),
        out_shape=jax.ShapeDtypeStruct((n,) + tuple(piece), x.dtype),
        in_specs=[pl.BlockSpec(memory_space=pl.ANY)],
        out_specs=pl.BlockSpec(memory_space=pl.ANY),
        scratch_shapes=[
            pltpu.SemaphoreType.DMA((n - 1,)),
            pltpu.SemaphoreType.DMA((n - 1,)),
            pltpu.SemaphoreType.DMA,
        ],
        compiler_params=pltpu.CompilerParams(collective_id=collective_id, has_side_effects=True),
    )(x)


def relay_gather_kernel(x_ref, out_ref, send_sem, recv_sem, self_sem, *, n):
    me = lax.axis_index("ctx")
    ring = n // 2
    z = me // 2
    side = me % 2
    partner = z * 2 + (1 - side)
    up = lax.rem(z + 1, ring) * 2 + side
    down = lax.rem(z + ring - 1, ring) * 2 + side
    barrier = pltpu.get_barrier_semaphore()
    for peer in (partner, up, down):
        pl.semaphore_signal(barrier, inc=1, device_id={"ctx": peer},
                            device_id_type=pl.DeviceIdType.MESH)
    pl.semaphore_wait(barrier, 3)
    local = pltpu.make_async_copy(x_ref, out_ref.at[me], self_sem)
    local.start()
    sends = []

    def send(slot, target, src):
        copy = pltpu.make_async_remote_copy(
            src_ref=src, dst_ref=out_ref.at[slot], send_sem=send_sem.at[len(sends)],
            recv_sem=recv_sem.at[slot], device_id={"ctx": target},
            device_id_type=pl.DeviceIdType.MESH,
        )
        copy.start()
        sends.append(copy)

    def arrive(slot):
        pltpu.make_async_remote_copy(
            src_ref=x_ref, dst_ref=out_ref.at[slot], send_sem=send_sem.at[0],
            recv_sem=recv_sem.at[slot], device_id={"ctx": partner},
            device_id_type=pl.DeviceIdType.MESH,
        ).wait_recv()

    def origin(step, offset):
        return lax.rem(z + step + 2 * ring, ring) * 2 + offset

    def send_part(slot, target, rows, sem_index):
        copy = pltpu.make_async_remote_copy(
            src_ref=out_ref.at[slot, rows], dst_ref=out_ref.at[slot, rows],
            send_sem=send_sem.at[len(sends)], recv_sem=recv_sem.at[sem_index],
            device_id={"ctx": target}, device_id_type=pl.DeviceIdType.MESH,
        )
        copy.start()
        sends.append(copy)

    def arrive_part(slot, rows, sem_index):
        pltpu.make_async_remote_copy(
            src_ref=out_ref.at[slot, rows], dst_ref=out_ref.at[slot, rows],
            send_sem=send_sem.at[0], recv_sem=recv_sem.at[sem_index],
            device_id={"ctx": partner}, device_id_type=pl.DeviceIdType.MESH,
        ).wait_recv()

    upward = ring // 2
    half = x_ref.shape[0] // 2
    top = pl.ds(0, half)
    bottom = pl.ds(half, half)
    send(me, partner, x_ref)
    send(me, up, x_ref)
    send(me, down, x_ref)
    arrive(partner)
    send(partner, up, out_ref.at[partner])
    send(partner, down, out_ref.at[partner])
    for step in range(2, upward + 1):
        for offset in (0, 1):
            slot = origin(-(step - 1), offset)
            arrive(slot)
            if step < upward:
                send(slot, up, out_ref.at[slot])
            else:
                send_part(slot, up, top, slot)
        for offset in (0, 1):
            slot = origin(step - 1, offset)
            arrive(slot)
            if step < upward:
                send(slot, down, out_ref.at[slot])
            else:
                send_part(slot, down, bottom, n + offset)
    for offset in (0, 1):
        arrive_part(origin(-upward, offset), top, origin(-upward, offset))
        arrive_part(origin(upward, offset), bottom, n + offset)
    for copy in sends:
        copy.wait_send()
    local.wait()


def relay_gather(x, collective_id):
    n = lax.axis_size("ctx")
    return pl.pallas_call(
        functools.partial(relay_gather_kernel, n=n),
        out_shape=jax.ShapeDtypeStruct((n,) + tuple(x.shape), x.dtype),
        in_specs=[pl.BlockSpec(memory_space=pl.ANY)],
        out_specs=pl.BlockSpec(memory_space=pl.ANY),
        scratch_shapes=[
            pltpu.SemaphoreType.DMA((n + 1,)),
            pltpu.SemaphoreType.DMA((n + 2,)),
            pltpu.SemaphoreType.DMA,
        ],
        compiler_params=pltpu.CompilerParams(collective_id=collective_id, has_side_effects=True),
    )(x)


def relay_reduce_kernel(t_ref, x_ref, tail_ref, out_ref, tails_ref, up_in, down_in, up_out,
                        down_out, side_out, side_in, tails_in, send_sem, recv_sem, tail_send,
                        tail_recv, *, n):
    me = lax.axis_index("ctx")
    ring = n // 2
    z = me // 2
    side = me % 2
    partner = z * 2 + (1 - side)
    up = lax.rem(z + 1, ring) * 2 + side
    down = lax.rem(z + ring - 1, ring) * 2 + side
    upward = ring // 2
    barrier = pltpu.get_barrier_semaphore()
    for d in range(1, n):
        pl.semaphore_signal(barrier, inc=1, device_id={"ctx": lax.rem(me + d, n)},
                            device_id_type=pl.DeviceIdType.MESH)
    pl.semaphore_wait(barrier, n - 1)
    tail_copies = []
    for d in range(1, n):
        copy = pltpu.make_async_remote_copy(
            src_ref=tail_ref, dst_ref=tails_in.at[me], send_sem=tail_send.at[d - 1],
            recv_sem=tail_recv.at[d - 1], device_id={"ctx": lax.rem(me + d, n)},
            device_id_type=pl.DeviceIdType.MESH,
        )
        copy.start()
        tail_copies.append(copy)
    tails_in[me] = tail_ref[...]
    sends = []

    def send(src, dst, target, sem_index):
        copy = pltpu.make_async_remote_copy(
            src_ref=src, dst_ref=dst, send_sem=send_sem.at[len(sends)],
            recv_sem=recv_sem.at[sem_index], device_id={"ctx": target},
            device_id_type=pl.DeviceIdType.MESH,
        )
        copy.start()
        sends.append(copy)
        return copy

    def own(target_z):
        base = lax.rem(target_z + 2 * ring, ring) * 2
        pieces = []
        for offset in (0, 1):
            total = jnp.zeros(x_ref.shape[1:], jnp.float32)
            for j in range(x_ref.shape[0]):
                total = total + jnp.where(t_ref[j] == base + offset, x_ref[j], 0.0)
            pieces.append(total)
        return jnp.stack(pieces)

    half = x_ref.shape[1] // 2
    top = pl.ds(0, half)
    bottom = pl.ds(half, half)
    pending_up = None
    pending_down = None
    for step in range(1, upward + 1):
        term = own(z + upward - step + 1)
        if step == 1:
            up_out[0, :, top] = term[:, :half].astype(up_out.dtype)
            pending_up = send(up_out.at[0, :, top], up_in.at[0, :, top], up, 0)
        else:
            pending_up.wait_recv()
            if step == 2:
                term = jnp.concatenate(
                    [term[:, :half] + up_in[0, :, top].astype(jnp.float32), term[:, half:]], axis=1
                )
            else:
                term = term + up_in[step - 2].astype(jnp.float32)
            up_out[step - 1] = term.astype(up_out.dtype)
            pending_up = send(up_out.at[step - 1], up_in.at[step - 1], up, step - 1)
        term = own(z - (upward - step + 1))
        if step == 1:
            down_out[0, :, bottom] = term[:, half:].astype(down_out.dtype)
            pending_down = send(down_out.at[0, :, bottom], down_in.at[0, :, bottom], down,
                                upward)
        else:
            pending_down.wait_recv()
            if step == 2:
                term = jnp.concatenate(
                    [term[:, :half], term[:, half:] + down_in[0, :, bottom].astype(jnp.float32)],
                    axis=1,
                )
            else:
                term = term + down_in[step - 2].astype(jnp.float32)
            down_out[step - 1] = term.astype(down_out.dtype)
            pending_down = send(down_out.at[step - 1], down_in.at[step - 1], down,
                                upward + step - 1)
    pending_up.wait_recv()
    pending_down.wait_recv()
    mine = (own(z) + up_in[upward - 1].astype(jnp.float32)
            + down_in[upward - 1].astype(jnp.float32))
    side_out[...] = jnp.where(side == 0, mine[1], mine[0])
    across = send(side_out, side_in, partner, 2 * upward)
    across.wait_recv()
    out_ref[...] = jnp.where(side == 0, mine[0], mine[1]) + side_in[...]
    for copy in sends:
        copy.wait_send()
    for copy in tail_copies:
        copy.wait_send()
    for copy in tail_copies:
        copy.wait_recv()
    tails_ref[...] = tails_in[...]


def relay_reduce(targets, partial, tail, n, collective_id):
    _, rows, cols = partial.shape
    ring = n // 2
    upward = ring // 2
    downward = upward
    vmem = pl.BlockSpec(memory_space=pltpu.VMEM)
    return pl.pallas_call(
        functools.partial(relay_reduce_kernel, n=n),
        out_shape=[
            jax.ShapeDtypeStruct((rows, cols), jnp.float32),
            jax.ShapeDtypeStruct((n,) + tuple(tail.shape), jnp.float32),
        ],
        in_specs=[pl.BlockSpec(memory_space=pltpu.SMEM), vmem, vmem],
        out_specs=[vmem, vmem],
        scratch_shapes=[
            pltpu.VMEM((upward, 2, rows, cols), jnp.bfloat16),
            pltpu.VMEM((downward, 2, rows, cols), jnp.bfloat16),
            pltpu.VMEM((upward, 2, rows, cols), jnp.bfloat16),
            pltpu.VMEM((downward, 2, rows, cols), jnp.bfloat16),
            pltpu.VMEM((rows, cols), jnp.float32),
            pltpu.VMEM((rows, cols), jnp.float32),
            pltpu.VMEM((n,) + tuple(tail.shape), jnp.float32),
            pltpu.SemaphoreType.DMA((upward + downward + 1,)),
            pltpu.SemaphoreType.DMA((upward + downward + 1,)),
            pltpu.SemaphoreType.DMA((n - 1,)),
            pltpu.SemaphoreType.DMA((n - 1,)),
        ],
        compiler_params=pltpu.CompilerParams(
            collective_id=collective_id, has_side_effects=True,
            vmem_limit_bytes=56 * 1024 * 1024,
        ),
    )(targets, partial, tail)


def on_device(query, key, value, output, output_gradient, parent, owner):
    count = lax.axis_size("ctx")
    me = lax.axis_index("ctx")
    tile = query.shape[1]
    width = key.shape[2]
    scale_factor = HEAD_WIDTH ** (-0.5)
    prompt_tiles = count // 8
    parent_row = parent[0]
    owner_row = owner[0]
    tiles = jnp.arange(count, dtype=jnp.int32)
    my_tile = jnp.sum(jnp.where(owner_row == me, tiles, 0))
    trained = my_tile >= prompt_tiles
    above = pick_entry(parent_row, my_tile)
    second = jnp.logical_and(trained, above >= prompt_tiles)
    slot_tiles = jnp.stack(
        [jnp.int32(0), jnp.int32(1), jnp.where(second, above, 1).astype(jnp.int32)]
    )
    slot_blocks = jnp.sum(
        jnp.where(slot_tiles[:, None] == tiles[None, :], owner_row[None, :], 0), axis=1
    ).astype(jnp.int32)
    flags = jnp.stack([trained, trained, second, trained]).astype(jnp.int32)

    pair = jnp.concatenate([key[0], value[0]], axis=1)
    gathered = relay_gather(pair, 0)
    targets = jnp.concatenate([slot_blocks, me[None].astype(jnp.int32)])
    dq, dq_sum, dk, dv, k_sum, v_sum = attention_grads(
        flags, targets, query[0], output_gradient[0], output[0], gathered, scale_factor
    )
    partial = jnp.concatenate([dk, dv], axis=2)
    total_rows = lax.axis_size("dp") * query.shape[0] * count * tile
    norm = total_rows ** (-0.5)
    wide = query.shape[2]
    tail_width = 2 * width
    tail_rows = 8
    tail = jnp.concatenate(
        [dq_sum[0], k_sum[0], v_sum[0],
         jnp.zeros((tail_rows * tail_width - wide - tail_width,), jnp.float32)]
    ).reshape(tail_rows, tail_width)
    grads, landed = relay_reduce(targets, partial, tail, count, 1)
    summed = landed[0]
    for peer in range(1, count):
        summed = summed + landed[peer]
    both = exchange(summed, "dp", False, 2)
    sums = (both[0] + both[1]).reshape(-1) * norm
    sum_q = sums[:wide]
    sum_k = sums[wide:wide + width]
    sum_v = sums[wide + width:wide + 2 * width]
    return (
        dq[None],
        grads[:, :width].astype(jnp.bfloat16)[None],
        grads[:, width:].astype(jnp.bfloat16)[None],
        sum_q,
        sum_k,
        sum_v,
    )


def solution(mesh):
    return jax.shard_map(
        on_device,
        mesh=mesh,
        in_specs=(
            P("dp", "ctx", "head"),
            P("dp", "ctx", "head"),
            P("dp", "ctx", "head"),
            P("dp", "ctx", "head"),
            P("dp", "ctx", "head"),
            P("dp", None),
            P("dp", None),
        ),
        out_specs=(
            P("dp", "ctx", "head"),
            P("dp", "ctx", "head"),
            P("dp", "ctx", "head"),
            P("head"),
            P("head"),
            P("head"),
        ),
        check_vma=False,
    )
```

```python
import functools

import jax
import jax.numpy as jnp
from jax import lax
from jax.experimental import pallas as pl
from jax.experimental.pallas import tpu as pltpu
from jax.sharding import PartitionSpec as P

HEAD_WIDTH = 128

NEGATIVE_FILL = -1e30


def pick_entry(vector, index):
    spots = jnp.arange(vector.shape[0], dtype=jnp.int32)
    return jnp.sum(jnp.where(spots == index, vector, 0), axis=0)


def pick_rows(matrix, index):
    spots = jnp.arange(matrix.shape[0], dtype=jnp.int32)
    return jnp.sum(jnp.where((spots == index)[:, None], matrix, 0.0), axis=0)


def attention_grads_kernel(flags_ref, blocks_ref, q_ref, g_ref, o_ref, k0, k1, k2, k3, v0, v1, v2,
                           v3, dq_ref, dqsum_ref, kv_ref, ksum_ref, vsum_ref, s_scr, *, scale):
    head = pl.program_id(0)
    k_refs = (k0, k1, k2, k3)
    v_refs = (v0, v1, v2, v3)
    slots = len(k_refs)

    width = q_ref.shape[1]
    dk_ref = kv_ref.at[:, :, pl.ds(0, width)]
    dv_ref = kv_ref.at[:, :, pl.ds(width, width)]

    @pl.when(head == 0)
    def _():
        kv_ref[...] = jnp.zeros_like(kv_ref)

    q = q_ref[...]
    g = g_ref[...]
    o = o_ref[...]
    rows = q.shape[0]
    delta = jnp.sum(g.astype(jnp.float32) * o.astype(jnp.float32), axis=1, keepdims=True)
    causal = (lax.broadcasted_iota(jnp.int32, (rows, rows), 0)
              >= lax.broadcasted_iota(jnp.int32, (rows, rows), 1))
    nt = (((1,), (1,)), ((), ()))
    tn = (((0,), (0,)), ((), ()))

    top = jnp.full((rows, 1), NEGATIVE_FILL, jnp.float32)
    for j in range(slots):
        keep = flags_ref[j] > 0
        if j == slots - 1:
            keep = jnp.logical_and(keep, causal)
        scores = lax.dot_general(q, k_refs[j][...], nt, preferred_element_type=jnp.float32) * scale
        scores = jnp.where(keep, scores, NEGATIVE_FILL)
        s_scr[j] = scores
        top = jnp.maximum(top, jnp.max(scores, axis=1, keepdims=True))

    total = jnp.zeros((rows, 1), jnp.float32)
    for j in range(slots):
        keep = flags_ref[j] > 0
        if j == slots - 1:
            keep = jnp.logical_and(keep, causal)
        probs = jnp.where(keep, jnp.exp(s_scr[j] - top), 0.0)
        s_scr[j] = probs
        total = total + jnp.sum(probs, axis=1, keepdims=True)
    inverse = jnp.where(total > 0, 1.0 / jnp.where(total > 0, total, 1.0), 0.0)

    dq = jnp.zeros((rows, q.shape[1]), jnp.float32)
    for j in range(slots):
        probs = s_scr[j] * inverse
        dv_ref[j] += lax.dot_general(probs.astype(jnp.bfloat16), g, tn,
                                     preferred_element_type=jnp.float32)
        dprobs = lax.dot_general(g, v_refs[j][...], nt, preferred_element_type=jnp.float32)
        dscores = (probs * (dprobs - delta)).astype(jnp.bfloat16)
        dq = dq + jnp.dot(dscores, k_refs[j][...], preferred_element_type=jnp.float32)
        dk_ref[j] += lax.dot_general(dscores, q, tn, preferred_element_type=jnp.float32) * scale
    dq = dq * scale
    dq_ref[...] = dq.astype(dq_ref.dtype)
    dqsum_ref[...] = jnp.sum(dq, axis=0, keepdims=True)

    @pl.when(head == pl.num_programs(0) - 1)
    def _():
        ksum_ref[...] = jnp.sum(jnp.sum(dk_ref[...], axis=0), axis=0, keepdims=True)
        vsum_ref[...] = jnp.sum(jnp.sum(dv_ref[...], axis=0), axis=0, keepdims=True)


def attention_grads(flags, blocks, q, g, o, gathered, scale):
    rows, wide = q.shape
    slots = blocks.shape[0]
    heads = wide // HEAD_WIDTH
    col = pl.BlockSpec((rows, HEAD_WIDTH), lambda h, f, b: (0, h))
    line = pl.BlockSpec((1, HEAD_WIDTH), lambda h, f, b: (0, h))
    fixed = pl.BlockSpec((1, HEAD_WIDTH), lambda h, f, b: (0, 0))
    pair_spec = pl.BlockSpec((slots, rows, 2 * HEAD_WIDTH), lambda h, f, b: (0, 0, 0))

    def pick(j, part):
        return pl.BlockSpec((None, rows, HEAD_WIDTH), lambda h, f, b: (b[j], 0, part))

    return pl.pallas_call(
        functools.partial(attention_grads_kernel, scale=scale),
        grid_spec=pltpu.PrefetchScalarGridSpec(
            num_scalar_prefetch=2,
            grid=(heads,),
            in_specs=[col, col, col] + [pick(j, 0) for j in range(slots)]
            + [pick(j, 1) for j in range(slots)],
            out_specs=[col, line, pair_spec, fixed, fixed],
            scratch_shapes=[pltpu.VMEM((slots, rows, rows), jnp.float32)],
        ),
        out_shape=[
            jax.ShapeDtypeStruct((rows, wide), jnp.bfloat16),
            jax.ShapeDtypeStruct((1, wide), jnp.float32),
            jax.ShapeDtypeStruct((slots, rows, 2 * HEAD_WIDTH), jnp.float32),
            jax.ShapeDtypeStruct((1, HEAD_WIDTH), jnp.float32),
            jax.ShapeDtypeStruct((1, HEAD_WIDTH), jnp.float32),
        ],
        compiler_params=pltpu.CompilerParams(
            dimension_semantics=("arbitrary",), vmem_limit_bytes=48 * 1024 * 1024
        ),
    )(flags, blocks, q, g, o, *([gathered] * (2 * slots)))


def exchange_kernel(x_ref, out_ref, send_sem, recv_sem, self_sem, *, axis, n, indexed):
    me = lax.axis_index(axis)
    barrier = pltpu.get_barrier_semaphore()
    for d in range(1, n):
        pl.semaphore_signal(
            barrier, inc=1, device_id={axis: lax.rem(me + d, n)},
            device_id_type=pl.DeviceIdType.MESH,
        )
    pl.semaphore_wait(barrier, n - 1)
    copies = []
    for d in range(1, n):
        peer = lax.rem(me + d, n)
        copy = pltpu.make_async_remote_copy(
            src_ref=x_ref.at[peer] if indexed else x_ref,
            dst_ref=out_ref.at[me],
            send_sem=send_sem.at[d - 1],
            recv_sem=recv_sem.at[d - 1],
            device_id={axis: peer},
            device_id_type=pl.DeviceIdType.MESH,
        )
        copy.start()
        copies.append(copy)
    local = pltpu.make_async_copy(x_ref.at[me] if indexed else x_ref, out_ref.at[me], self_sem)
    local.start()
    for copy in copies:
        copy.wait_send()
    for copy in copies:
        copy.wait_recv()
    local.wait()


def exchange(x, axis, indexed, collective_id):
    n = lax.axis_size(axis)
    piece = x.shape[1:] if indexed else x.shape
    return pl.pallas_call(
        functools.partial(exchange_kernel, axis=axis, n=n, indexed=indexed),
        out_shape=jax.ShapeDtypeStruct((n,) + tuple(piece), x.dtype),
        in_specs=[pl.BlockSpec(memory_space=pl.ANY)],
        out_specs=pl.BlockSpec(memory_space=pl.ANY),
        scratch_shapes=[
            pltpu.SemaphoreType.DMA((n - 1,)),
            pltpu.SemaphoreType.DMA((n - 1,)),
            pltpu.SemaphoreType.DMA,
        ],
        compiler_params=pltpu.CompilerParams(collective_id=collective_id, has_side_effects=True),
    )(x)


def relay_gather_kernel(x_ref, out_ref, send_sem, recv_sem, self_sem, *, n):
    me = lax.axis_index("ctx")
    ring = n // 2
    z = me // 2
    side = me % 2
    partner = z * 2 + (1 - side)
    up = lax.rem(z + 1, ring) * 2 + side
    down = lax.rem(z + ring - 1, ring) * 2 + side
    barrier = pltpu.get_barrier_semaphore()
    for peer in (partner, up, down):
        pl.semaphore_signal(barrier, inc=1, device_id={"ctx": peer},
                            device_id_type=pl.DeviceIdType.MESH)
    pl.semaphore_wait(barrier, 3)
    local = pltpu.make_async_copy(x_ref, out_ref.at[me], self_sem)
    local.start()
    sends = []

    def send(slot, target, src):
        copy = pltpu.make_async_remote_copy(
            src_ref=src, dst_ref=out_ref.at[slot], send_sem=send_sem.at[len(sends)],
            recv_sem=recv_sem.at[slot], device_id={"ctx": target},
            device_id_type=pl.DeviceIdType.MESH,
        )
        copy.start()
        sends.append(copy)

    def arrive(slot):
        pltpu.make_async_remote_copy(
            src_ref=x_ref, dst_ref=out_ref.at[slot], send_sem=send_sem.at[0],
            recv_sem=recv_sem.at[slot], device_id={"ctx": partner},
            device_id_type=pl.DeviceIdType.MESH,
        ).wait_recv()

    def origin(step, offset):
        return lax.rem(z + step + 2 * ring, ring) * 2 + offset

    def send_part(slot, target, rows, sem_index):
        copy = pltpu.make_async_remote_copy(
            src_ref=out_ref.at[slot, rows], dst_ref=out_ref.at[slot, rows],
            send_sem=send_sem.at[len(sends)], recv_sem=recv_sem.at[sem_index],
            device_id={"ctx": target}, device_id_type=pl.DeviceIdType.MESH,
        )
        copy.start()
        sends.append(copy)

    def arrive_part(slot, rows, sem_index):
        pltpu.make_async_remote_copy(
            src_ref=out_ref.at[slot, rows], dst_ref=out_ref.at[slot, rows],
            send_sem=send_sem.at[0], recv_sem=recv_sem.at[sem_index],
            device_id={"ctx": partner}, device_id_type=pl.DeviceIdType.MESH,
        ).wait_recv()

    upward = ring // 2
    half = x_ref.shape[0] // 2
    top = pl.ds(0, half)
    bottom = pl.ds(half, half)
    send(me, partner, x_ref)
    send(me, up, x_ref)
    send(me, down, x_ref)
    arrive(partner)
    send(partner, up, out_ref.at[partner])
    send(partner, down, out_ref.at[partner])
    for step in range(2, upward + 1):
        for offset in (0, 1):
            slot = origin(-(step - 1), offset)
            arrive(slot)
            if step < upward:
                send(slot, up, out_ref.at[slot])
            else:
                send_part(slot, up, top, slot)
        for offset in (0, 1):
            slot = origin(step - 1, offset)
            arrive(slot)
            if step < upward:
                send(slot, down, out_ref.at[slot])
            else:
                send_part(slot, down, bottom, n + offset)
    for offset in (0, 1):
        arrive_part(origin(-upward, offset), top, origin(-upward, offset))
        arrive_part(origin(upward, offset), bottom, n + offset)
    for copy in sends:
        copy.wait_send()
    local.wait()


def relay_gather(x, collective_id):
    n = lax.axis_size("ctx")
    return pl.pallas_call(
        functools.partial(relay_gather_kernel, n=n),
        out_shape=jax.ShapeDtypeStruct((n,) + tuple(x.shape), x.dtype),
        in_specs=[pl.BlockSpec(memory_space=pl.ANY)],
        out_specs=pl.BlockSpec(memory_space=pl.ANY),
        scratch_shapes=[
            pltpu.SemaphoreType.DMA((n + 1,)),
            pltpu.SemaphoreType.DMA((n + 2,)),
            pltpu.SemaphoreType.DMA,
        ],
        compiler_params=pltpu.CompilerParams(collective_id=collective_id, has_side_effects=True),
    )(x)


def relay_reduce_kernel(t_ref, x_ref, tail_ref, dk_ref, dv_ref, tails_ref, up_in, down_in, up_out,
                        down_out, side_out, side_in, tails_in, send_sem, recv_sem, tail_send,
                        tail_recv, *, n):
    me = lax.axis_index("ctx")
    ring = n // 2
    z = me // 2
    side = me % 2
    partner = z * 2 + (1 - side)
    up = lax.rem(z + 1, ring) * 2 + side
    down = lax.rem(z + ring - 1, ring) * 2 + side
    upward = ring // 2
    barrier = pltpu.get_barrier_semaphore()
    for d in range(1, n):
        pl.semaphore_signal(barrier, inc=1, device_id={"ctx": lax.rem(me + d, n)},
                            device_id_type=pl.DeviceIdType.MESH)
    pl.semaphore_wait(barrier, n - 1)
    tail_copies = []
    for d in range(1, n):
        copy = pltpu.make_async_remote_copy(
            src_ref=tail_ref, dst_ref=tails_in.at[me], send_sem=tail_send.at[d - 1],
            recv_sem=tail_recv.at[d - 1], device_id={"ctx": lax.rem(me + d, n)},
            device_id_type=pl.DeviceIdType.MESH,
        )
        copy.start()
        tail_copies.append(copy)
    tails_in[me] = tail_ref[...]
    sends = []

    def send(src, dst, target, sem_index):
        copy = pltpu.make_async_remote_copy(
            src_ref=src, dst_ref=dst, send_sem=send_sem.at[len(sends)],
            recv_sem=recv_sem.at[sem_index], device_id={"ctx": target},
            device_id_type=pl.DeviceIdType.MESH,
        )
        copy.start()
        sends.append(copy)
        return copy

    def own(target_z):
        base = lax.rem(target_z + 2 * ring, ring) * 2
        pieces = []
        for offset in (0, 1):
            total = jnp.zeros(x_ref.shape[1:], jnp.float32)
            for j in range(x_ref.shape[0]):
                total = total + jnp.where(t_ref[j] == base + offset, x_ref[j], 0.0)
            pieces.append(total)
        return jnp.stack(pieces)

    half = x_ref.shape[1] // 2
    top = pl.ds(0, half)
    bottom = pl.ds(half, half)
    pending_up = None
    pending_down = None
    for step in range(1, upward + 1):
        term = own(z + upward - step + 1)
        if step == 1:
            up_out[0, :, top] = term[:, :half].astype(up_out.dtype)
            pending_up = send(up_out.at[0, :, top], up_in.at[0, :, top], up, 0)
        else:
            pending_up.wait_recv()
            if step == 2:
                term = jnp.concatenate(
                    [term[:, :half] + up_in[0, :, top].astype(jnp.float32), term[:, half:]], axis=1
                )
            else:
                term = term + up_in[step - 2].astype(jnp.float32)
            up_out[step - 1] = term.astype(up_out.dtype)
            pending_up = send(up_out.at[step - 1], up_in.at[step - 1], up, step - 1)
        term = own(z - (upward - step + 1))
        if step == 1:
            down_out[0, :, bottom] = term[:, half:].astype(down_out.dtype)
            pending_down = send(down_out.at[0, :, bottom], down_in.at[0, :, bottom], down,
                                upward)
        else:
            pending_down.wait_recv()
            if step == 2:
                term = jnp.concatenate(
                    [term[:, :half], term[:, half:] + down_in[0, :, bottom].astype(jnp.float32)],
                    axis=1,
                )
            else:
                term = term + down_in[step - 2].astype(jnp.float32)
            down_out[step - 1] = term.astype(down_out.dtype)
            pending_down = send(down_out.at[step - 1], down_in.at[step - 1], down,
                                upward + step - 1)
    pending_up.wait_recv()
    pending_down.wait_recv()
    mine = (own(z) + up_in[upward - 1].astype(jnp.float32)
            + down_in[upward - 1].astype(jnp.float32))
    side_out[...] = jnp.where(side == 0, mine[1], mine[0])
    across = send(side_out, side_in, partner, 2 * upward)
    across.wait_recv()
    grads = jnp.where(side == 0, mine[0], mine[1]) + side_in[...]
    width = dk_ref.shape[1]
    dk_ref[...] = grads[:, :width].astype(dk_ref.dtype)
    dv_ref[...] = grads[:, width:].astype(dv_ref.dtype)
    for copy in sends:
        copy.wait_send()
    for copy in tail_copies:
        copy.wait_send()
    for copy in tail_copies:
        copy.wait_recv()
    summed = tails_in[0]
    for peer in range(1, n):
        summed = summed + tails_in[peer]
    tails_ref[...] = summed


def relay_reduce(targets, partial, tail, n, collective_id):
    _, rows, cols = partial.shape
    ring = n // 2
    upward = ring // 2
    downward = upward
    vmem = pl.BlockSpec(memory_space=pltpu.VMEM)
    return pl.pallas_call(
        functools.partial(relay_reduce_kernel, n=n),
        out_shape=[
            jax.ShapeDtypeStruct((rows, cols // 2), jnp.bfloat16),
            jax.ShapeDtypeStruct((rows, cols // 2), jnp.bfloat16),
            jax.ShapeDtypeStruct(tuple(tail.shape), jnp.float32),
        ],
        in_specs=[pl.BlockSpec(memory_space=pltpu.SMEM), vmem, vmem],
        out_specs=[vmem, vmem, vmem],
        scratch_shapes=[
            pltpu.VMEM((upward, 2, rows, cols), jnp.bfloat16),
            pltpu.VMEM((downward, 2, rows, cols), jnp.bfloat16),
            pltpu.VMEM((upward, 2, rows, cols), jnp.bfloat16),
            pltpu.VMEM((downward, 2, rows, cols), jnp.bfloat16),
            pltpu.VMEM((rows, cols), jnp.float32),
            pltpu.VMEM((rows, cols), jnp.float32),
            pltpu.VMEM((n,) + tuple(tail.shape), jnp.float32),
            pltpu.SemaphoreType.DMA((upward + downward + 1,)),
            pltpu.SemaphoreType.DMA((upward + downward + 1,)),
            pltpu.SemaphoreType.DMA((n - 1,)),
            pltpu.SemaphoreType.DMA((n - 1,)),
        ],
        compiler_params=pltpu.CompilerParams(
            collective_id=collective_id, has_side_effects=True,
            vmem_limit_bytes=56 * 1024 * 1024,
        ),
    )(targets, partial, tail)


def on_device(query, key, value, output, output_gradient, parent, owner):
    count = lax.axis_size("ctx")
    me = lax.axis_index("ctx")
    tile = query.shape[1]
    width = key.shape[2]
    scale_factor = HEAD_WIDTH ** (-0.5)
    prompt_tiles = count // 8
    parent_row = parent[0]
    owner_row = owner[0]
    tiles = jnp.arange(count, dtype=jnp.int32)
    my_tile = jnp.sum(jnp.where(owner_row == me, tiles, 0))
    trained = my_tile >= prompt_tiles
    above = pick_entry(parent_row, my_tile)
    second = jnp.logical_and(trained, above >= prompt_tiles)
    slot_tiles = jnp.stack(
        [jnp.int32(0), jnp.int32(1), jnp.where(second, above, 1).astype(jnp.int32)]
    )
    slot_blocks = jnp.sum(
        jnp.where(slot_tiles[:, None] == tiles[None, :], owner_row[None, :], 0), axis=1
    ).astype(jnp.int32)
    flags = jnp.stack([trained, trained, second, trained]).astype(jnp.int32)

    pair = jnp.concatenate([key[0], value[0]], axis=1)
    gathered = relay_gather(pair, 0)
    targets = jnp.concatenate([slot_blocks, me[None].astype(jnp.int32)])
    dq, dq_sum, partial, k_sum, v_sum = attention_grads(
        flags, targets, query[0], output_gradient[0], output[0], gathered, scale_factor
    )
    total_rows = lax.axis_size("dp") * query.shape[0] * count * tile
    norm = total_rows ** (-0.5)
    wide = query.shape[2]
    tail_width = 2 * width
    tail_rows = 8
    tail = jnp.concatenate(
        [dq_sum[0], k_sum[0], v_sum[0],
         jnp.zeros((tail_rows * tail_width - wide - tail_width,), jnp.float32)]
    ).reshape(tail_rows, tail_width)
    d_key, d_value, summed = relay_reduce(targets, partial, tail, count, 1)
    both = exchange(summed, "dp", False, 2)
    sums = (both[0] + both[1]).reshape(-1) * norm
    sum_q = sums[:wide]
    sum_k = sums[wide:wide + width]
    sum_v = sums[wide + width:wide + 2 * width]
    return (
        dq[None],
        d_key[None],
        d_value[None],
        sum_q,
        sum_k,
        sum_v,
    )


def solution(mesh):
    return jax.shard_map(
        on_device,
        mesh=mesh,
        in_specs=(
            P("dp", "ctx", "head"),
            P("dp", "ctx", "head"),
            P("dp", "ctx", "head"),
            P("dp", "ctx", "head"),
            P("dp", "ctx", "head"),
            P("dp", None),
            P("dp", None),
        ),
        out_specs=(
            P("dp", "ctx", "head"),
            P("dp", "ctx", "head"),
            P("dp", "ctx", "head"),
            P("head"),
            P("head"),
            P("head"),
        ),
        check_vma=False,
    )
```

```python
import functools

import jax
import jax.numpy as jnp
from jax import lax
from jax.experimental import pallas as pl
from jax.experimental.pallas import tpu as pltpu
from jax.sharding import PartitionSpec as P

HEAD_WIDTH = 128

NEGATIVE_FILL = -1e30


def pick_entry(vector, index):
    spots = jnp.arange(vector.shape[0], dtype=jnp.int32)
    return jnp.sum(jnp.where(spots == index, vector, 0), axis=0)


def pick_rows(matrix, index):
    spots = jnp.arange(matrix.shape[0], dtype=jnp.int32)
    return jnp.sum(jnp.where((spots == index)[:, None], matrix, 0.0), axis=0)


def attention_grads_kernel(flags_ref, blocks_ref, q_ref, g_ref, o_ref, k0, k1, k2, k3, v0, v1, v2,
                           v3, dq_ref, dqsum_ref, kv_ref, ksum_ref, vsum_ref, s_scr, *, scale):
    head = pl.program_id(0)
    k_refs = (k0, k1, k2, k3)
    v_refs = (v0, v1, v2, v3)
    slots = len(k_refs)

    width = q_ref.shape[1]
    dk_ref = kv_ref.at[:, :, pl.ds(0, width)]
    dv_ref = kv_ref.at[:, :, pl.ds(width, width)]

    @pl.when(head == 0)
    def _():
        kv_ref[...] = jnp.zeros_like(kv_ref)

    q = q_ref[...]
    g = g_ref[...]
    o = o_ref[...]
    rows = q.shape[0]
    delta = jnp.sum(g.astype(jnp.float32) * o.astype(jnp.float32), axis=1, keepdims=True)
    causal = (lax.broadcasted_iota(jnp.int32, (rows, rows), 0)
              >= lax.broadcasted_iota(jnp.int32, (rows, rows), 1))
    nt = (((1,), (1,)), ((), ()))
    tn = (((0,), (0,)), ((), ()))

    top = jnp.full((rows, 1), NEGATIVE_FILL, jnp.float32)
    for j in range(slots):
        keep = flags_ref[j] > 0
        if j == slots - 1:
            keep = jnp.logical_and(keep, causal)
        scores = lax.dot_general(q, k_refs[j][...], nt, preferred_element_type=jnp.float32) * scale
        scores = jnp.where(keep, scores, NEGATIVE_FILL)
        s_scr[j] = scores
        top = jnp.maximum(top, jnp.max(scores, axis=1, keepdims=True))

    total = jnp.zeros((rows, 1), jnp.float32)
    for j in range(slots):
        keep = flags_ref[j] > 0
        if j == slots - 1:
            keep = jnp.logical_and(keep, causal)
        probs = jnp.where(keep, jnp.exp(s_scr[j] - top), 0.0)
        s_scr[j] = probs
        total = total + jnp.sum(probs, axis=1, keepdims=True)
    inverse = jnp.where(total > 0, 1.0 / jnp.where(total > 0, total, 1.0), 0.0)

    dq = jnp.zeros((rows, q.shape[1]), jnp.float32)
    for j in range(slots):
        probs = s_scr[j] * inverse
        dv_ref[j] += lax.dot_general(probs.astype(jnp.bfloat16), g, tn,
                                     preferred_element_type=jnp.float32)
        dprobs = lax.dot_general(g, v_refs[j][...], nt, preferred_element_type=jnp.float32)
        dscores = (probs * (dprobs - delta)).astype(jnp.bfloat16)
        dq = dq + jnp.dot(dscores, k_refs[j][...], preferred_element_type=jnp.float32)
        dk_ref[j] += lax.dot_general(dscores, q, tn, preferred_element_type=jnp.float32) * scale
    dq = dq * scale
    dq_ref[...] = dq.astype(dq_ref.dtype)
    dqsum_ref[...] = jnp.sum(dq, axis=0, keepdims=True)

    @pl.when(head == pl.num_programs(0) - 1)
    def _():
        ksum_ref[...] = jnp.sum(jnp.sum(dk_ref[...], axis=0), axis=0, keepdims=True)
        vsum_ref[...] = jnp.sum(jnp.sum(dv_ref[...], axis=0), axis=0, keepdims=True)


def attention_grads(flags, blocks, q, g, o, gathered, scale):
    rows, wide = q.shape
    slots = blocks.shape[0]
    heads = wide // HEAD_WIDTH
    col = pl.BlockSpec((rows, HEAD_WIDTH), lambda h, f, b: (0, h))
    line = pl.BlockSpec((1, HEAD_WIDTH), lambda h, f, b: (0, h))
    fixed = pl.BlockSpec((1, HEAD_WIDTH), lambda h, f, b: (0, 0))
    pair_spec = pl.BlockSpec((slots, rows, 2 * HEAD_WIDTH), lambda h, f, b: (0, 0, 0))

    def pick(j, part):
        return pl.BlockSpec((None, rows, HEAD_WIDTH), lambda h, f, b: (b[j], 0, part))

    return pl.pallas_call(
        functools.partial(attention_grads_kernel, scale=scale),
        grid_spec=pltpu.PrefetchScalarGridSpec(
            num_scalar_prefetch=2,
            grid=(heads,),
            in_specs=[col, col, col] + [pick(j, 0) for j in range(slots)]
            + [pick(j, 1) for j in range(slots)],
            out_specs=[col, line, pair_spec, fixed, fixed],
            scratch_shapes=[pltpu.VMEM((slots, rows, rows), jnp.float32)],
        ),
        out_shape=[
            jax.ShapeDtypeStruct((rows, wide), jnp.bfloat16),
            jax.ShapeDtypeStruct((1, wide), jnp.float32),
            jax.ShapeDtypeStruct((slots, rows, 2 * HEAD_WIDTH), jnp.float32),
            jax.ShapeDtypeStruct((1, HEAD_WIDTH), jnp.float32),
            jax.ShapeDtypeStruct((1, HEAD_WIDTH), jnp.float32),
        ],
        compiler_params=pltpu.CompilerParams(
            dimension_semantics=("arbitrary",), vmem_limit_bytes=48 * 1024 * 1024
        ),
    )(flags, blocks, q, g, o, *([gathered] * (2 * slots)))


def exchange_kernel(x_ref, out_ref, send_sem, recv_sem, self_sem, *, axis, n, indexed):
    me = lax.axis_index(axis)
    barrier = pltpu.get_barrier_semaphore()
    for d in range(1, n):
        pl.semaphore_signal(
            barrier, inc=1, device_id={axis: lax.rem(me + d, n)},
            device_id_type=pl.DeviceIdType.MESH,
        )
    pl.semaphore_wait(barrier, n - 1)
    copies = []
    for d in range(1, n):
        peer = lax.rem(me + d, n)
        copy = pltpu.make_async_remote_copy(
            src_ref=x_ref.at[peer] if indexed else x_ref,
            dst_ref=out_ref.at[me],
            send_sem=send_sem.at[d - 1],
            recv_sem=recv_sem.at[d - 1],
            device_id={axis: peer},
            device_id_type=pl.DeviceIdType.MESH,
        )
        copy.start()
        copies.append(copy)
    local = pltpu.make_async_copy(x_ref.at[me] if indexed else x_ref, out_ref.at[me], self_sem)
    local.start()
    for copy in copies:
        copy.wait_send()
    for copy in copies:
        copy.wait_recv()
    local.wait()


def exchange(x, axis, indexed, collective_id):
    n = lax.axis_size(axis)
    piece = x.shape[1:] if indexed else x.shape
    return pl.pallas_call(
        functools.partial(exchange_kernel, axis=axis, n=n, indexed=indexed),
        out_shape=jax.ShapeDtypeStruct((n,) + tuple(piece), x.dtype),
        in_specs=[pl.BlockSpec(memory_space=pl.ANY)],
        out_specs=pl.BlockSpec(memory_space=pl.ANY),
        scratch_shapes=[
            pltpu.SemaphoreType.DMA((n - 1,)),
            pltpu.SemaphoreType.DMA((n - 1,)),
            pltpu.SemaphoreType.DMA,
        ],
        compiler_params=pltpu.CompilerParams(collective_id=collective_id, has_side_effects=True),
    )(x)


def relay_gather_kernel(x_ref, out_ref, send_sem, recv_sem, self_sem, *, n):
    me = lax.axis_index("ctx")
    ring = n // 2
    z = me // 2
    side = me % 2
    partner = z * 2 + (1 - side)
    up = lax.rem(z + 1, ring) * 2 + side
    down = lax.rem(z + ring - 1, ring) * 2 + side
    barrier = pltpu.get_barrier_semaphore()
    for peer in (partner, up, down):
        pl.semaphore_signal(barrier, inc=1, device_id={"ctx": peer},
                            device_id_type=pl.DeviceIdType.MESH)
    pl.semaphore_wait(barrier, 3)
    local = pltpu.make_async_copy(x_ref, out_ref.at[me], self_sem)
    local.start()
    sends = []

    def send(slot, target, src):
        copy = pltpu.make_async_remote_copy(
            src_ref=src, dst_ref=out_ref.at[slot], send_sem=send_sem.at[len(sends)],
            recv_sem=recv_sem.at[slot], device_id={"ctx": target},
            device_id_type=pl.DeviceIdType.MESH,
        )
        copy.start()
        sends.append(copy)

    def arrive(slot):
        pltpu.make_async_remote_copy(
            src_ref=x_ref, dst_ref=out_ref.at[slot], send_sem=send_sem.at[0],
            recv_sem=recv_sem.at[slot], device_id={"ctx": partner},
            device_id_type=pl.DeviceIdType.MESH,
        ).wait_recv()

    def origin(step, offset):
        return lax.rem(z + step + 2 * ring, ring) * 2 + offset

    def send_part(slot, target, rows, sem_index):
        copy = pltpu.make_async_remote_copy(
            src_ref=out_ref.at[slot, rows], dst_ref=out_ref.at[slot, rows],
            send_sem=send_sem.at[len(sends)], recv_sem=recv_sem.at[sem_index],
            device_id={"ctx": target}, device_id_type=pl.DeviceIdType.MESH,
        )
        copy.start()
        sends.append(copy)

    def arrive_part(slot, rows, sem_index):
        pltpu.make_async_remote_copy(
            src_ref=out_ref.at[slot, rows], dst_ref=out_ref.at[slot, rows],
            send_sem=send_sem.at[0], recv_sem=recv_sem.at[sem_index],
            device_id={"ctx": partner}, device_id_type=pl.DeviceIdType.MESH,
        ).wait_recv()

    upward = ring // 2
    half = x_ref.shape[0] // 2
    top = pl.ds(0, half)
    bottom = pl.ds(half, half)
    send(me, partner, x_ref)
    send(me, up, x_ref)
    send(me, down, x_ref)
    arrive(partner)
    send(partner, up, out_ref.at[partner])
    send(partner, down, out_ref.at[partner])
    for step in range(2, upward + 1):
        for offset in (0, 1):
            slot = origin(-(step - 1), offset)
            arrive(slot)
            if step < upward:
                send(slot, up, out_ref.at[slot])
            else:
                send_part(slot, up, top, slot)
        for offset in (0, 1):
            slot = origin(step - 1, offset)
            arrive(slot)
            if step < upward:
                send(slot, down, out_ref.at[slot])
            else:
                send_part(slot, down, bottom, n + offset)
    for offset in (0, 1):
        arrive_part(origin(-upward, offset), top, origin(-upward, offset))
        arrive_part(origin(upward, offset), bottom, n + offset)
    for copy in sends:
        copy.wait_send()
    local.wait()


def relay_gather(x, collective_id):
    n = lax.axis_size("ctx")
    return pl.pallas_call(
        functools.partial(relay_gather_kernel, n=n),
        out_shape=jax.ShapeDtypeStruct((n,) + tuple(x.shape), x.dtype),
        in_specs=[pl.BlockSpec(memory_space=pl.ANY)],
        out_specs=pl.BlockSpec(memory_space=pl.ANY),
        scratch_shapes=[
            pltpu.SemaphoreType.DMA((n + 1,)),
            pltpu.SemaphoreType.DMA((n + 2,)),
            pltpu.SemaphoreType.DMA,
        ],
        compiler_params=pltpu.CompilerParams(collective_id=collective_id, has_side_effects=True),
    )(x)


def relay_reduce_kernel(t_ref, x_ref, tail_ref, out_ref, tails_ref, up_in, down_in, up_out,
                        down_out, side_out, side_in, tails_in, send_sem, recv_sem, tail_send,
                        tail_recv, *, n):
    me = lax.axis_index("ctx")
    ring = n // 2
    z = me // 2
    side = me % 2
    partner = z * 2 + (1 - side)
    up = lax.rem(z + 1, ring) * 2 + side
    down = lax.rem(z + ring - 1, ring) * 2 + side
    upward = ring // 2
    barrier = pltpu.get_barrier_semaphore()
    for d in range(1, n):
        pl.semaphore_signal(barrier, inc=1, device_id={"ctx": lax.rem(me + d, n)},
                            device_id_type=pl.DeviceIdType.MESH)
    pl.semaphore_wait(barrier, n - 1)
    tail_copies = []
    for d in range(1, n):
        copy = pltpu.make_async_remote_copy(
            src_ref=tail_ref, dst_ref=tails_in.at[me], send_sem=tail_send.at[d - 1],
            recv_sem=tail_recv.at[d - 1], device_id={"ctx": lax.rem(me + d, n)},
            device_id_type=pl.DeviceIdType.MESH,
        )
        copy.start()
        tail_copies.append(copy)
    tails_in[me] = tail_ref[...]
    sends = []

    def send(src, dst, target, sem_index):
        copy = pltpu.make_async_remote_copy(
            src_ref=src, dst_ref=dst, send_sem=send_sem.at[len(sends)],
            recv_sem=recv_sem.at[sem_index], device_id={"ctx": target},
            device_id_type=pl.DeviceIdType.MESH,
        )
        copy.start()
        sends.append(copy)
        return copy

    def own(target_z):
        base = lax.rem(target_z + 2 * ring, ring) * 2
        pieces = []
        for offset in (0, 1):
            total = jnp.zeros(x_ref.shape[1:], jnp.float32)
            for j in range(x_ref.shape[0]):
                total = total + jnp.where(t_ref[j] == base + offset, x_ref[j], 0.0)
            pieces.append(total)
        return jnp.stack(pieces)

    half = x_ref.shape[1] // 2
    top = pl.ds(0, half)
    bottom = pl.ds(half, half)
    pending_up = None
    pending_down = None
    for step in range(1, upward + 1):
        term = own(z + upward - step + 1)
        if step == 1:
            up_out[0, :, top] = term[:, :half].astype(up_out.dtype)
            pending_up = send(up_out.at[0, :, top], up_in.at[0, :, top], up, 0)
        else:
            pending_up.wait_recv()
            if step == 2:
                term = jnp.concatenate(
                    [term[:, :half] + up_in[0, :, top].astype(jnp.float32), term[:, half:]], axis=1
                )
            else:
                term = term + up_in[step - 2].astype(jnp.float32)
            up_out[step - 1] = term.astype(up_out.dtype)
            pending_up = send(up_out.at[step - 1], up_in.at[step - 1], up, step - 1)
        term = own(z - (upward - step + 1))
        if step == 1:
            down_out[0, :, bottom] = term[:, half:].astype(down_out.dtype)
            pending_down = send(down_out.at[0, :, bottom], down_in.at[0, :, bottom], down,
                                upward)
        else:
            pending_down.wait_recv()
            if step == 2:
                term = jnp.concatenate(
                    [term[:, :half], term[:, half:] + down_in[0, :, bottom].astype(jnp.float32)],
                    axis=1,
                )
            else:
                term = term + down_in[step - 2].astype(jnp.float32)
            down_out[step - 1] = term.astype(down_out.dtype)
            pending_down = send(down_out.at[step - 1], down_in.at[step - 1], down,
                                upward + step - 1)
    pending_up.wait_recv()
    pending_down.wait_recv()
    mine = (own(z) + up_in[upward - 1].astype(jnp.float32)
            + down_in[upward - 1].astype(jnp.float32))
    side_out[...] = jnp.where(side == 0, mine[1], mine[0])
    across = send(side_out, side_in, partner, 2 * upward)
    across.wait_recv()
    out_ref[...] = jnp.where(side == 0, mine[0], mine[1]) + side_in[...]
    for copy in sends:
        copy.wait_send()
    for copy in tail_copies:
        copy.wait_send()
    for copy in tail_copies:
        copy.wait_recv()
    summed = tails_in[0]
    for peer in range(1, n):
        summed = summed + tails_in[peer]
    tails_ref[...] = summed


def relay_reduce(targets, partial, tail, n, collective_id):
    _, rows, cols = partial.shape
    ring = n // 2
    upward = ring // 2
    downward = upward
    vmem = pl.BlockSpec(memory_space=pltpu.VMEM)
    return pl.pallas_call(
        functools.partial(relay_reduce_kernel, n=n),
        out_shape=[
            jax.ShapeDtypeStruct((rows, cols), jnp.float32),
            jax.ShapeDtypeStruct(tuple(tail.shape), jnp.float32),
        ],
        in_specs=[pl.BlockSpec(memory_space=pltpu.SMEM), vmem, vmem],
        out_specs=[vmem, vmem],
        scratch_shapes=[
            pltpu.VMEM((upward, 2, rows, cols), jnp.bfloat16),
            pltpu.VMEM((downward, 2, rows, cols), jnp.bfloat16),
            pltpu.VMEM((upward, 2, rows, cols), jnp.bfloat16),
            pltpu.VMEM((downward, 2, rows, cols), jnp.bfloat16),
            pltpu.VMEM((rows, cols), jnp.float32),
            pltpu.VMEM((rows, cols), jnp.float32),
            pltpu.VMEM((n,) + tuple(tail.shape), jnp.float32),
            pltpu.SemaphoreType.DMA((upward + downward + 1,)),
            pltpu.SemaphoreType.DMA((upward + downward + 1,)),
            pltpu.SemaphoreType.DMA((n - 1,)),
            pltpu.SemaphoreType.DMA((n - 1,)),
        ],
        compiler_params=pltpu.CompilerParams(
            collective_id=collective_id, has_side_effects=True,
            vmem_limit_bytes=56 * 1024 * 1024,
        ),
    )(targets, partial, tail)


def on_device(query, key, value, output, output_gradient, parent, owner):
    count = lax.axis_size("ctx")
    me = lax.axis_index("ctx")
    tile = query.shape[1]
    width = key.shape[2]
    scale_factor = HEAD_WIDTH ** (-0.5)
    prompt_tiles = count // 8
    parent_row = parent[0]
    owner_row = owner[0]
    tiles = jnp.arange(count, dtype=jnp.int32)
    my_tile = jnp.sum(jnp.where(owner_row == me, tiles, 0))
    trained = my_tile >= prompt_tiles
    above = pick_entry(parent_row, my_tile)
    second = jnp.logical_and(trained, above >= prompt_tiles)
    slot_tiles = jnp.stack(
        [jnp.int32(0), jnp.int32(1), jnp.where(second, above, 1).astype(jnp.int32)]
    )
    slot_blocks = jnp.sum(
        jnp.where(slot_tiles[:, None] == tiles[None, :], owner_row[None, :], 0), axis=1
    ).astype(jnp.int32)
    flags = jnp.stack([trained, trained, second, trained]).astype(jnp.int32)

    pair = jnp.concatenate([key[0], value[0]], axis=1)
    gathered = relay_gather(pair, 0)
    targets = jnp.concatenate([slot_blocks, me[None].astype(jnp.int32)])
    dq, dq_sum, partial, k_sum, v_sum = attention_grads(
        flags, targets, query[0], output_gradient[0], output[0], gathered, scale_factor
    )
    total_rows = lax.axis_size("dp") * query.shape[0] * count * tile
    norm = total_rows ** (-0.5)
    wide = query.shape[2]
    tail_width = 2 * width
    tail_rows = 8
    tail = jnp.concatenate(
        [dq_sum[0], k_sum[0], v_sum[0],
         jnp.zeros((tail_rows * tail_width - wide - tail_width,), jnp.float32)]
    ).reshape(tail_rows, tail_width)
    grads, summed = relay_reduce(targets, partial, tail, count, 1)
    both = exchange(summed, "dp", False, 2)
    sums = (both[0] + both[1]).reshape(-1) * norm
    sum_q = sums[:wide]
    sum_k = sums[wide:wide + width]
    sum_v = sums[wide + width:wide + 2 * width]
    return (
        dq[None],
        grads[:, :width].astype(jnp.bfloat16)[None],
        grads[:, width:].astype(jnp.bfloat16)[None],
        sum_q,
        sum_k,
        sum_v,
    )


def solution(mesh):
    return jax.shard_map(
        on_device,
        mesh=mesh,
        in_specs=(
            P("dp", "ctx", "head"),
            P("dp", "ctx", "head"),
            P("dp", "ctx", "head"),
            P("dp", "ctx", "head"),
            P("dp", "ctx", "head"),
            P("dp", None),
            P("dp", None),
        ),
        out_specs=(
            P("dp", "ctx", "head"),
            P("dp", "ctx", "head"),
            P("dp", "ctx", "head"),
            P("head"),
            P("head"),
            P("head"),
        ),
        check_vma=False,
    )
```

```python
import functools

import jax
import jax.numpy as jnp
from jax import lax
from jax.experimental import pallas as pl
from jax.experimental.pallas import tpu as pltpu
from jax.sharding import PartitionSpec as P

HEAD_WIDTH = 128

NEGATIVE_FILL = -1e30


def pick_entry(vector, index):
    spots = jnp.arange(vector.shape[0], dtype=jnp.int32)
    return jnp.sum(jnp.where(spots == index, vector, 0), axis=0)


def pick_rows(matrix, index):
    spots = jnp.arange(matrix.shape[0], dtype=jnp.int32)
    return jnp.sum(jnp.where((spots == index)[:, None], matrix, 0.0), axis=0)


def attention_grads_kernel(flags_ref, blocks_ref, q_ref, g_ref, o_ref, k0, k1, k2, k3, v0, v1, v2,
                           v3, dq_ref, dqsum_ref, kv_ref, ksum_ref, vsum_ref, s_scr, *, scale):
    head = pl.program_id(0)
    k_refs = (k0, k1, k2, k3)
    v_refs = (v0, v1, v2, v3)
    slots = len(k_refs)

    width = q_ref.shape[1]
    dk_ref = kv_ref.at[:, :, pl.ds(0, width)]
    dv_ref = kv_ref.at[:, :, pl.ds(width, width)]

    @pl.when(head == 0)
    def _():
        kv_ref[...] = jnp.zeros_like(kv_ref)

    q = q_ref[...]
    g = g_ref[...]
    o = o_ref[...]
    rows = q.shape[0]
    delta = jnp.sum(g.astype(jnp.float32) * o.astype(jnp.float32), axis=1, keepdims=True)
    causal = (lax.broadcasted_iota(jnp.int32, (rows, rows), 0)
              >= lax.broadcasted_iota(jnp.int32, (rows, rows), 1))
    nt = (((1,), (1,)), ((), ()))
    tn = (((0,), (0,)), ((), ()))

    top = jnp.full((rows, 1), NEGATIVE_FILL, jnp.float32)
    for j in range(slots):
        keep = flags_ref[slots + j] > 0
        if j == slots - 1:
            keep = jnp.logical_and(keep, causal)
        scores = lax.dot_general(q, k_refs[j][...], nt, preferred_element_type=jnp.float32) * scale
        scores = jnp.where(keep, scores, NEGATIVE_FILL)
        s_scr[j] = scores
        top = jnp.maximum(top, jnp.max(scores, axis=1, keepdims=True))

    total = jnp.zeros((rows, 1), jnp.float32)
    for j in range(slots):
        keep = flags_ref[slots + j] > 0
        if j == slots - 1:
            keep = jnp.logical_and(keep, causal)
        probs = jnp.where(keep, jnp.exp(s_scr[j] - top), 0.0)
        s_scr[j] = probs
        total = total + jnp.sum(probs, axis=1, keepdims=True)
    inverse = jnp.where(total > 0, 1.0 / jnp.where(total > 0, total, 1.0), 0.0)

    dq = jnp.zeros((rows, q.shape[1]), jnp.float32)
    for j in range(slots):
        probs = s_scr[j] * inverse
        dv_ref[j] += lax.dot_general(probs.astype(jnp.bfloat16), g, tn,
                                     preferred_element_type=jnp.float32)
        dprobs = lax.dot_general(g, v_refs[j][...], nt, preferred_element_type=jnp.float32)
        dscores = (probs * (dprobs - delta)).astype(jnp.bfloat16)
        dq = dq + jnp.dot(dscores, k_refs[j][...], preferred_element_type=jnp.float32)
        dk_ref[j] += lax.dot_general(dscores, q, tn, preferred_element_type=jnp.float32) * scale
    dq = dq * scale
    dq_ref[...] = dq.astype(dq_ref.dtype)
    dqsum_ref[...] = jnp.sum(dq, axis=0, keepdims=True)

    @pl.when(head == pl.num_programs(0) - 1)
    def _():
        ksum_ref[...] = jnp.sum(jnp.sum(dk_ref[...], axis=0), axis=0, keepdims=True)
        vsum_ref[...] = jnp.sum(jnp.sum(dv_ref[...], axis=0), axis=0, keepdims=True)


def attention_grads(flags, blocks, q, g, o, gathered, scale):
    rows, wide = q.shape
    slots = blocks.shape[0] // 2
    heads = wide // HEAD_WIDTH
    col = pl.BlockSpec((rows, HEAD_WIDTH), lambda h, f, b: (0, h))
    line = pl.BlockSpec((1, HEAD_WIDTH), lambda h, f, b: (0, h))
    fixed = pl.BlockSpec((1, HEAD_WIDTH), lambda h, f, b: (0, 0))
    pair_spec = pl.BlockSpec((slots, rows, 2 * HEAD_WIDTH), lambda h, f, b: (0, 0, 0))

    def pick(j, part):
        return pl.BlockSpec((None, rows, HEAD_WIDTH), lambda h, f, b: (b[j], 0, part))

    return pl.pallas_call(
        functools.partial(attention_grads_kernel, scale=scale),
        grid_spec=pltpu.PrefetchScalarGridSpec(
            num_scalar_prefetch=2,
            grid=(heads,),
            in_specs=[col, col, col] + [pick(j, 0) for j in range(slots)]
            + [pick(j, 1) for j in range(slots)],
            out_specs=[col, line, pair_spec, fixed, fixed],
            scratch_shapes=[pltpu.VMEM((slots, rows, rows), jnp.float32)],
        ),
        out_shape=[
            jax.ShapeDtypeStruct((rows, wide), jnp.bfloat16),
            jax.ShapeDtypeStruct((1, wide), jnp.float32),
            jax.ShapeDtypeStruct((slots, rows, 2 * HEAD_WIDTH), jnp.float32),
            jax.ShapeDtypeStruct((1, HEAD_WIDTH), jnp.float32),
            jax.ShapeDtypeStruct((1, HEAD_WIDTH), jnp.float32),
        ],
        compiler_params=pltpu.CompilerParams(
            dimension_semantics=("arbitrary",), vmem_limit_bytes=48 * 1024 * 1024
        ),
    )(flags, blocks, q, g, o, *([gathered] * (2 * slots)))


def exchange_kernel(x_ref, out_ref, send_sem, recv_sem, self_sem, *, axis, n, indexed):
    me = lax.axis_index(axis)
    barrier = pltpu.get_barrier_semaphore()
    for d in range(1, n):
        pl.semaphore_signal(
            barrier, inc=1, device_id={axis: lax.rem(me + d, n)},
            device_id_type=pl.DeviceIdType.MESH,
        )
    pl.semaphore_wait(barrier, n - 1)
    copies = []
    for d in range(1, n):
        peer = lax.rem(me + d, n)
        copy = pltpu.make_async_remote_copy(
            src_ref=x_ref.at[peer] if indexed else x_ref,
            dst_ref=out_ref.at[me],
            send_sem=send_sem.at[d - 1],
            recv_sem=recv_sem.at[d - 1],
            device_id={axis: peer},
            device_id_type=pl.DeviceIdType.MESH,
        )
        copy.start()
        copies.append(copy)
    local = pltpu.make_async_copy(x_ref.at[me] if indexed else x_ref, out_ref.at[me], self_sem)
    local.start()
    for copy in copies:
        copy.wait_send()
    for copy in copies:
        copy.wait_recv()
    local.wait()


def exchange(x, axis, indexed, collective_id):
    n = lax.axis_size(axis)
    piece = x.shape[1:] if indexed else x.shape
    return pl.pallas_call(
        functools.partial(exchange_kernel, axis=axis, n=n, indexed=indexed),
        out_shape=jax.ShapeDtypeStruct((n,) + tuple(piece), x.dtype),
        in_specs=[pl.BlockSpec(memory_space=pl.ANY)],
        out_specs=pl.BlockSpec(memory_space=pl.ANY),
        scratch_shapes=[
            pltpu.SemaphoreType.DMA((n - 1,)),
            pltpu.SemaphoreType.DMA((n - 1,)),
            pltpu.SemaphoreType.DMA,
        ],
        compiler_params=pltpu.CompilerParams(collective_id=collective_id, has_side_effects=True),
    )(x)


def relay_gather_kernel(owner_ref, parent_ref, x_ref, out_ref, info_ref, send_sem, recv_sem,
                        self_sem, *, n, prompt):
    me = lax.axis_index("ctx")
    ring = n // 2
    z = me // 2
    side = me % 2
    partner = z * 2 + (1 - side)
    up = lax.rem(z + 1, ring) * 2 + side
    down = lax.rem(z + ring - 1, ring) * 2 + side
    barrier = pltpu.get_barrier_semaphore()
    for peer in (partner, up, down):
        pl.semaphore_signal(barrier, inc=1, device_id={"ctx": peer},
                            device_id_type=pl.DeviceIdType.MESH)
    pl.semaphore_wait(barrier, 3)
    local = pltpu.make_async_copy(x_ref, out_ref.at[me], self_sem)
    local.start()
    sends = []

    def send(slot, target, src):
        copy = pltpu.make_async_remote_copy(
            src_ref=src, dst_ref=out_ref.at[slot], send_sem=send_sem.at[len(sends)],
            recv_sem=recv_sem.at[slot], device_id={"ctx": target},
            device_id_type=pl.DeviceIdType.MESH,
        )
        copy.start()
        sends.append(copy)

    def arrive(slot):
        pltpu.make_async_remote_copy(
            src_ref=x_ref, dst_ref=out_ref.at[slot], send_sem=send_sem.at[0],
            recv_sem=recv_sem.at[slot], device_id={"ctx": partner},
            device_id_type=pl.DeviceIdType.MESH,
        ).wait_recv()

    def origin(step, offset):
        return lax.rem(z + step + 2 * ring, ring) * 2 + offset

    def send_part(slot, target, rows, sem_index):
        copy = pltpu.make_async_remote_copy(
            src_ref=out_ref.at[slot, rows], dst_ref=out_ref.at[slot, rows],
            send_sem=send_sem.at[len(sends)], recv_sem=recv_sem.at[sem_index],
            device_id={"ctx": target}, device_id_type=pl.DeviceIdType.MESH,
        )
        copy.start()
        sends.append(copy)

    def arrive_part(slot, rows, sem_index):
        pltpu.make_async_remote_copy(
            src_ref=out_ref.at[slot, rows], dst_ref=out_ref.at[slot, rows],
            send_sem=send_sem.at[0], recv_sem=recv_sem.at[sem_index],
            device_id={"ctx": partner}, device_id_type=pl.DeviceIdType.MESH,
        ).wait_recv()

    upward = ring // 2
    half = x_ref.shape[0] // 2
    top = pl.ds(0, half)
    bottom = pl.ds(half, half)
    send(me, partner, x_ref)
    send(me, up, x_ref)
    send(me, down, x_ref)
    arrive(partner)
    send(partner, up, out_ref.at[partner])
    send(partner, down, out_ref.at[partner])
    my_tile = jnp.int32(0)
    for tile in range(owner_ref.shape[1]):
        my_tile = my_tile + jnp.where(owner_ref[0, tile] == me, tile, 0)
    trained = my_tile >= prompt
    last = owner_ref.shape[1] - 1
    above = parent_ref[0, jnp.clip(my_tile, 0, last)]
    second = jnp.logical_and(trained, above >= prompt)
    info_ref[0] = owner_ref[0, 0]
    info_ref[1] = owner_ref[0, 1]
    info_ref[2] = owner_ref[0, jnp.clip(jnp.where(second, above, 1), 0, last)]
    info_ref[3] = me
    info_ref[4] = trained.astype(jnp.int32)
    info_ref[5] = trained.astype(jnp.int32)
    info_ref[6] = second.astype(jnp.int32)
    info_ref[7] = trained.astype(jnp.int32)
    for step in range(2, upward + 1):
        for offset in (0, 1):
            slot = origin(-(step - 1), offset)
            arrive(slot)
            if step < upward:
                send(slot, up, out_ref.at[slot])
            else:
                send_part(slot, up, top, slot)
        for offset in (0, 1):
            slot = origin(step - 1, offset)
            arrive(slot)
            if step < upward:
                send(slot, down, out_ref.at[slot])
            else:
                send_part(slot, down, bottom, n + offset)
    for offset in (0, 1):
        arrive_part(origin(-upward, offset), top, origin(-upward, offset))
        arrive_part(origin(upward, offset), bottom, n + offset)
    for copy in sends:
        copy.wait_send()
    local.wait()


def relay_gather(owner, parent, x, prompt, collective_id):
    n = lax.axis_size("ctx")
    smem = pl.BlockSpec(memory_space=pltpu.SMEM)
    return pl.pallas_call(
        functools.partial(relay_gather_kernel, n=n, prompt=prompt),
        out_shape=[
            jax.ShapeDtypeStruct((n,) + tuple(x.shape), x.dtype),
            jax.ShapeDtypeStruct((8,), jnp.int32),
        ],
        in_specs=[smem, smem, pl.BlockSpec(memory_space=pl.ANY)],
        out_specs=[pl.BlockSpec(memory_space=pl.ANY), smem],
        scratch_shapes=[
            pltpu.SemaphoreType.DMA((n + 1,)),
            pltpu.SemaphoreType.DMA((n + 2,)),
            pltpu.SemaphoreType.DMA,
        ],
        compiler_params=pltpu.CompilerParams(collective_id=collective_id, has_side_effects=True),
    )(owner, parent, x)


def relay_reduce_kernel(t_ref, x_ref, tail_ref, out_ref, tails_ref, up_in, down_in, up_out,
                        down_out, side_out, side_in, tails_in, send_sem, recv_sem, tail_send,
                        tail_recv, *, n):
    me = lax.axis_index("ctx")
    ring = n // 2
    z = me // 2
    side = me % 2
    partner = z * 2 + (1 - side)
    up = lax.rem(z + 1, ring) * 2 + side
    down = lax.rem(z + ring - 1, ring) * 2 + side
    upward = ring // 2
    barrier = pltpu.get_barrier_semaphore()
    for d in range(1, n):
        pl.semaphore_signal(barrier, inc=1, device_id={"ctx": lax.rem(me + d, n)},
                            device_id_type=pl.DeviceIdType.MESH)
    pl.semaphore_wait(barrier, n - 1)
    tail_copies = []
    for d in range(1, n):
        copy = pltpu.make_async_remote_copy(
            src_ref=tail_ref, dst_ref=tails_in.at[me], send_sem=tail_send.at[d - 1],
            recv_sem=tail_recv.at[d - 1], device_id={"ctx": lax.rem(me + d, n)},
            device_id_type=pl.DeviceIdType.MESH,
        )
        copy.start()
        tail_copies.append(copy)
    tails_in[me] = tail_ref[...]
    sends = []

    def send(src, dst, target, sem_index):
        copy = pltpu.make_async_remote_copy(
            src_ref=src, dst_ref=dst, send_sem=send_sem.at[len(sends)],
            recv_sem=recv_sem.at[sem_index], device_id={"ctx": target},
            device_id_type=pl.DeviceIdType.MESH,
        )
        copy.start()
        sends.append(copy)
        return copy

    def own(target_z):
        base = lax.rem(target_z + 2 * ring, ring) * 2
        pieces = []
        for offset in (0, 1):
            total = jnp.zeros(x_ref.shape[1:], jnp.float32)
            for j in range(x_ref.shape[0]):
                total = total + jnp.where(t_ref[j] == base + offset, x_ref[j], 0.0)
            pieces.append(total)
        return jnp.stack(pieces)

    half = x_ref.shape[1] // 2
    top = pl.ds(0, half)
    bottom = pl.ds(half, half)
    pending_up = None
    pending_down = None
    for step in range(1, upward + 1):
        term = own(z + upward - step + 1)
        if step == 1:
            up_out[0, :, top] = term[:, :half].astype(up_out.dtype)
            pending_up = send(up_out.at[0, :, top], up_in.at[0, :, top], up, 0)
        else:
            pending_up.wait_recv()
            if step == 2:
                term = jnp.concatenate(
                    [term[:, :half] + up_in[0, :, top].astype(jnp.float32), term[:, half:]], axis=1
                )
            else:
                term = term + up_in[step - 2].astype(jnp.float32)
            up_out[step - 1] = term.astype(up_out.dtype)
            pending_up = send(up_out.at[step - 1], up_in.at[step - 1], up, step - 1)
        term = own(z - (upward - step + 1))
        if step == 1:
            down_out[0, :, bottom] = term[:, half:].astype(down_out.dtype)
            pending_down = send(down_out.at[0, :, bottom], down_in.at[0, :, bottom], down,
                                upward)
        else:
            pending_down.wait_recv()
            if step == 2:
                term = jnp.concatenate(
                    [term[:, :half], term[:, half:] + down_in[0, :, bottom].astype(jnp.float32)],
                    axis=1,
                )
            else:
                term = term + down_in[step - 2].astype(jnp.float32)
            down_out[step - 1] = term.astype(down_out.dtype)
            pending_down = send(down_out.at[step - 1], down_in.at[step - 1], down,
                                upward + step - 1)
    pending_up.wait_recv()
    pending_down.wait_recv()
    mine = (own(z) + up_in[upward - 1].astype(jnp.float32)
            + down_in[upward - 1].astype(jnp.float32))
    side_out[...] = jnp.where(side == 0, mine[1], mine[0])
    across = send(side_out, side_in, partner, 2 * upward)
    across.wait_recv()
    out_ref[...] = jnp.where(side == 0, mine[0], mine[1]) + side_in[...]
    for copy in sends:
        copy.wait_send()
    for copy in tail_copies:
        copy.wait_send()
    for copy in tail_copies:
        copy.wait_recv()
    summed = tails_in[0]
    for peer in range(1, n):
        summed = summed + tails_in[peer]
    tails_ref[...] = summed


def relay_reduce(targets, partial, tail, n, collective_id):
    _, rows, cols = partial.shape
    ring = n // 2
    upward = ring // 2
    downward = upward
    vmem = pl.BlockSpec(memory_space=pltpu.VMEM)
    return pl.pallas_call(
        functools.partial(relay_reduce_kernel, n=n),
        out_shape=[
            jax.ShapeDtypeStruct((rows, cols), jnp.float32),
            jax.ShapeDtypeStruct(tuple(tail.shape), jnp.float32),
        ],
        in_specs=[pl.BlockSpec(memory_space=pltpu.SMEM), vmem, vmem],
        out_specs=[vmem, vmem],
        scratch_shapes=[
            pltpu.VMEM((upward, 2, rows, cols), jnp.bfloat16),
            pltpu.VMEM((downward, 2, rows, cols), jnp.bfloat16),
            pltpu.VMEM((upward, 2, rows, cols), jnp.bfloat16),
            pltpu.VMEM((downward, 2, rows, cols), jnp.bfloat16),
            pltpu.VMEM((rows, cols), jnp.float32),
            pltpu.VMEM((rows, cols), jnp.float32),
            pltpu.VMEM((n,) + tuple(tail.shape), jnp.float32),
            pltpu.SemaphoreType.DMA((upward + downward + 1,)),
            pltpu.SemaphoreType.DMA((upward + downward + 1,)),
            pltpu.SemaphoreType.DMA((n - 1,)),
            pltpu.SemaphoreType.DMA((n - 1,)),
        ],
        compiler_params=pltpu.CompilerParams(
            collective_id=collective_id, has_side_effects=True,
            vmem_limit_bytes=56 * 1024 * 1024,
        ),
    )(targets, partial, tail)


def on_device(query, key, value, output, output_gradient, parent, owner):
    count = lax.axis_size("ctx")
    me = lax.axis_index("ctx")
    tile = query.shape[1]
    width = key.shape[2]
    scale_factor = HEAD_WIDTH ** (-0.5)
    prompt_tiles = count // 8
    pair = jnp.concatenate([key[0], value[0]], axis=1)
    gathered, info = relay_gather(owner, parent, pair, prompt_tiles, 0)
    dq, dq_sum, partial, k_sum, v_sum = attention_grads(
        info, info, query[0], output_gradient[0], output[0], gathered, scale_factor
    )
    total_rows = lax.axis_size("dp") * query.shape[0] * count * tile
    norm = total_rows ** (-0.5)
    wide = query.shape[2]
    tail_width = 2 * width
    tail_rows = 8
    tail = jnp.concatenate(
        [dq_sum[0], k_sum[0], v_sum[0],
         jnp.zeros((tail_rows * tail_width - wide - tail_width,), jnp.float32)]
    ).reshape(tail_rows, tail_width)
    grads, summed = relay_reduce(info, partial, tail, count, 1)
    both = exchange(summed, "dp", False, 2)
    sums = (both[0] + both[1]).reshape(-1) * norm
    sum_q = sums[:wide]
    sum_k = sums[wide:wide + width]
    sum_v = sums[wide + width:wide + 2 * width]
    return (
        dq[None],
        grads[:, :width].astype(jnp.bfloat16)[None],
        grads[:, width:].astype(jnp.bfloat16)[None],
        sum_q,
        sum_k,
        sum_v,
    )


def solution(mesh):
    return jax.shard_map(
        on_device,
        mesh=mesh,
        in_specs=(
            P("dp", "ctx", "head"),
            P("dp", "ctx", "head"),
            P("dp", "ctx", "head"),
            P("dp", "ctx", "head"),
            P("dp", "ctx", "head"),
            P("dp", None),
            P("dp", None),
        ),
        out_specs=(
            P("dp", "ctx", "head"),
            P("dp", "ctx", "head"),
            P("dp", "ctx", "head"),
            P("head"),
            P("head"),
            P("head"),
        ),
        check_vma=False,
    )
```

```python
import functools

import jax
import jax.numpy as jnp
from jax import lax
from jax.experimental import pallas as pl
from jax.experimental.pallas import tpu as pltpu
from jax.sharding import PartitionSpec as P

HEAD_WIDTH = 128

NEGATIVE_FILL = -1e30


def pick_entry(vector, index):
    spots = jnp.arange(vector.shape[0], dtype=jnp.int32)
    return jnp.sum(jnp.where(spots == index, vector, 0), axis=0)


def pick_rows(matrix, index):
    spots = jnp.arange(matrix.shape[0], dtype=jnp.int32)
    return jnp.sum(jnp.where((spots == index)[:, None], matrix, 0.0), axis=0)


def attention_grads_kernel(flags_ref, q_ref, g_ref, o_ref, k0, k1, k2, k3, v0, v1, v2,
                           v3, dq_ref, dqsum_ref, kv_ref, ksum_ref, vsum_ref, s_scr, *, scale):
    head = pl.program_id(0)
    k_refs = (k0, k1, k2, k3)
    v_refs = (v0, v1, v2, v3)
    slots = len(k_refs)

    width = q_ref.shape[1]
    dk_ref = kv_ref.at[:, :, pl.ds(0, width)]
    dv_ref = kv_ref.at[:, :, pl.ds(width, width)]

    @pl.when(head == 0)
    def _():
        kv_ref[...] = jnp.zeros_like(kv_ref)

    q = q_ref[...]
    g = g_ref[...]
    o = o_ref[...]
    rows = q.shape[0]
    delta = jnp.sum(g.astype(jnp.float32) * o.astype(jnp.float32), axis=1, keepdims=True)
    causal = (lax.broadcasted_iota(jnp.int32, (rows, rows), 0)
              >= lax.broadcasted_iota(jnp.int32, (rows, rows), 1))
    nt = (((1,), (1,)), ((), ()))
    tn = (((0,), (0,)), ((), ()))

    top = jnp.full((rows, 1), NEGATIVE_FILL, jnp.float32)
    for j in range(slots):
        keep = flags_ref[slots + j] > 0
        if j == slots - 1:
            keep = jnp.logical_and(keep, causal)
        scores = lax.dot_general(q, k_refs[j][...], nt, preferred_element_type=jnp.float32) * scale
        scores = jnp.where(keep, scores, NEGATIVE_FILL)
        s_scr[j] = scores
        top = jnp.maximum(top, jnp.max(scores, axis=1, keepdims=True))

    total = jnp.zeros((rows, 1), jnp.float32)
    for j in range(slots):
        keep = flags_ref[slots + j] > 0
        if j == slots - 1:
            keep = jnp.logical_and(keep, causal)
        probs = jnp.where(keep, jnp.exp(s_scr[j] - top), 0.0)
        s_scr[j] = probs
        total = total + jnp.sum(probs, axis=1, keepdims=True)
    inverse = jnp.where(total > 0, 1.0 / jnp.where(total > 0, total, 1.0), 0.0)

    dq = jnp.zeros((rows, q.shape[1]), jnp.float32)
    for j in range(slots):
        probs = s_scr[j] * inverse
        dv_ref[j] += lax.dot_general(probs.astype(jnp.bfloat16), g, tn,
                                     preferred_element_type=jnp.float32)
        dprobs = lax.dot_general(g, v_refs[j][...], nt, preferred_element_type=jnp.float32)
        dscores = (probs * (dprobs - delta)).astype(jnp.bfloat16)
        dq = dq + jnp.dot(dscores, k_refs[j][...], preferred_element_type=jnp.float32)
        dk_ref[j] += lax.dot_general(dscores, q, tn, preferred_element_type=jnp.float32) * scale
    dq = dq * scale
    dq_ref[...] = dq.astype(dq_ref.dtype)
    dqsum_ref[...] = jnp.sum(dq, axis=0, keepdims=True)

    @pl.when(head == pl.num_programs(0) - 1)
    def _():
        ksum_ref[...] = jnp.sum(jnp.sum(dk_ref[...], axis=0), axis=0, keepdims=True)
        vsum_ref[...] = jnp.sum(jnp.sum(dv_ref[...], axis=0), axis=0, keepdims=True)


def attention_grads(blocks, q, g, o, gathered, scale):
    rows, wide = q.shape
    slots = blocks.shape[0] // 2
    heads = wide // HEAD_WIDTH
    col = pl.BlockSpec((rows, HEAD_WIDTH), lambda h, b: (0, h))
    line = pl.BlockSpec((1, HEAD_WIDTH), lambda h, b: (0, h))
    fixed = pl.BlockSpec((1, HEAD_WIDTH), lambda h, b: (0, 0))
    pair_spec = pl.BlockSpec((slots, rows, 2 * HEAD_WIDTH), lambda h, b: (0, 0, 0))

    def pick(j, part):
        return pl.BlockSpec((None, rows, HEAD_WIDTH), lambda h, b: (b[j], 0, part))

    return pl.pallas_call(
        functools.partial(attention_grads_kernel, scale=scale),
        grid_spec=pltpu.PrefetchScalarGridSpec(
            num_scalar_prefetch=1,
            grid=(heads,),
            in_specs=[col, col, col] + [pick(j, 0) for j in range(slots)]
            + [pick(j, 1) for j in range(slots)],
            out_specs=[col, line, pair_spec, fixed, fixed],
            scratch_shapes=[pltpu.VMEM((slots, rows, rows), jnp.float32)],
        ),
        out_shape=[
            jax.ShapeDtypeStruct((rows, wide), jnp.bfloat16),
            jax.ShapeDtypeStruct((1, wide), jnp.float32),
            jax.ShapeDtypeStruct((slots, rows, 2 * HEAD_WIDTH), jnp.float32),
            jax.ShapeDtypeStruct((1, HEAD_WIDTH), jnp.float32),
            jax.ShapeDtypeStruct((1, HEAD_WIDTH), jnp.float32),
        ],
        compiler_params=pltpu.CompilerParams(
            dimension_semantics=("arbitrary",), vmem_limit_bytes=48 * 1024 * 1024
        ),
    )(blocks, q, g, o, *([gathered] * (2 * slots)))


def exchange_kernel(x_ref, out_ref, send_sem, recv_sem, self_sem, *, axis, n, indexed):
    me = lax.axis_index(axis)
    barrier = pltpu.get_barrier_semaphore()
    for d in range(1, n):
        pl.semaphore_signal(
            barrier, inc=1, device_id={axis: lax.rem(me + d, n)},
            device_id_type=pl.DeviceIdType.MESH,
        )
    pl.semaphore_wait(barrier, n - 1)
    copies = []
    for d in range(1, n):
        peer = lax.rem(me + d, n)
        copy = pltpu.make_async_remote_copy(
            src_ref=x_ref.at[peer] if indexed else x_ref,
            dst_ref=out_ref.at[me],
            send_sem=send_sem.at[d - 1],
            recv_sem=recv_sem.at[d - 1],
            device_id={axis: peer},
            device_id_type=pl.DeviceIdType.MESH,
        )
        copy.start()
        copies.append(copy)
    local = pltpu.make_async_copy(x_ref.at[me] if indexed else x_ref, out_ref.at[me], self_sem)
    local.start()
    for copy in copies:
        copy.wait_send()
    for copy in copies:
        copy.wait_recv()
    local.wait()


def exchange(x, axis, indexed, collective_id):
    n = lax.axis_size(axis)
    piece = x.shape[1:] if indexed else x.shape
    return pl.pallas_call(
        functools.partial(exchange_kernel, axis=axis, n=n, indexed=indexed),
        out_shape=jax.ShapeDtypeStruct((n,) + tuple(piece), x.dtype),
        in_specs=[pl.BlockSpec(memory_space=pl.ANY)],
        out_specs=pl.BlockSpec(memory_space=pl.ANY),
        scratch_shapes=[
            pltpu.SemaphoreType.DMA((n - 1,)),
            pltpu.SemaphoreType.DMA((n - 1,)),
            pltpu.SemaphoreType.DMA,
        ],
        compiler_params=pltpu.CompilerParams(collective_id=collective_id, has_side_effects=True),
    )(x)


def relay_gather_kernel(owner_ref, parent_ref, x_ref, out_ref, info_ref, send_sem, recv_sem,
                        self_sem, *, n, prompt):
    me = lax.axis_index("ctx")
    ring = n // 2
    z = me // 2
    side = me % 2
    partner = z * 2 + (1 - side)
    up = lax.rem(z + 1, ring) * 2 + side
    down = lax.rem(z + ring - 1, ring) * 2 + side
    barrier = pltpu.get_barrier_semaphore()
    for peer in (partner, up, down):
        pl.semaphore_signal(barrier, inc=1, device_id={"ctx": peer},
                            device_id_type=pl.DeviceIdType.MESH)
    pl.semaphore_wait(barrier, 3)
    local = pltpu.make_async_copy(x_ref, out_ref.at[me], self_sem)
    local.start()
    sends = []

    def send(slot, target, src):
        copy = pltpu.make_async_remote_copy(
            src_ref=src, dst_ref=out_ref.at[slot], send_sem=send_sem.at[len(sends)],
            recv_sem=recv_sem.at[slot], device_id={"ctx": target},
            device_id_type=pl.DeviceIdType.MESH,
        )
        copy.start()
        sends.append(copy)

    def arrive(slot):
        pltpu.make_async_remote_copy(
            src_ref=x_ref, dst_ref=out_ref.at[slot], send_sem=send_sem.at[0],
            recv_sem=recv_sem.at[slot], device_id={"ctx": partner},
            device_id_type=pl.DeviceIdType.MESH,
        ).wait_recv()

    def origin(step, offset):
        return lax.rem(z + step + 2 * ring, ring) * 2 + offset

    def send_part(slot, target, rows, sem_index):
        copy = pltpu.make_async_remote_copy(
            src_ref=out_ref.at[slot, rows], dst_ref=out_ref.at[slot, rows],
            send_sem=send_sem.at[len(sends)], recv_sem=recv_sem.at[sem_index],
            device_id={"ctx": target}, device_id_type=pl.DeviceIdType.MESH,
        )
        copy.start()
        sends.append(copy)

    def arrive_part(slot, rows, sem_index):
        pltpu.make_async_remote_copy(
            src_ref=out_ref.at[slot, rows], dst_ref=out_ref.at[slot, rows],
            send_sem=send_sem.at[0], recv_sem=recv_sem.at[sem_index],
            device_id={"ctx": partner}, device_id_type=pl.DeviceIdType.MESH,
        ).wait_recv()

    upward = ring // 2
    half = x_ref.shape[0] // 2
    top = pl.ds(0, half)
    bottom = pl.ds(half, half)
    send(me, partner, x_ref)
    send(me, up, x_ref)
    send(me, down, x_ref)
    arrive(partner)
    send(partner, up, out_ref.at[partner])
    send(partner, down, out_ref.at[partner])
    my_tile = jnp.int32(0)
    for tile in range(owner_ref.shape[1]):
        my_tile = my_tile + jnp.where(owner_ref[0, tile] == me, tile, 0)
    trained = my_tile >= prompt
    last = owner_ref.shape[1] - 1
    above = parent_ref[0, jnp.clip(my_tile, 0, last)]
    second = jnp.logical_and(trained, above >= prompt)
    info_ref[0] = owner_ref[0, 0]
    info_ref[1] = owner_ref[0, 1]
    info_ref[2] = owner_ref[0, jnp.clip(jnp.where(second, above, 1), 0, last)]
    info_ref[3] = me
    info_ref[4] = trained.astype(jnp.int32)
    info_ref[5] = trained.astype(jnp.int32)
    info_ref[6] = second.astype(jnp.int32)
    info_ref[7] = trained.astype(jnp.int32)
    for step in range(2, upward + 1):
        for offset in (0, 1):
            slot = origin(-(step - 1), offset)
            arrive(slot)
            if step < upward:
                send(slot, up, out_ref.at[slot])
            else:
                send_part(slot, up, top, slot)
        for offset in (0, 1):
            slot = origin(step - 1, offset)
            arrive(slot)
            if step < upward:
                send(slot, down, out_ref.at[slot])
            else:
                send_part(slot, down, bottom, n + offset)
    for offset in (0, 1):
        arrive_part(origin(-upward, offset), top, origin(-upward, offset))
        arrive_part(origin(upward, offset), bottom, n + offset)
    for copy in sends:
        copy.wait_send()
    local.wait()


def relay_gather(owner, parent, x, prompt, collective_id):
    n = lax.axis_size("ctx")
    smem = pl.BlockSpec(memory_space=pltpu.SMEM)
    return pl.pallas_call(
        functools.partial(relay_gather_kernel, n=n, prompt=prompt),
        out_shape=[
            jax.ShapeDtypeStruct((n,) + tuple(x.shape), x.dtype),
            jax.ShapeDtypeStruct((8,), jnp.int32),
        ],
        in_specs=[smem, smem, pl.BlockSpec(memory_space=pl.ANY)],
        out_specs=[pl.BlockSpec(memory_space=pl.ANY), smem],
        scratch_shapes=[
            pltpu.SemaphoreType.DMA((n + 1,)),
            pltpu.SemaphoreType.DMA((n + 2,)),
            pltpu.SemaphoreType.DMA,
        ],
        compiler_params=pltpu.CompilerParams(collective_id=collective_id, has_side_effects=True),
    )(owner, parent, x)


def relay_reduce_kernel(t_ref, x_ref, tail_ref, out_ref, tails_ref, up_in, down_in, up_out,
                        down_out, side_out, side_in, tails_in, send_sem, recv_sem, tail_send,
                        tail_recv, *, n):
    me = lax.axis_index("ctx")
    ring = n // 2
    z = me // 2
    side = me % 2
    partner = z * 2 + (1 - side)
    up = lax.rem(z + 1, ring) * 2 + side
    down = lax.rem(z + ring - 1, ring) * 2 + side
    upward = ring // 2
    barrier = pltpu.get_barrier_semaphore()
    for d in range(1, n):
        pl.semaphore_signal(barrier, inc=1, device_id={"ctx": lax.rem(me + d, n)},
                            device_id_type=pl.DeviceIdType.MESH)
    pl.semaphore_wait(barrier, n - 1)
    tail_copies = []
    for d in range(1, n):
        copy = pltpu.make_async_remote_copy(
            src_ref=tail_ref, dst_ref=tails_in.at[me], send_sem=tail_send.at[d - 1],
            recv_sem=tail_recv.at[d - 1], device_id={"ctx": lax.rem(me + d, n)},
            device_id_type=pl.DeviceIdType.MESH,
        )
        copy.start()
        tail_copies.append(copy)
    tails_in[me] = tail_ref[...]
    sends = []

    def send(src, dst, target, sem_index):
        copy = pltpu.make_async_remote_copy(
            src_ref=src, dst_ref=dst, send_sem=send_sem.at[len(sends)],
            recv_sem=recv_sem.at[sem_index], device_id={"ctx": target},
            device_id_type=pl.DeviceIdType.MESH,
        )
        copy.start()
        sends.append(copy)
        return copy

    def own(target_z):
        base = lax.rem(target_z + 2 * ring, ring) * 2
        pieces = []
        for offset in (0, 1):
            total = jnp.zeros(x_ref.shape[1:], jnp.float32)
            for j in range(x_ref.shape[0]):
                total = total + jnp.where(t_ref[j] == base + offset, x_ref[j], 0.0)
            pieces.append(total)
        return jnp.stack(pieces)

    half = x_ref.shape[1] // 2
    top = pl.ds(0, half)
    bottom = pl.ds(half, half)
    pending_up = None
    pending_down = None
    for step in range(1, upward + 1):
        term = own(z + upward - step + 1)
        if step == 1:
            up_out[0, :, top] = term[:, :half].astype(up_out.dtype)
            pending_up = send(up_out.at[0, :, top], up_in.at[0, :, top], up, 0)
        else:
            pending_up.wait_recv()
            if step == 2:
                term = jnp.concatenate(
                    [term[:, :half] + up_in[0, :, top].astype(jnp.float32), term[:, half:]], axis=1
                )
            else:
                term = term + up_in[step - 2].astype(jnp.float32)
            up_out[step - 1] = term.astype(up_out.dtype)
            pending_up = send(up_out.at[step - 1], up_in.at[step - 1], up, step - 1)
        term = own(z - (upward - step + 1))
        if step == 1:
            down_out[0, :, bottom] = term[:, half:].astype(down_out.dtype)
            pending_down = send(down_out.at[0, :, bottom], down_in.at[0, :, bottom], down,
                                upward)
        else:
            pending_down.wait_recv()
            if step == 2:
                term = jnp.concatenate(
                    [term[:, :half], term[:, half:] + down_in[0, :, bottom].astype(jnp.float32)],
                    axis=1,
                )
            else:
                term = term + down_in[step - 2].astype(jnp.float32)
            down_out[step - 1] = term.astype(down_out.dtype)
            pending_down = send(down_out.at[step - 1], down_in.at[step - 1], down,
                                upward + step - 1)
    pending_up.wait_recv()
    pending_down.wait_recv()
    mine = (own(z) + up_in[upward - 1].astype(jnp.float32)
            + down_in[upward - 1].astype(jnp.float32))
    side_out[...] = jnp.where(side == 0, mine[1], mine[0])
    across = send(side_out, side_in, partner, 2 * upward)
    across.wait_recv()
    out_ref[...] = jnp.where(side == 0, mine[0], mine[1]) + side_in[...]
    for copy in sends:
        copy.wait_send()
    for copy in tail_copies:
        copy.wait_send()
    for copy in tail_copies:
        copy.wait_recv()
    summed = tails_in[0]
    for peer in range(1, n):
        summed = summed + tails_in[peer]
    tails_ref[...] = summed


def relay_reduce(targets, partial, tail, n, collective_id):
    _, rows, cols = partial.shape
    ring = n // 2
    upward = ring // 2
    downward = upward
    vmem = pl.BlockSpec(memory_space=pltpu.VMEM)
    return pl.pallas_call(
        functools.partial(relay_reduce_kernel, n=n),
        out_shape=[
            jax.ShapeDtypeStruct((rows, cols), jnp.float32),
            jax.ShapeDtypeStruct(tuple(tail.shape), jnp.float32),
        ],
        in_specs=[pl.BlockSpec(memory_space=pltpu.SMEM), vmem, vmem],
        out_specs=[vmem, vmem],
        scratch_shapes=[
            pltpu.VMEM((upward, 2, rows, cols), jnp.bfloat16),
            pltpu.VMEM((downward, 2, rows, cols), jnp.bfloat16),
            pltpu.VMEM((upward, 2, rows, cols), jnp.bfloat16),
            pltpu.VMEM((downward, 2, rows, cols), jnp.bfloat16),
            pltpu.VMEM((rows, cols), jnp.float32),
            pltpu.VMEM((rows, cols), jnp.float32),
            pltpu.VMEM((n,) + tuple(tail.shape), jnp.float32),
            pltpu.SemaphoreType.DMA((upward + downward + 1,)),
            pltpu.SemaphoreType.DMA((upward + downward + 1,)),
            pltpu.SemaphoreType.DMA((n - 1,)),
            pltpu.SemaphoreType.DMA((n - 1,)),
        ],
        compiler_params=pltpu.CompilerParams(
            collective_id=collective_id, has_side_effects=True,
            vmem_limit_bytes=56 * 1024 * 1024,
        ),
    )(targets, partial, tail)


def on_device(query, key, value, output, output_gradient, parent, owner):
    count = lax.axis_size("ctx")
    me = lax.axis_index("ctx")
    tile = query.shape[1]
    width = key.shape[2]
    scale_factor = HEAD_WIDTH ** (-0.5)
    prompt_tiles = count // 8
    pair = jnp.concatenate([key[0], value[0]], axis=1)
    gathered, info = relay_gather(owner, parent, pair, prompt_tiles, 0)
    dq, dq_sum, partial, k_sum, v_sum = attention_grads(
        info, query[0], output_gradient[0], output[0], gathered, scale_factor
    )
    total_rows = lax.axis_size("dp") * query.shape[0] * count * tile
    norm = total_rows ** (-0.5)
    wide = query.shape[2]
    tail_width = 2 * width
    tail_rows = 8
    tail = jnp.concatenate(
        [dq_sum[0], k_sum[0], v_sum[0],
         jnp.zeros((tail_rows * tail_width - wide - tail_width,), jnp.float32)]
    ).reshape(tail_rows, tail_width)
    grads, summed = relay_reduce(info, partial, tail, count, 1)
    both = exchange(summed, "dp", False, 2)
    sums = (both[0] + both[1]).reshape(-1) * norm
    sum_q = sums[:wide]
    sum_k = sums[wide:wide + width]
    sum_v = sums[wide + width:wide + 2 * width]
    return (
        dq[None],
        grads[:, :width].astype(jnp.bfloat16)[None],
        grads[:, width:].astype(jnp.bfloat16)[None],
        sum_q,
        sum_k,
        sum_v,
    )


def solution(mesh):
    return jax.shard_map(
        on_device,
        mesh=mesh,
        in_specs=(
            P("dp", "ctx", "head"),
            P("dp", "ctx", "head"),
            P("dp", "ctx", "head"),
            P("dp", "ctx", "head"),
            P("dp", "ctx", "head"),
            P("dp", None),
            P("dp", None),
        ),
        out_specs=(
            P("dp", "ctx", "head"),
            P("dp", "ctx", "head"),
            P("dp", "ctx", "head"),
            P("head"),
            P("head"),
            P("head"),
        ),
        check_vma=False,
    )
```

```python
import functools

import jax
import jax.numpy as jnp
from jax import lax
from jax.experimental import pallas as pl
from jax.experimental.pallas import tpu as pltpu
from jax.sharding import PartitionSpec as P

HEAD_WIDTH = 128

NEGATIVE_FILL = -1e30


def pick_entry(vector, index):
    spots = jnp.arange(vector.shape[0], dtype=jnp.int32)
    return jnp.sum(jnp.where(spots == index, vector, 0), axis=0)


def pick_rows(matrix, index):
    spots = jnp.arange(matrix.shape[0], dtype=jnp.int32)
    return jnp.sum(jnp.where((spots == index)[:, None], matrix, 0.0), axis=0)


def attention_grads_kernel(flags_ref, q_ref, g_ref, o_ref, k0, k1, k2, k3, v0, v1, v2,
                           v3, dq_ref, dqsum_ref, kv_ref, ksum_ref, vsum_ref, s_scr, *, scale):
    head = pl.program_id(0)
    k_refs = (k0, k1, k2, k3)
    v_refs = (v0, v1, v2, v3)
    slots = len(k_refs)

    width = q_ref.shape[1]
    dk_ref = kv_ref.at[:, :, pl.ds(0, width)]
    dv_ref = kv_ref.at[:, :, pl.ds(width, width)]

    @pl.when(head == 0)
    def _():
        kv_ref[...] = jnp.zeros_like(kv_ref)

    q = q_ref[...]
    g = g_ref[...]
    o = o_ref[...]
    rows = q.shape[0]
    delta = jnp.sum(g.astype(jnp.float32) * o.astype(jnp.float32), axis=1, keepdims=True)
    causal = (lax.broadcasted_iota(jnp.int32, (rows, rows), 0)
              >= lax.broadcasted_iota(jnp.int32, (rows, rows), 1))
    nt = (((1,), (1,)), ((), ()))
    tn = (((0,), (0,)), ((), ()))

    top = jnp.full((rows, 1), NEGATIVE_FILL, jnp.float32)
    for j in range(slots):
        keep = flags_ref[slots + j] > 0
        if j == slots - 1:
            keep = jnp.logical_and(keep, causal)
        scores = lax.dot_general(q, k_refs[j][...], nt, preferred_element_type=jnp.float32) * scale
        scores = jnp.where(keep, scores, NEGATIVE_FILL)
        s_scr[j] = scores
        top = jnp.maximum(top, jnp.max(scores, axis=1, keepdims=True))

    total = jnp.zeros((rows, 1), jnp.float32)
    for j in range(slots):
        keep = flags_ref[slots + j] > 0
        if j == slots - 1:
            keep = jnp.logical_and(keep, causal)
        probs = jnp.where(keep, jnp.exp(s_scr[j] - top), 0.0)
        s_scr[j] = probs
        total = total + jnp.sum(probs, axis=1, keepdims=True)
    inverse = jnp.where(total > 0, 1.0 / jnp.where(total > 0, total, 1.0), 0.0)

    dq = jnp.zeros((rows, q.shape[1]), jnp.float32)
    for j in range(slots):
        probs = s_scr[j] * inverse
        dv_ref[j] += lax.dot_general(probs.astype(jnp.bfloat16), g, tn,
                                     preferred_element_type=jnp.float32)
        dprobs = lax.dot_general(g, v_refs[j][...], nt, preferred_element_type=jnp.float32)
        dscores = (probs * (dprobs - delta)).astype(jnp.bfloat16)
        dq = dq + jnp.dot(dscores, k_refs[j][...], preferred_element_type=jnp.float32)
        dk_ref[j] += lax.dot_general(dscores, q, tn, preferred_element_type=jnp.float32) * scale
    dq = dq * scale
    dq_ref[...] = dq.astype(dq_ref.dtype)
    dqsum_ref[...] = jnp.sum(dq, axis=0, keepdims=True)

    @pl.when(head == pl.num_programs(0) - 1)
    def _():
        ksum_ref[...] = jnp.sum(jnp.sum(dk_ref[...], axis=0), axis=0, keepdims=True)
        vsum_ref[...] = jnp.sum(jnp.sum(dv_ref[...], axis=0), axis=0, keepdims=True)


def attention_grads(blocks, q, g, o, gathered, scale):
    rows, wide = q.shape
    slots = blocks.shape[0] // 2
    heads = wide // HEAD_WIDTH
    col = pl.BlockSpec((rows, HEAD_WIDTH), lambda h, b: (0, h))
    line = pl.BlockSpec((1, HEAD_WIDTH), lambda h, b: (0, h))
    fixed = pl.BlockSpec((1, HEAD_WIDTH), lambda h, b: (0, 0))
    pair_spec = pl.BlockSpec((slots, rows, 2 * HEAD_WIDTH), lambda h, b: (0, 0, 0))

    def pick(j, part):
        return pl.BlockSpec((None, rows, HEAD_WIDTH), lambda h, b: (b[j], 0, part))

    return pl.pallas_call(
        functools.partial(attention_grads_kernel, scale=scale),
        grid_spec=pltpu.PrefetchScalarGridSpec(
            num_scalar_prefetch=1,
            grid=(heads,),
            in_specs=[col, col, col] + [pick(j, 0) for j in range(slots)]
            + [pick(j, 1) for j in range(slots)],
            out_specs=[col, line, pair_spec, fixed, fixed],
            scratch_shapes=[pltpu.VMEM((slots, rows, rows), jnp.float32)],
        ),
        out_shape=[
            jax.ShapeDtypeStruct((rows, wide), jnp.bfloat16),
            jax.ShapeDtypeStruct((1, wide), jnp.float32),
            jax.ShapeDtypeStruct((slots, rows, 2 * HEAD_WIDTH), jnp.float32),
            jax.ShapeDtypeStruct((1, HEAD_WIDTH), jnp.float32),
            jax.ShapeDtypeStruct((1, HEAD_WIDTH), jnp.float32),
        ],
        compiler_params=pltpu.CompilerParams(
            dimension_semantics=("arbitrary",), vmem_limit_bytes=63 * 1024 * 1024
        ),
    )(blocks, q, g, o, *([gathered] * (2 * slots)))


def exchange_kernel(x_ref, out_ref, send_sem, recv_sem, self_sem, *, axis, n, indexed):
    me = lax.axis_index(axis)
    barrier = pltpu.get_barrier_semaphore()
    for d in range(1, n):
        pl.semaphore_signal(
            barrier, inc=1, device_id={axis: lax.rem(me + d, n)},
            device_id_type=pl.DeviceIdType.MESH,
        )
    pl.semaphore_wait(barrier, n - 1)
    copies = []
    for d in range(1, n):
        peer = lax.rem(me + d, n)
        copy = pltpu.make_async_remote_copy(
            src_ref=x_ref.at[peer] if indexed else x_ref,
            dst_ref=out_ref.at[me],
            send_sem=send_sem.at[d - 1],
            recv_sem=recv_sem.at[d - 1],
            device_id={axis: peer},
            device_id_type=pl.DeviceIdType.MESH,
        )
        copy.start()
        copies.append(copy)
    local = pltpu.make_async_copy(x_ref.at[me] if indexed else x_ref, out_ref.at[me], self_sem)
    local.start()
    for copy in copies:
        copy.wait_send()
    for copy in copies:
        copy.wait_recv()
    local.wait()


def exchange(x, axis, indexed, collective_id):
    n = lax.axis_size(axis)
    piece = x.shape[1:] if indexed else x.shape
    return pl.pallas_call(
        functools.partial(exchange_kernel, axis=axis, n=n, indexed=indexed),
        out_shape=jax.ShapeDtypeStruct((n,) + tuple(piece), x.dtype),
        in_specs=[pl.BlockSpec(memory_space=pl.ANY)],
        out_specs=pl.BlockSpec(memory_space=pl.ANY),
        scratch_shapes=[
            pltpu.SemaphoreType.DMA((n - 1,)),
            pltpu.SemaphoreType.DMA((n - 1,)),
            pltpu.SemaphoreType.DMA,
        ],
        compiler_params=pltpu.CompilerParams(collective_id=collective_id, has_side_effects=True),
    )(x)


def relay_gather_kernel(owner_ref, parent_ref, x_ref, out_ref, info_ref, send_sem, recv_sem,
                        self_sem, *, n, prompt):
    me = lax.axis_index("ctx")
    ring = n // 2
    z = me // 2
    side = me % 2
    partner = z * 2 + (1 - side)
    up = lax.rem(z + 1, ring) * 2 + side
    down = lax.rem(z + ring - 1, ring) * 2 + side
    barrier = pltpu.get_barrier_semaphore()
    for peer in (partner, up, down):
        pl.semaphore_signal(barrier, inc=1, device_id={"ctx": peer},
                            device_id_type=pl.DeviceIdType.MESH)
    pl.semaphore_wait(barrier, 3)
    local = pltpu.make_async_copy(x_ref, out_ref.at[me], self_sem)
    local.start()
    sends = []

    def send(slot, target, src):
        copy = pltpu.make_async_remote_copy(
            src_ref=src, dst_ref=out_ref.at[slot], send_sem=send_sem.at[len(sends)],
            recv_sem=recv_sem.at[slot], device_id={"ctx": target},
            device_id_type=pl.DeviceIdType.MESH,
        )
        copy.start()
        sends.append(copy)

    def arrive(slot):
        pltpu.make_async_remote_copy(
            src_ref=x_ref, dst_ref=out_ref.at[slot], send_sem=send_sem.at[0],
            recv_sem=recv_sem.at[slot], device_id={"ctx": partner},
            device_id_type=pl.DeviceIdType.MESH,
        ).wait_recv()

    def origin(step, offset):
        return lax.rem(z + step + 2 * ring, ring) * 2 + offset

    def send_part(slot, target, rows, sem_index):
        copy = pltpu.make_async_remote_copy(
            src_ref=out_ref.at[slot, rows], dst_ref=out_ref.at[slot, rows],
            send_sem=send_sem.at[len(sends)], recv_sem=recv_sem.at[sem_index],
            device_id={"ctx": target}, device_id_type=pl.DeviceIdType.MESH,
        )
        copy.start()
        sends.append(copy)

    def arrive_part(slot, rows, sem_index):
        pltpu.make_async_remote_copy(
            src_ref=out_ref.at[slot, rows], dst_ref=out_ref.at[slot, rows],
            send_sem=send_sem.at[0], recv_sem=recv_sem.at[sem_index],
            device_id={"ctx": partner}, device_id_type=pl.DeviceIdType.MESH,
        ).wait_recv()

    upward = ring // 2
    half = x_ref.shape[0] // 2
    top = pl.ds(0, half)
    bottom = pl.ds(half, half)
    send(me, partner, x_ref)
    send(me, up, x_ref)
    send(me, down, x_ref)
    arrive(partner)
    send(partner, up, out_ref.at[partner])
    send(partner, down, out_ref.at[partner])
    my_tile = jnp.int32(0)
    for tile in range(owner_ref.shape[1]):
        my_tile = my_tile + jnp.where(owner_ref[0, tile] == me, tile, 0)
    trained = my_tile >= prompt
    last = owner_ref.shape[1] - 1
    above = parent_ref[0, jnp.clip(my_tile, 0, last)]
    second = jnp.logical_and(trained, above >= prompt)
    info_ref[0] = owner_ref[0, 0]
    info_ref[1] = owner_ref[0, 1]
    info_ref[2] = owner_ref[0, jnp.clip(jnp.where(second, above, 1), 0, last)]
    info_ref[3] = me
    info_ref[4] = trained.astype(jnp.int32)
    info_ref[5] = trained.astype(jnp.int32)
    info_ref[6] = second.astype(jnp.int32)
    info_ref[7] = trained.astype(jnp.int32)
    for step in range(2, upward + 1):
        for offset in (0, 1):
            slot = origin(-(step - 1), offset)
            arrive(slot)
            if step < upward:
                send(slot, up, out_ref.at[slot])
            else:
                send_part(slot, up, top, slot)
        for offset in (0, 1):
            slot = origin(step - 1, offset)
            arrive(slot)
            if step < upward:
                send(slot, down, out_ref.at[slot])
            else:
                send_part(slot, down, bottom, n + offset)
    for offset in (0, 1):
        arrive_part(origin(-upward, offset), top, origin(-upward, offset))
        arrive_part(origin(upward, offset), bottom, n + offset)
    for copy in sends:
        copy.wait_send()
    local.wait()


def relay_gather(owner, parent, x, prompt, collective_id):
    n = lax.axis_size("ctx")
    smem = pl.BlockSpec(memory_space=pltpu.SMEM)
    return pl.pallas_call(
        functools.partial(relay_gather_kernel, n=n, prompt=prompt),
        out_shape=[
            jax.ShapeDtypeStruct((n,) + tuple(x.shape), x.dtype),
            jax.ShapeDtypeStruct((8,), jnp.int32),
        ],
        in_specs=[smem, smem, pl.BlockSpec(memory_space=pl.ANY)],
        out_specs=[pl.BlockSpec(memory_space=pl.ANY), smem],
        scratch_shapes=[
            pltpu.SemaphoreType.DMA((n + 1,)),
            pltpu.SemaphoreType.DMA((n + 2,)),
            pltpu.SemaphoreType.DMA,
        ],
        compiler_params=pltpu.CompilerParams(collective_id=collective_id, has_side_effects=True),
    )(owner, parent, x)


def relay_reduce_kernel(t_ref, x_ref, tail_ref, out_ref, tails_ref, up_in, down_in, up_out,
                        down_out, side_out, side_in, tails_in, send_sem, recv_sem, tail_send,
                        tail_recv, *, n):
    me = lax.axis_index("ctx")
    ring = n // 2
    z = me // 2
    side = me % 2
    partner = z * 2 + (1 - side)
    up = lax.rem(z + 1, ring) * 2 + side
    down = lax.rem(z + ring - 1, ring) * 2 + side
    upward = ring // 2
    barrier = pltpu.get_barrier_semaphore()
    for d in range(1, n):
        pl.semaphore_signal(barrier, inc=1, device_id={"ctx": lax.rem(me + d, n)},
                            device_id_type=pl.DeviceIdType.MESH)
    pl.semaphore_wait(barrier, n - 1)
    tail_copies = []
    for d in range(1, n):
        copy = pltpu.make_async_remote_copy(
            src_ref=tail_ref, dst_ref=tails_in.at[me], send_sem=tail_send.at[d - 1],
            recv_sem=tail_recv.at[d - 1], device_id={"ctx": lax.rem(me + d, n)},
            device_id_type=pl.DeviceIdType.MESH,
        )
        copy.start()
        tail_copies.append(copy)
    tails_in[me] = tail_ref[...]
    sends = []

    def send(src, dst, target, sem_index):
        copy = pltpu.make_async_remote_copy(
            src_ref=src, dst_ref=dst, send_sem=send_sem.at[len(sends)],
            recv_sem=recv_sem.at[sem_index], device_id={"ctx": target},
            device_id_type=pl.DeviceIdType.MESH,
        )
        copy.start()
        sends.append(copy)
        return copy

    def own(target_z):
        base = lax.rem(target_z + 2 * ring, ring) * 2
        pieces = []
        for offset in (0, 1):
            total = jnp.zeros(x_ref.shape[1:], jnp.float32)
            for j in range(x_ref.shape[0]):
                total = total + jnp.where(t_ref[j] == base + offset, x_ref[j], 0.0)
            pieces.append(total)
        return jnp.stack(pieces)

    half = x_ref.shape[1] // 2
    top = pl.ds(0, half)
    bottom = pl.ds(half, half)
    pending_up = None
    pending_down = None
    for step in range(1, upward + 1):
        term = own(z + upward - step + 1)
        if step == 1:
            up_out[0, :, top] = term[:, :half].astype(up_out.dtype)
            pending_up = send(up_out.at[0, :, top], up_in.at[0, :, top], up, 0)
        else:
            pending_up.wait_recv()
            if step == 2:
                term = jnp.concatenate(
                    [term[:, :half] + up_in[0, :, top].astype(jnp.float32), term[:, half:]], axis=1
                )
            else:
                term = term + up_in[step - 2].astype(jnp.float32)
            up_out[step - 1] = term.astype(up_out.dtype)
            pending_up = send(up_out.at[step - 1], up_in.at[step - 1], up, step - 1)
        term = own(z - (upward - step + 1))
        if step == 1:
            down_out[0, :, bottom] = term[:, half:].astype(down_out.dtype)
            pending_down = send(down_out.at[0, :, bottom], down_in.at[0, :, bottom], down,
                                upward)
        else:
            pending_down.wait_recv()
            if step == 2:
                term = jnp.concatenate(
                    [term[:, :half], term[:, half:] + down_in[0, :, bottom].astype(jnp.float32)],
                    axis=1,
                )
            else:
                term = term + down_in[step - 2].astype(jnp.float32)
            down_out[step - 1] = term.astype(down_out.dtype)
            pending_down = send(down_out.at[step - 1], down_in.at[step - 1], down,
                                upward + step - 1)
    pending_up.wait_recv()
    pending_down.wait_recv()
    mine = (own(z) + up_in[upward - 1].astype(jnp.float32)
            + down_in[upward - 1].astype(jnp.float32))
    side_out[...] = jnp.where(side == 0, mine[1], mine[0])
    across = send(side_out, side_in, partner, 2 * upward)
    across.wait_recv()
    out_ref[...] = jnp.where(side == 0, mine[0], mine[1]) + side_in[...]
    for copy in sends:
        copy.wait_send()
    for copy in tail_copies:
        copy.wait_send()
    for copy in tail_copies:
        copy.wait_recv()
    summed = tails_in[0]
    for peer in range(1, n):
        summed = summed + tails_in[peer]
    tails_ref[...] = summed


def relay_reduce(targets, partial, tail, n, collective_id):
    _, rows, cols = partial.shape
    ring = n // 2
    upward = ring // 2
    downward = upward
    vmem = pl.BlockSpec(memory_space=pltpu.VMEM)
    return pl.pallas_call(
        functools.partial(relay_reduce_kernel, n=n),
        out_shape=[
            jax.ShapeDtypeStruct((rows, cols), jnp.float32),
            jax.ShapeDtypeStruct(tuple(tail.shape), jnp.float32),
        ],
        in_specs=[pl.BlockSpec(memory_space=pltpu.SMEM), vmem, vmem],
        out_specs=[vmem, vmem],
        scratch_shapes=[
            pltpu.VMEM((upward, 2, rows, cols), jnp.bfloat16),
            pltpu.VMEM((downward, 2, rows, cols), jnp.bfloat16),
            pltpu.VMEM((upward, 2, rows, cols), jnp.bfloat16),
            pltpu.VMEM((downward, 2, rows, cols), jnp.bfloat16),
            pltpu.VMEM((rows, cols), jnp.float32),
            pltpu.VMEM((rows, cols), jnp.float32),
            pltpu.VMEM((n,) + tuple(tail.shape), jnp.float32),
            pltpu.SemaphoreType.DMA((upward + downward + 1,)),
            pltpu.SemaphoreType.DMA((upward + downward + 1,)),
            pltpu.SemaphoreType.DMA((n - 1,)),
            pltpu.SemaphoreType.DMA((n - 1,)),
        ],
        compiler_params=pltpu.CompilerParams(
            collective_id=collective_id, has_side_effects=True,
            vmem_limit_bytes=56 * 1024 * 1024,
        ),
    )(targets, partial, tail)


def on_device(query, key, value, output, output_gradient, parent, owner):
    count = lax.axis_size("ctx")
    me = lax.axis_index("ctx")
    tile = query.shape[1]
    width = key.shape[2]
    scale_factor = HEAD_WIDTH ** (-0.5)
    prompt_tiles = count // 8
    pair = jnp.concatenate([key[0], value[0]], axis=1)
    gathered, info = relay_gather(owner, parent, pair, prompt_tiles, 0)
    dq, dq_sum, partial, k_sum, v_sum = attention_grads(
        info, query[0], output_gradient[0], output[0], gathered, scale_factor
    )
    total_rows = lax.axis_size("dp") * query.shape[0] * count * tile
    norm = total_rows ** (-0.5)
    wide = query.shape[2]
    tail_width = 2 * width
    tail_rows = 8
    tail = jnp.concatenate(
        [dq_sum[0], k_sum[0], v_sum[0],
         jnp.zeros((tail_rows * tail_width - wide - tail_width,), jnp.float32)]
    ).reshape(tail_rows, tail_width)
    grads, summed = relay_reduce(info, partial, tail, count, 1)
    both = exchange(summed, "dp", False, 2)
    sums = (both[0] + both[1]).reshape(-1) * norm
    sum_q = sums[:wide]
    sum_k = sums[wide:wide + width]
    sum_v = sums[wide + width:wide + 2 * width]
    return (
        dq[None],
        grads[:, :width].astype(jnp.bfloat16)[None],
        grads[:, width:].astype(jnp.bfloat16)[None],
        sum_q,
        sum_k,
        sum_v,
    )


def solution(mesh):
    return jax.shard_map(
        on_device,
        mesh=mesh,
        in_specs=(
            P("dp", "ctx", "head"),
            P("dp", "ctx", "head"),
            P("dp", "ctx", "head"),
            P("dp", "ctx", "head"),
            P("dp", "ctx", "head"),
            P("dp", None),
            P("dp", None),
        ),
        out_specs=(
            P("dp", "ctx", "head"),
            P("dp", "ctx", "head"),
            P("dp", "ctx", "head"),
            P("head"),
            P("head"),
            P("head"),
        ),
        check_vma=False,
    )
```

```python
import functools

import jax
import jax.numpy as jnp
from jax import lax
from jax.experimental import pallas as pl
from jax.experimental.pallas import tpu as pltpu
from jax.sharding import PartitionSpec as P

HEAD_WIDTH = 128

NEGATIVE_FILL = -1e30


def pick_entry(vector, index):
    spots = jnp.arange(vector.shape[0], dtype=jnp.int32)
    return jnp.sum(jnp.where(spots == index, vector, 0), axis=0)


def pick_rows(matrix, index):
    spots = jnp.arange(matrix.shape[0], dtype=jnp.int32)
    return jnp.sum(jnp.where((spots == index)[:, None], matrix, 0.0), axis=0)


def attention_grads_kernel(flags_ref, q_ref, g_ref, o_ref, k0, k1, k2, k3, v0, v1, v2,
                           v3, dq_ref, kv_ref, tail_ref, s_scr, *, scale):
    head = pl.program_id(0)
    k_refs = (k0, k1, k2, k3)
    v_refs = (v0, v1, v2, v3)
    slots = len(k_refs)

    width = q_ref.shape[1]
    dk_ref = kv_ref.at[:, :, pl.ds(0, width)]
    dv_ref = kv_ref.at[:, :, pl.ds(width, width)]

    @pl.when(head == 0)
    def _():
        kv_ref[...] = jnp.zeros_like(kv_ref)
        tail_ref[...] = jnp.zeros_like(tail_ref)

    q = q_ref[...]
    g = g_ref[...]
    o = o_ref[...]
    rows = q.shape[0]
    delta = jnp.sum(g.astype(jnp.float32) * o.astype(jnp.float32), axis=1, keepdims=True)
    causal = (lax.broadcasted_iota(jnp.int32, (rows, rows), 0)
              >= lax.broadcasted_iota(jnp.int32, (rows, rows), 1))
    nt = (((1,), (1,)), ((), ()))
    tn = (((0,), (0,)), ((), ()))

    top = jnp.full((rows, 1), NEGATIVE_FILL, jnp.float32)
    for j in range(slots):
        keep = flags_ref[slots + j] > 0
        if j == slots - 1:
            keep = jnp.logical_and(keep, causal)
        scores = lax.dot_general(q, k_refs[j][...], nt, preferred_element_type=jnp.float32) * scale
        scores = jnp.where(keep, scores, NEGATIVE_FILL)
        s_scr[j] = scores
        top = jnp.maximum(top, jnp.max(scores, axis=1, keepdims=True))

    total = jnp.zeros((rows, 1), jnp.float32)
    for j in range(slots):
        keep = flags_ref[slots + j] > 0
        if j == slots - 1:
            keep = jnp.logical_and(keep, causal)
        probs = jnp.where(keep, jnp.exp(s_scr[j] - top), 0.0)
        s_scr[j] = probs
        total = total + jnp.sum(probs, axis=1, keepdims=True)
    inverse = jnp.where(total > 0, 1.0 / jnp.where(total > 0, total, 1.0), 0.0)

    dq = jnp.zeros((rows, q.shape[1]), jnp.float32)
    for j in range(slots):
        probs = s_scr[j] * inverse
        dv_ref[j] += lax.dot_general(probs.astype(jnp.bfloat16), g, tn,
                                     preferred_element_type=jnp.float32)
        dprobs = lax.dot_general(g, v_refs[j][...], nt, preferred_element_type=jnp.float32)
        dscores = (probs * (dprobs - delta)).astype(jnp.bfloat16)
        dq = dq + jnp.dot(dscores, k_refs[j][...], preferred_element_type=jnp.float32)
        dk_ref[j] += lax.dot_general(dscores, q, tn, preferred_element_type=jnp.float32) * scale
    dq = dq * scale
    dq_ref[...] = dq.astype(dq_ref.dtype)
    tail_ref[pl.ds(head, 1), :] = jnp.sum(dq, axis=0, keepdims=True)

    @pl.when(head == pl.num_programs(0) - 1)
    def _():
        heads = pl.num_programs(0)
        tail_ref[pl.ds(heads, 1), :] = jnp.sum(jnp.sum(dk_ref[...], axis=0), axis=0, keepdims=True)
        tail_ref[pl.ds(heads + 1, 1), :] = jnp.sum(
            jnp.sum(dv_ref[...], axis=0), axis=0, keepdims=True
        )


def attention_grads(blocks, q, g, o, gathered, scale):
    rows, wide = q.shape
    slots = blocks.shape[0] // 2
    heads = wide // HEAD_WIDTH
    col = pl.BlockSpec((rows, HEAD_WIDTH), lambda h, b: (0, h))
    tail_spec = pl.BlockSpec((8, HEAD_WIDTH), lambda h, b: (0, 0))
    pair_spec = pl.BlockSpec((slots, rows, 2 * HEAD_WIDTH), lambda h, b: (0, 0, 0))

    def pick(j, part):
        return pl.BlockSpec((None, rows, HEAD_WIDTH), lambda h, b: (b[j], 0, part))

    return pl.pallas_call(
        functools.partial(attention_grads_kernel, scale=scale),
        grid_spec=pltpu.PrefetchScalarGridSpec(
            num_scalar_prefetch=1,
            grid=(heads,),
            in_specs=[col, col, col] + [pick(j, 0) for j in range(slots)]
            + [pick(j, 1) for j in range(slots)],
            out_specs=[col, pair_spec, tail_spec],
            scratch_shapes=[pltpu.VMEM((slots, rows, rows), jnp.float32)],
        ),
        out_shape=[
            jax.ShapeDtypeStruct((rows, wide), jnp.bfloat16),
            jax.ShapeDtypeStruct((slots, rows, 2 * HEAD_WIDTH), jnp.float32),
            jax.ShapeDtypeStruct((8, HEAD_WIDTH), jnp.float32),
        ],
        compiler_params=pltpu.CompilerParams(
            dimension_semantics=("arbitrary",), vmem_limit_bytes=63 * 1024 * 1024
        ),
    )(blocks, q, g, o, *([gathered] * (2 * slots)))


def exchange_kernel(x_ref, out_ref, send_sem, recv_sem, self_sem, *, axis, n, indexed):
    me = lax.axis_index(axis)
    barrier = pltpu.get_barrier_semaphore()
    for d in range(1, n):
        pl.semaphore_signal(
            barrier, inc=1, device_id={axis: lax.rem(me + d, n)},
            device_id_type=pl.DeviceIdType.MESH,
        )
    pl.semaphore_wait(barrier, n - 1)
    copies = []
    for d in range(1, n):
        peer = lax.rem(me + d, n)
        copy = pltpu.make_async_remote_copy(
            src_ref=x_ref.at[peer] if indexed else x_ref,
            dst_ref=out_ref.at[me],
            send_sem=send_sem.at[d - 1],
            recv_sem=recv_sem.at[d - 1],
            device_id={axis: peer},
            device_id_type=pl.DeviceIdType.MESH,
        )
        copy.start()
        copies.append(copy)
    local = pltpu.make_async_copy(x_ref.at[me] if indexed else x_ref, out_ref.at[me], self_sem)
    local.start()
    for copy in copies:
        copy.wait_send()
    for copy in copies:
        copy.wait_recv()
    local.wait()


def exchange(x, axis, indexed, collective_id):
    n = lax.axis_size(axis)
    piece = x.shape[1:] if indexed else x.shape
    return pl.pallas_call(
        functools.partial(exchange_kernel, axis=axis, n=n, indexed=indexed),
        out_shape=jax.ShapeDtypeStruct((n,) + tuple(piece), x.dtype),
        in_specs=[pl.BlockSpec(memory_space=pl.ANY)],
        out_specs=pl.BlockSpec(memory_space=pl.ANY),
        scratch_shapes=[
            pltpu.SemaphoreType.DMA((n - 1,)),
            pltpu.SemaphoreType.DMA((n - 1,)),
            pltpu.SemaphoreType.DMA,
        ],
        compiler_params=pltpu.CompilerParams(collective_id=collective_id, has_side_effects=True),
    )(x)


def relay_gather_kernel(owner_ref, parent_ref, x_ref, out_ref, info_ref, send_sem, recv_sem,
                        self_sem, *, n, prompt):
    me = lax.axis_index("ctx")
    ring = n // 2
    z = me // 2
    side = me % 2
    partner = z * 2 + (1 - side)
    up = lax.rem(z + 1, ring) * 2 + side
    down = lax.rem(z + ring - 1, ring) * 2 + side
    barrier = pltpu.get_barrier_semaphore()
    for peer in (partner, up, down):
        pl.semaphore_signal(barrier, inc=1, device_id={"ctx": peer},
                            device_id_type=pl.DeviceIdType.MESH)
    pl.semaphore_wait(barrier, 3)
    local = pltpu.make_async_copy(x_ref, out_ref.at[me], self_sem)
    local.start()
    sends = []

    def send(slot, target, src):
        copy = pltpu.make_async_remote_copy(
            src_ref=src, dst_ref=out_ref.at[slot], send_sem=send_sem.at[len(sends)],
            recv_sem=recv_sem.at[slot], device_id={"ctx": target},
            device_id_type=pl.DeviceIdType.MESH,
        )
        copy.start()
        sends.append(copy)

    def arrive(slot):
        pltpu.make_async_remote_copy(
            src_ref=x_ref, dst_ref=out_ref.at[slot], send_sem=send_sem.at[0],
            recv_sem=recv_sem.at[slot], device_id={"ctx": partner},
            device_id_type=pl.DeviceIdType.MESH,
        ).wait_recv()

    def origin(step, offset):
        return lax.rem(z + step + 2 * ring, ring) * 2 + offset

    def send_part(slot, target, rows, sem_index):
        copy = pltpu.make_async_remote_copy(
            src_ref=out_ref.at[slot, rows], dst_ref=out_ref.at[slot, rows],
            send_sem=send_sem.at[len(sends)], recv_sem=recv_sem.at[sem_index],
            device_id={"ctx": target}, device_id_type=pl.DeviceIdType.MESH,
        )
        copy.start()
        sends.append(copy)

    def arrive_part(slot, rows, sem_index):
        pltpu.make_async_remote_copy(
            src_ref=out_ref.at[slot, rows], dst_ref=out_ref.at[slot, rows],
            send_sem=send_sem.at[0], recv_sem=recv_sem.at[sem_index],
            device_id={"ctx": partner}, device_id_type=pl.DeviceIdType.MESH,
        ).wait_recv()

    upward = ring // 2
    half = x_ref.shape[0] // 2
    top = pl.ds(0, half)
    bottom = pl.ds(half, half)
    send(me, partner, x_ref)
    send(me, up, x_ref)
    send(me, down, x_ref)
    arrive(partner)
    send(partner, up, out_ref.at[partner])
    send(partner, down, out_ref.at[partner])
    my_tile = jnp.int32(0)
    for tile in range(owner_ref.shape[1]):
        my_tile = my_tile + jnp.where(owner_ref[0, tile] == me, tile, 0)
    trained = my_tile >= prompt
    last = owner_ref.shape[1] - 1
    above = parent_ref[0, jnp.clip(my_tile, 0, last)]
    second = jnp.logical_and(trained, above >= prompt)
    info_ref[0] = owner_ref[0, 0]
    info_ref[1] = owner_ref[0, 1]
    info_ref[2] = owner_ref[0, jnp.clip(jnp.where(second, above, 1), 0, last)]
    info_ref[3] = me
    info_ref[4] = trained.astype(jnp.int32)
    info_ref[5] = trained.astype(jnp.int32)
    info_ref[6] = second.astype(jnp.int32)
    info_ref[7] = trained.astype(jnp.int32)
    for step in range(2, upward + 1):
        for offset in (0, 1):
            slot = origin(-(step - 1), offset)
            arrive(slot)
            if step < upward:
                send(slot, up, out_ref.at[slot])
            else:
                send_part(slot, up, top, slot)
        for offset in (0, 1):
            slot = origin(step - 1, offset)
            arrive(slot)
            if step < upward:
                send(slot, down, out_ref.at[slot])
            else:
                send_part(slot, down, bottom, n + offset)
    for offset in (0, 1):
        arrive_part(origin(-upward, offset), top, origin(-upward, offset))
        arrive_part(origin(upward, offset), bottom, n + offset)
    for copy in sends:
        copy.wait_send()
    local.wait()


def relay_gather(owner, parent, x, prompt, collective_id):
    n = lax.axis_size("ctx")
    smem = pl.BlockSpec(memory_space=pltpu.SMEM)
    return pl.pallas_call(
        functools.partial(relay_gather_kernel, n=n, prompt=prompt),
        out_shape=[
            jax.ShapeDtypeStruct((n,) + tuple(x.shape), x.dtype),
            jax.ShapeDtypeStruct((8,), jnp.int32),
        ],
        in_specs=[smem, smem, pl.BlockSpec(memory_space=pl.ANY)],
        out_specs=[pl.BlockSpec(memory_space=pl.ANY), smem],
        scratch_shapes=[
            pltpu.SemaphoreType.DMA((n + 1,)),
            pltpu.SemaphoreType.DMA((n + 2,)),
            pltpu.SemaphoreType.DMA,
        ],
        compiler_params=pltpu.CompilerParams(collective_id=collective_id, has_side_effects=True),
    )(owner, parent, x)


def relay_reduce_kernel(t_ref, x_ref, tail_ref, out_ref, tails_ref, up_in, down_in, up_out,
                        down_out, side_out, side_in, tails_in, send_sem, recv_sem, tail_send,
                        tail_recv, *, n):
    me = lax.axis_index("ctx")
    ring = n // 2
    z = me // 2
    side = me % 2
    partner = z * 2 + (1 - side)
    up = lax.rem(z + 1, ring) * 2 + side
    down = lax.rem(z + ring - 1, ring) * 2 + side
    upward = ring // 2
    barrier = pltpu.get_barrier_semaphore()
    for d in range(1, n):
        pl.semaphore_signal(barrier, inc=1, device_id={"ctx": lax.rem(me + d, n)},
                            device_id_type=pl.DeviceIdType.MESH)
    pl.semaphore_wait(barrier, n - 1)
    tail_copies = []
    for d in range(1, n):
        copy = pltpu.make_async_remote_copy(
            src_ref=tail_ref, dst_ref=tails_in.at[me], send_sem=tail_send.at[d - 1],
            recv_sem=tail_recv.at[d - 1], device_id={"ctx": lax.rem(me + d, n)},
            device_id_type=pl.DeviceIdType.MESH,
        )
        copy.start()
        tail_copies.append(copy)
    tails_in[me] = tail_ref[...]
    sends = []

    def send(src, dst, target, sem_index):
        copy = pltpu.make_async_remote_copy(
            src_ref=src, dst_ref=dst, send_sem=send_sem.at[len(sends)],
            recv_sem=recv_sem.at[sem_index], device_id={"ctx": target},
            device_id_type=pl.DeviceIdType.MESH,
        )
        copy.start()
        sends.append(copy)
        return copy

    def own(target_z):
        base = lax.rem(target_z + 2 * ring, ring) * 2
        pieces = []
        for offset in (0, 1):
            total = jnp.zeros(x_ref.shape[1:], jnp.float32)
            for j in range(x_ref.shape[0]):
                total = total + jnp.where(t_ref[j] == base + offset, x_ref[j], 0.0)
            pieces.append(total)
        return jnp.stack(pieces)

    half = x_ref.shape[1] // 2
    top = pl.ds(0, half)
    bottom = pl.ds(half, half)
    pending_up = None
    pending_down = None
    for step in range(1, upward + 1):
        term = own(z + upward - step + 1)
        if step == 1:
            up_out[0, :, top] = term[:, :half].astype(up_out.dtype)
            pending_up = send(up_out.at[0, :, top], up_in.at[0, :, top], up, 0)
        else:
            pending_up.wait_recv()
            if step == 2:
                term = jnp.concatenate(
                    [term[:, :half] + up_in[0, :, top].astype(jnp.float32), term[:, half:]], axis=1
                )
            else:
                term = term + up_in[step - 2].astype(jnp.float32)
            up_out[step - 1] = term.astype(up_out.dtype)
            pending_up = send(up_out.at[step - 1], up_in.at[step - 1], up, step - 1)
        term = own(z - (upward - step + 1))
        if step == 1:
            down_out[0, :, bottom] = term[:, half:].astype(down_out.dtype)
            pending_down = send(down_out.at[0, :, bottom], down_in.at[0, :, bottom], down,
                                upward)
        else:
            pending_down.wait_recv()
            if step == 2:
                term = jnp.concatenate(
                    [term[:, :half], term[:, half:] + down_in[0, :, bottom].astype(jnp.float32)],
                    axis=1,
                )
            else:
                term = term + down_in[step - 2].astype(jnp.float32)
            down_out[step - 1] = term.astype(down_out.dtype)
            pending_down = send(down_out.at[step - 1], down_in.at[step - 1], down,
                                upward + step - 1)
    pending_up.wait_recv()
    pending_down.wait_recv()
    mine = (own(z) + up_in[upward - 1].astype(jnp.float32)
            + down_in[upward - 1].astype(jnp.float32))
    side_out[...] = jnp.where(side == 0, mine[1], mine[0])
    across = send(side_out, side_in, partner, 2 * upward)
    across.wait_recv()
    out_ref[...] = jnp.where(side == 0, mine[0], mine[1]) + side_in[...]
    for copy in sends:
        copy.wait_send()
    for copy in tail_copies:
        copy.wait_send()
    for copy in tail_copies:
        copy.wait_recv()
    summed = tails_in[0]
    for peer in range(1, n):
        summed = summed + tails_in[peer]
    tails_ref[...] = summed


def relay_reduce(targets, partial, tail, n, collective_id):
    _, rows, cols = partial.shape
    ring = n // 2
    upward = ring // 2
    downward = upward
    vmem = pl.BlockSpec(memory_space=pltpu.VMEM)
    return pl.pallas_call(
        functools.partial(relay_reduce_kernel, n=n),
        out_shape=[
            jax.ShapeDtypeStruct((rows, cols), jnp.float32),
            jax.ShapeDtypeStruct(tuple(tail.shape), jnp.float32),
        ],
        in_specs=[pl.BlockSpec(memory_space=pltpu.SMEM), vmem, vmem],
        out_specs=[vmem, vmem],
        scratch_shapes=[
            pltpu.VMEM((upward, 2, rows, cols), jnp.bfloat16),
            pltpu.VMEM((downward, 2, rows, cols), jnp.bfloat16),
            pltpu.VMEM((upward, 2, rows, cols), jnp.bfloat16),
            pltpu.VMEM((downward, 2, rows, cols), jnp.bfloat16),
            pltpu.VMEM((rows, cols), jnp.float32),
            pltpu.VMEM((rows, cols), jnp.float32),
            pltpu.VMEM((n,) + tuple(tail.shape), jnp.float32),
            pltpu.SemaphoreType.DMA((upward + downward + 1,)),
            pltpu.SemaphoreType.DMA((upward + downward + 1,)),
            pltpu.SemaphoreType.DMA((n - 1,)),
            pltpu.SemaphoreType.DMA((n - 1,)),
        ],
        compiler_params=pltpu.CompilerParams(
            collective_id=collective_id, has_side_effects=True,
            vmem_limit_bytes=56 * 1024 * 1024,
        ),
    )(targets, partial, tail)


def on_device(query, key, value, output, output_gradient, parent, owner):
    count = lax.axis_size("ctx")
    me = lax.axis_index("ctx")
    tile = query.shape[1]
    width = key.shape[2]
    scale_factor = HEAD_WIDTH ** (-0.5)
    prompt_tiles = count // 8
    pair = jnp.concatenate([key[0], value[0]], axis=1)
    gathered, info = relay_gather(owner, parent, pair, prompt_tiles, 0)
    dq, partial, tail = attention_grads(
        info, query[0], output_gradient[0], output[0], gathered, scale_factor
    )
    total_rows = lax.axis_size("dp") * query.shape[0] * count * tile
    norm = total_rows ** (-0.5)
    wide = query.shape[2]
    grads, summed = relay_reduce(info, partial, tail, count, 1)
    both = exchange(summed, "dp", False, 2)
    sums = (both[0] + both[1]).reshape(-1) * norm
    sum_q = sums[:wide]
    sum_k = sums[wide:wide + HEAD_WIDTH]
    sum_v = sums[wide + HEAD_WIDTH:wide + 2 * HEAD_WIDTH]
    return (
        dq[None],
        grads[:, :width].astype(jnp.bfloat16)[None],
        grads[:, width:].astype(jnp.bfloat16)[None],
        sum_q,
        sum_k,
        sum_v,
    )


def solution(mesh):
    return jax.shard_map(
        on_device,
        mesh=mesh,
        in_specs=(
            P("dp", "ctx", "head"),
            P("dp", "ctx", "head"),
            P("dp", "ctx", "head"),
            P("dp", "ctx", "head"),
            P("dp", "ctx", "head"),
            P("dp", None),
            P("dp", None),
        ),
        out_specs=(
            P("dp", "ctx", "head"),
            P("dp", "ctx", "head"),
            P("dp", "ctx", "head"),
            P("head"),
            P("head"),
            P("head"),
        ),
        check_vma=False,
    )
```

```python
import functools

import jax
import jax.numpy as jnp
from jax import lax
from jax.experimental import pallas as pl
from jax.experimental.pallas import tpu as pltpu
from jax.sharding import PartitionSpec as P

HEAD_WIDTH = 128

NEGATIVE_FILL = -1e30


def pick_entry(vector, index):
    spots = jnp.arange(vector.shape[0], dtype=jnp.int32)
    return jnp.sum(jnp.where(spots == index, vector, 0), axis=0)


def pick_rows(matrix, index):
    spots = jnp.arange(matrix.shape[0], dtype=jnp.int32)
    return jnp.sum(jnp.where((spots == index)[:, None], matrix, 0.0), axis=0)


def attention_grads_kernel(flags_ref, q_ref, g_ref, o_ref, k0, k1, k2, k3, v0, v1, v2,
                           v3, dq_ref, kv_ref, tail_ref, s_scr, *, scale):
    head = pl.program_id(0)
    k_refs = (k0, k1, k2, k3)
    v_refs = (v0, v1, v2, v3)
    slots = len(k_refs)

    width = q_ref.shape[1]
    dk_ref = kv_ref.at[:, :, pl.ds(0, width)]
    dv_ref = kv_ref.at[:, :, pl.ds(width, width)]

    @pl.when(head == 0)
    def _():
        kv_ref[...] = jnp.zeros_like(kv_ref)
        tail_ref[...] = jnp.zeros_like(tail_ref)

    q = q_ref[...]
    g = g_ref[...]
    o = o_ref[...]
    rows = q.shape[0]
    delta = jnp.sum(g.astype(jnp.float32) * o.astype(jnp.float32), axis=1, keepdims=True)
    causal = (lax.broadcasted_iota(jnp.int32, (rows, rows), 0)
              >= lax.broadcasted_iota(jnp.int32, (rows, rows), 1))
    nt = (((1,), (1,)), ((), ()))
    tn = (((0,), (0,)), ((), ()))

    top = jnp.full((rows, 1), NEGATIVE_FILL, jnp.float32)
    for j in range(slots):
        keep = flags_ref[slots + j] > 0
        if j == slots - 1:
            keep = jnp.logical_and(keep, causal)
        scores = lax.dot_general(q, k_refs[j][...], nt, preferred_element_type=jnp.float32) * scale
        scores = jnp.where(keep, scores, NEGATIVE_FILL)
        s_scr[j] = scores
        top = jnp.maximum(top, jnp.max(scores, axis=1, keepdims=True))

    total = jnp.zeros((rows, 1), jnp.float32)
    for j in range(slots):
        keep = flags_ref[slots + j] > 0
        if j == slots - 1:
            keep = jnp.logical_and(keep, causal)
        probs = jnp.where(keep, jnp.exp(s_scr[j] - top), 0.0)
        s_scr[j] = probs
        total = total + jnp.sum(probs, axis=1, keepdims=True)
    inverse = jnp.where(total > 0, 1.0 / jnp.where(total > 0, total, 1.0), 0.0)

    dq = jnp.zeros((rows, q.shape[1]), jnp.float32)
    for j in range(slots):
        probs = s_scr[j] * inverse
        dv_ref[j] += lax.dot_general(probs.astype(jnp.bfloat16), g, tn,
                                     preferred_element_type=jnp.float32)
        dprobs = lax.dot_general(g, v_refs[j][...], nt, preferred_element_type=jnp.float32)
        dscores = (probs * (dprobs - delta)).astype(jnp.bfloat16)
        dq = dq + jnp.dot(dscores, k_refs[j][...], preferred_element_type=jnp.float32)
        dk_ref[j] += lax.dot_general(dscores, q, tn, preferred_element_type=jnp.float32) * scale
    dq = dq * scale
    dq_ref[...] = dq.astype(dq_ref.dtype)
    tail_ref[pl.ds(head, 1), :] = jnp.sum(dq, axis=0, keepdims=True)

    @pl.when(head == pl.num_programs(0) - 1)
    def _():
        heads = pl.num_programs(0)
        tail_ref[pl.ds(heads, 1), :] = jnp.sum(jnp.sum(dk_ref[...], axis=0), axis=0, keepdims=True)
        tail_ref[pl.ds(heads + 1, 1), :] = jnp.sum(
            jnp.sum(dv_ref[...], axis=0), axis=0, keepdims=True
        )


def attention_grads(blocks, q, g, o, gathered, scale):
    rows, wide = q.shape
    slots = blocks.shape[0] // 2
    heads = wide // HEAD_WIDTH
    col = pl.BlockSpec((rows, HEAD_WIDTH), lambda h, b: (0, h))
    tail_spec = pl.BlockSpec((8, HEAD_WIDTH), lambda h, b: (0, 0))
    pair_spec = pl.BlockSpec((slots, rows, 2 * HEAD_WIDTH), lambda h, b: (0, 0, 0))

    def pick(j, part):
        return pl.BlockSpec((None, rows, HEAD_WIDTH), lambda h, b: (b[j], 0, part))

    return pl.pallas_call(
        functools.partial(attention_grads_kernel, scale=scale),
        grid_spec=pltpu.PrefetchScalarGridSpec(
            num_scalar_prefetch=1,
            grid=(heads,),
            in_specs=[col, col, col] + [pick(j, 0) for j in range(slots)]
            + [pick(j, 1) for j in range(slots)],
            out_specs=[col, pair_spec, tail_spec],
            scratch_shapes=[pltpu.VMEM((slots, rows, rows), jnp.float32)],
        ),
        out_shape=[
            jax.ShapeDtypeStruct((rows, wide), jnp.bfloat16),
            jax.ShapeDtypeStruct((slots, rows, 2 * HEAD_WIDTH), jnp.float32),
            jax.ShapeDtypeStruct((8, HEAD_WIDTH), jnp.float32),
        ],
        compiler_params=pltpu.CompilerParams(
            dimension_semantics=("arbitrary",), vmem_limit_bytes=63 * 1024 * 1024
        ),
    )(blocks, q, g, o, *([gathered] * (2 * slots)))


def exchange_kernel(x_ref, out_ref, send_sem, recv_sem, self_sem, *, axis, n, indexed):
    me = lax.axis_index(axis)
    barrier = pltpu.get_barrier_semaphore()
    for d in range(1, n):
        pl.semaphore_signal(
            barrier, inc=1, device_id={axis: lax.rem(me + d, n)},
            device_id_type=pl.DeviceIdType.MESH,
        )
    pl.semaphore_wait(barrier, n - 1)
    copies = []
    for d in range(1, n):
        peer = lax.rem(me + d, n)
        copy = pltpu.make_async_remote_copy(
            src_ref=x_ref.at[peer] if indexed else x_ref,
            dst_ref=out_ref.at[me],
            send_sem=send_sem.at[d - 1],
            recv_sem=recv_sem.at[d - 1],
            device_id={axis: peer},
            device_id_type=pl.DeviceIdType.MESH,
        )
        copy.start()
        copies.append(copy)
    local = pltpu.make_async_copy(x_ref.at[me] if indexed else x_ref, out_ref.at[me], self_sem)
    local.start()
    for copy in copies:
        copy.wait_send()
    for copy in copies:
        copy.wait_recv()
    local.wait()


def exchange(x, axis, indexed, collective_id):
    n = lax.axis_size(axis)
    piece = x.shape[1:] if indexed else x.shape
    return pl.pallas_call(
        functools.partial(exchange_kernel, axis=axis, n=n, indexed=indexed),
        out_shape=jax.ShapeDtypeStruct((n,) + tuple(piece), x.dtype),
        in_specs=[pl.BlockSpec(memory_space=pl.ANY)],
        out_specs=pl.BlockSpec(memory_space=pl.ANY),
        scratch_shapes=[
            pltpu.SemaphoreType.DMA((n - 1,)),
            pltpu.SemaphoreType.DMA((n - 1,)),
            pltpu.SemaphoreType.DMA,
        ],
        compiler_params=pltpu.CompilerParams(collective_id=collective_id, has_side_effects=True),
    )(x)


def relay_gather_kernel(owner_ref, parent_ref, x_ref, out_ref, info_ref, send_sem, recv_sem,
                        self_sem, *, n, prompt):
    me = lax.axis_index("ctx")
    ring = n // 2
    z = me // 2
    side = me % 2
    partner = z * 2 + (1 - side)
    up = lax.rem(z + 1, ring) * 2 + side
    down = lax.rem(z + ring - 1, ring) * 2 + side
    barrier = pltpu.get_barrier_semaphore()
    for peer in (partner, up, down):
        pl.semaphore_signal(barrier, inc=1, device_id={"ctx": peer},
                            device_id_type=pl.DeviceIdType.MESH)
    pl.semaphore_wait(barrier, 3)
    local = pltpu.make_async_copy(x_ref, out_ref.at[me], self_sem)
    local.start()
    sends = []

    def send(slot, target, src):
        copy = pltpu.make_async_remote_copy(
            src_ref=src, dst_ref=out_ref.at[slot], send_sem=send_sem.at[len(sends)],
            recv_sem=recv_sem.at[slot], device_id={"ctx": target},
            device_id_type=pl.DeviceIdType.MESH,
        )
        copy.start()
        sends.append(copy)

    def arrive(slot):
        pltpu.make_async_remote_copy(
            src_ref=x_ref, dst_ref=out_ref.at[slot], send_sem=send_sem.at[0],
            recv_sem=recv_sem.at[slot], device_id={"ctx": partner},
            device_id_type=pl.DeviceIdType.MESH,
        ).wait_recv()

    def origin(step, offset):
        return lax.rem(z + step + 2 * ring, ring) * 2 + offset

    def send_part(slot, target, rows, sem_index):
        copy = pltpu.make_async_remote_copy(
            src_ref=out_ref.at[slot, rows], dst_ref=out_ref.at[slot, rows],
            send_sem=send_sem.at[len(sends)], recv_sem=recv_sem.at[sem_index],
            device_id={"ctx": target}, device_id_type=pl.DeviceIdType.MESH,
        )
        copy.start()
        sends.append(copy)

    def arrive_part(slot, rows, sem_index):
        pltpu.make_async_remote_copy(
            src_ref=out_ref.at[slot, rows], dst_ref=out_ref.at[slot, rows],
            send_sem=send_sem.at[0], recv_sem=recv_sem.at[sem_index],
            device_id={"ctx": partner}, device_id_type=pl.DeviceIdType.MESH,
        ).wait_recv()

    upward = ring // 2
    half = x_ref.shape[0] // 2
    top = pl.ds(0, half)
    bottom = pl.ds(half, half)
    send(me, partner, x_ref)
    send(me, up, x_ref)
    send(me, down, x_ref)
    arrive(partner)
    send(partner, up, out_ref.at[partner])
    send(partner, down, out_ref.at[partner])
    my_tile = jnp.int32(0)
    for tile in range(owner_ref.shape[1]):
        my_tile = my_tile + jnp.where(owner_ref[0, tile] == me, tile, 0)
    trained = my_tile >= prompt
    last = owner_ref.shape[1] - 1
    above = parent_ref[0, jnp.clip(my_tile, 0, last)]
    second = jnp.logical_and(trained, above >= prompt)
    info_ref[0] = owner_ref[0, 0]
    info_ref[1] = owner_ref[0, 1]
    info_ref[2] = owner_ref[0, jnp.clip(jnp.where(second, above, 1), 0, last)]
    info_ref[3] = me
    info_ref[4] = trained.astype(jnp.int32)
    info_ref[5] = trained.astype(jnp.int32)
    info_ref[6] = second.astype(jnp.int32)
    info_ref[7] = trained.astype(jnp.int32)
    for step in range(2, upward + 1):
        for offset in (0, 1):
            slot = origin(-(step - 1), offset)
            arrive(slot)
            if step < upward:
                send(slot, up, out_ref.at[slot])
            else:
                send_part(slot, up, top, slot)
        for offset in (0, 1):
            slot = origin(step - 1, offset)
            arrive(slot)
            if step < upward:
                send(slot, down, out_ref.at[slot])
            else:
                send_part(slot, down, bottom, n + offset)
    for offset in (0, 1):
        arrive_part(origin(-upward, offset), top, origin(-upward, offset))
        arrive_part(origin(upward, offset), bottom, n + offset)
    for copy in sends:
        copy.wait_send()
    local.wait()


def relay_gather(owner, parent, x, prompt, collective_id):
    n = lax.axis_size("ctx")
    smem = pl.BlockSpec(memory_space=pltpu.SMEM)
    return pl.pallas_call(
        functools.partial(relay_gather_kernel, n=n, prompt=prompt),
        out_shape=[
            jax.ShapeDtypeStruct((n,) + tuple(x.shape), x.dtype),
            jax.ShapeDtypeStruct((8,), jnp.int32),
        ],
        in_specs=[smem, smem, pl.BlockSpec(memory_space=pl.ANY)],
        out_specs=[pl.BlockSpec(memory_space=pl.ANY), smem],
        scratch_shapes=[
            pltpu.SemaphoreType.DMA((n + 1,)),
            pltpu.SemaphoreType.DMA((n + 2,)),
            pltpu.SemaphoreType.DMA,
        ],
        compiler_params=pltpu.CompilerParams(collective_id=collective_id, has_side_effects=True),
    )(owner, parent, x)


def relay_reduce_kernel(t_ref, x_ref, tail_ref, out_ref, tails_ref, up_in, down_in, up_out,
                        down_out, side_out, side_in, tails_in, pair_out, pair_in, send_sem,
                        recv_sem, tail_send, tail_recv, pair_sem, *, n):
    me = lax.axis_index("ctx")
    ring = n // 2
    z = me // 2
    side = me % 2
    partner = z * 2 + (1 - side)
    up = lax.rem(z + 1, ring) * 2 + side
    down = lax.rem(z + ring - 1, ring) * 2 + side
    upward = ring // 2
    barrier = pltpu.get_barrier_semaphore()
    for d in range(1, n):
        pl.semaphore_signal(barrier, inc=1, device_id={"ctx": lax.rem(me + d, n)},
                            device_id_type=pl.DeviceIdType.MESH)
    other = 1 - lax.axis_index("dp")
    pl.semaphore_signal(barrier, inc=1, device_id={"dp": other},
                        device_id_type=pl.DeviceIdType.MESH)
    pl.semaphore_wait(barrier, n)
    tail_copies = []
    for d in range(1, n):
        copy = pltpu.make_async_remote_copy(
            src_ref=tail_ref, dst_ref=tails_in.at[me], send_sem=tail_send.at[d - 1],
            recv_sem=tail_recv.at[d - 1], device_id={"ctx": lax.rem(me + d, n)},
            device_id_type=pl.DeviceIdType.MESH,
        )
        copy.start()
        tail_copies.append(copy)
    tails_in[me] = tail_ref[...]
    sends = []

    def send(src, dst, target, sem_index):
        copy = pltpu.make_async_remote_copy(
            src_ref=src, dst_ref=dst, send_sem=send_sem.at[len(sends)],
            recv_sem=recv_sem.at[sem_index], device_id={"ctx": target},
            device_id_type=pl.DeviceIdType.MESH,
        )
        copy.start()
        sends.append(copy)
        return copy

    def own(target_z):
        base = lax.rem(target_z + 2 * ring, ring) * 2
        pieces = []
        for offset in (0, 1):
            total = jnp.zeros(x_ref.shape[1:], jnp.float32)
            for j in range(x_ref.shape[0]):
                total = total + jnp.where(t_ref[j] == base + offset, x_ref[j], 0.0)
            pieces.append(total)
        return jnp.stack(pieces)

    half = x_ref.shape[1] // 2
    top = pl.ds(0, half)
    bottom = pl.ds(half, half)
    pending_up = None
    pending_down = None
    for step in range(1, upward + 1):
        term = own(z + upward - step + 1)
        if step == 1:
            up_out[0, :, top] = term[:, :half].astype(up_out.dtype)
            pending_up = send(up_out.at[0, :, top], up_in.at[0, :, top], up, 0)
        else:
            pending_up.wait_recv()
            if step == 2:
                term = jnp.concatenate(
                    [term[:, :half] + up_in[0, :, top].astype(jnp.float32), term[:, half:]], axis=1
                )
            else:
                term = term + up_in[step - 2].astype(jnp.float32)
            up_out[step - 1] = term.astype(up_out.dtype)
            pending_up = send(up_out.at[step - 1], up_in.at[step - 1], up, step - 1)
        term = own(z - (upward - step + 1))
        if step == 1:
            down_out[0, :, bottom] = term[:, half:].astype(down_out.dtype)
            pending_down = send(down_out.at[0, :, bottom], down_in.at[0, :, bottom], down,
                                upward)
        else:
            pending_down.wait_recv()
            if step == 2:
                term = jnp.concatenate(
                    [term[:, :half], term[:, half:] + down_in[0, :, bottom].astype(jnp.float32)],
                    axis=1,
                )
            else:
                term = term + down_in[step - 2].astype(jnp.float32)
            down_out[step - 1] = term.astype(down_out.dtype)
            pending_down = send(down_out.at[step - 1], down_in.at[step - 1], down,
                                upward + step - 1)
    pending_up.wait_recv()
    pending_down.wait_recv()
    mine = (own(z) + up_in[upward - 1].astype(jnp.float32)
            + down_in[upward - 1].astype(jnp.float32))
    side_out[...] = jnp.where(side == 0, mine[1], mine[0])
    across = send(side_out, side_in, partner, 2 * upward)
    across.wait_recv()
    out_ref[...] = jnp.where(side == 0, mine[0], mine[1]) + side_in[...]
    for copy in sends:
        copy.wait_send()
    for copy in tail_copies:
        copy.wait_send()
    for copy in tail_copies:
        copy.wait_recv()
    summed = tails_in[0]
    for peer in range(1, n):
        summed = summed + tails_in[peer]
    pair_out[...] = summed
    swap = pltpu.make_async_remote_copy(
        src_ref=pair_out, dst_ref=pair_in, send_sem=pair_sem.at[0], recv_sem=pair_sem.at[1],
        device_id={"dp": other}, device_id_type=pl.DeviceIdType.MESH,
    )
    swap.start()
    swap.wait_send()
    swap.wait_recv()
    tails_ref[...] = summed + pair_in[...]


def relay_reduce(targets, partial, tail, n, collective_id):
    _, rows, cols = partial.shape
    ring = n // 2
    upward = ring // 2
    downward = upward
    vmem = pl.BlockSpec(memory_space=pltpu.VMEM)
    return pl.pallas_call(
        functools.partial(relay_reduce_kernel, n=n),
        out_shape=[
            jax.ShapeDtypeStruct((rows, cols), jnp.float32),
            jax.ShapeDtypeStruct(tuple(tail.shape), jnp.float32),
        ],
        in_specs=[pl.BlockSpec(memory_space=pltpu.SMEM), vmem, vmem],
        out_specs=[vmem, vmem],
        scratch_shapes=[
            pltpu.VMEM((upward, 2, rows, cols), jnp.bfloat16),
            pltpu.VMEM((downward, 2, rows, cols), jnp.bfloat16),
            pltpu.VMEM((upward, 2, rows, cols), jnp.bfloat16),
            pltpu.VMEM((downward, 2, rows, cols), jnp.bfloat16),
            pltpu.VMEM((rows, cols), jnp.float32),
            pltpu.VMEM((rows, cols), jnp.float32),
            pltpu.VMEM((n,) + tuple(tail.shape), jnp.float32),
            pltpu.VMEM(tuple(tail.shape), jnp.float32),
            pltpu.VMEM(tuple(tail.shape), jnp.float32),
            pltpu.SemaphoreType.DMA((upward + downward + 1,)),
            pltpu.SemaphoreType.DMA((upward + downward + 1,)),
            pltpu.SemaphoreType.DMA((n - 1,)),
            pltpu.SemaphoreType.DMA((n - 1,)),
            pltpu.SemaphoreType.DMA((2,)),
        ],
        compiler_params=pltpu.CompilerParams(
            collective_id=collective_id, has_side_effects=True,
            vmem_limit_bytes=56 * 1024 * 1024,
        ),
    )(targets, partial, tail)


def on_device(query, key, value, output, output_gradient, parent, owner):
    count = lax.axis_size("ctx")
    me = lax.axis_index("ctx")
    tile = query.shape[1]
    width = key.shape[2]
    scale_factor = HEAD_WIDTH ** (-0.5)
    prompt_tiles = count // 8
    pair = jnp.concatenate([key[0], value[0]], axis=1)
    gathered, info = relay_gather(owner, parent, pair, prompt_tiles, 0)
    dq, partial, tail = attention_grads(
        info, query[0], output_gradient[0], output[0], gathered, scale_factor
    )
    total_rows = lax.axis_size("dp") * query.shape[0] * count * tile
    norm = total_rows ** (-0.5)
    wide = query.shape[2]
    grads, summed = relay_reduce(info, partial, tail, count, 1)
    sums = summed.reshape(-1) * norm
    sum_q = sums[:wide]
    sum_k = sums[wide:wide + HEAD_WIDTH]
    sum_v = sums[wide + HEAD_WIDTH:wide + 2 * HEAD_WIDTH]
    return (
        dq[None],
        grads[:, :width].astype(jnp.bfloat16)[None],
        grads[:, width:].astype(jnp.bfloat16)[None],
        sum_q,
        sum_k,
        sum_v,
    )


def solution(mesh):
    return jax.shard_map(
        on_device,
        mesh=mesh,
        in_specs=(
            P("dp", "ctx", "head"),
            P("dp", "ctx", "head"),
            P("dp", "ctx", "head"),
            P("dp", "ctx", "head"),
            P("dp", "ctx", "head"),
            P("dp", None),
            P("dp", None),
        ),
        out_specs=(
            P("dp", "ctx", "head"),
            P("dp", "ctx", "head"),
            P("dp", "ctx", "head"),
            P("head"),
            P("head"),
            P("head"),
        ),
        check_vma=False,
    )
```

```python
import functools

import jax
import jax.numpy as jnp
from jax import lax
from jax.experimental import pallas as pl
from jax.experimental.pallas import tpu as pltpu
from jax.sharding import PartitionSpec as P

HEAD_WIDTH = 128

NEGATIVE_FILL = -1e30


def pick_entry(vector, index):
    spots = jnp.arange(vector.shape[0], dtype=jnp.int32)
    return jnp.sum(jnp.where(spots == index, vector, 0), axis=0)


def pick_rows(matrix, index):
    spots = jnp.arange(matrix.shape[0], dtype=jnp.int32)
    return jnp.sum(jnp.where((spots == index)[:, None], matrix, 0.0), axis=0)


def attention_grads_kernel(flags_ref, q_ref, g_ref, o_ref, k0, k1, k2, k3, v0, v1, v2,
                           v3, dq_ref, kv_ref, tail_ref, s_scr, *, scale):
    head = pl.program_id(0)
    k_refs = (k0, k1, k2, k3)
    v_refs = (v0, v1, v2, v3)
    slots = len(k_refs)

    width = q_ref.shape[1]
    dk_ref = kv_ref.at[:, :, pl.ds(0, width)]
    dv_ref = kv_ref.at[:, :, pl.ds(width, width)]

    @pl.when(head == 0)
    def _():
        kv_ref[...] = jnp.zeros_like(kv_ref)
        tail_ref[...] = jnp.zeros_like(tail_ref)

    q = q_ref[...]
    g = g_ref[...]
    o = o_ref[...]
    rows = q.shape[0]
    delta = jnp.sum(g.astype(jnp.float32) * o.astype(jnp.float32), axis=1, keepdims=True)
    causal = (lax.broadcasted_iota(jnp.int32, (rows, rows), 0)
              >= lax.broadcasted_iota(jnp.int32, (rows, rows), 1))
    nt = (((1,), (1,)), ((), ()))
    tn = (((0,), (0,)), ((), ()))

    top = jnp.full((rows, 1), NEGATIVE_FILL, jnp.float32)
    for j in range(slots):
        keep = flags_ref[slots + j] > 0
        if j == slots - 1:
            keep = jnp.logical_and(keep, causal)
        scores = lax.dot_general(q, k_refs[j][...], nt, preferred_element_type=jnp.float32) * scale
        scores = jnp.where(keep, scores, NEGATIVE_FILL)
        s_scr[j] = scores
        top = jnp.maximum(top, jnp.max(scores, axis=1, keepdims=True))

    total = jnp.zeros((rows, 1), jnp.float32)
    for j in range(slots):
        keep = flags_ref[slots + j] > 0
        if j == slots - 1:
            keep = jnp.logical_and(keep, causal)
        probs = jnp.where(keep, jnp.exp(s_scr[j] - top), 0.0)
        s_scr[j] = probs
        total = total + jnp.sum(probs, axis=1, keepdims=True)
    inverse = jnp.where(total > 0, 1.0 / jnp.where(total > 0, total, 1.0), 0.0)

    dq = jnp.zeros((rows, q.shape[1]), jnp.float32)
    for j in range(slots):
        probs = s_scr[j] * inverse
        dv_ref[j] += lax.dot_general(probs.astype(jnp.bfloat16), g, tn,
                                     preferred_element_type=jnp.float32)
        dprobs = lax.dot_general(g, v_refs[j][...], nt, preferred_element_type=jnp.float32)
        dscores = (probs * (dprobs - delta)).astype(jnp.bfloat16)
        dq = dq + jnp.dot(dscores, k_refs[j][...], preferred_element_type=jnp.float32)
        dk_ref[j] += lax.dot_general(dscores, q, tn, preferred_element_type=jnp.float32) * scale
    dq = dq * scale
    dq_ref[...] = dq.astype(dq_ref.dtype)
    tail_ref[pl.ds(head, 1), :] = jnp.sum(dq, axis=0, keepdims=True)

    @pl.when(head == pl.num_programs(0) - 1)
    def _():
        heads = pl.num_programs(0)
        tail_ref[pl.ds(heads, 1), :] = jnp.sum(jnp.sum(dk_ref[...], axis=0), axis=0, keepdims=True)
        tail_ref[pl.ds(heads + 1, 1), :] = jnp.sum(
            jnp.sum(dv_ref[...], axis=0), axis=0, keepdims=True
        )


def attention_grads(blocks, q, g, o, gathered, scale):
    rows, wide = q.shape
    slots = blocks.shape[0] // 2
    heads = wide // HEAD_WIDTH
    col = pl.BlockSpec((rows, HEAD_WIDTH), lambda h, b: (0, h))
    tail_spec = pl.BlockSpec((8, HEAD_WIDTH), lambda h, b: (0, 0))
    pair_spec = pl.BlockSpec((slots, rows, 2 * HEAD_WIDTH), lambda h, b: (0, 0, 0))

    def pick(j, part):
        return pl.BlockSpec((None, rows, HEAD_WIDTH), lambda h, b: (b[j], 0, part))

    return pl.pallas_call(
        functools.partial(attention_grads_kernel, scale=scale),
        grid_spec=pltpu.PrefetchScalarGridSpec(
            num_scalar_prefetch=1,
            grid=(heads,),
            in_specs=[col, col, col] + [pick(j, 0) for j in range(slots)]
            + [pick(j, 1) for j in range(slots)],
            out_specs=[col, pair_spec, tail_spec],
            scratch_shapes=[pltpu.VMEM((slots, rows, rows), jnp.float32)],
        ),
        out_shape=[
            jax.ShapeDtypeStruct((rows, wide), jnp.bfloat16),
            jax.ShapeDtypeStruct((slots, rows, 2 * HEAD_WIDTH), jnp.float32),
            jax.ShapeDtypeStruct((8, HEAD_WIDTH), jnp.float32),
        ],
        compiler_params=pltpu.CompilerParams(
            dimension_semantics=("arbitrary",), vmem_limit_bytes=63 * 1024 * 1024
        ),
    )(blocks, q, g, o, *([gathered] * (2 * slots)))


def exchange_kernel(x_ref, out_ref, send_sem, recv_sem, self_sem, *, axis, n, indexed):
    me = lax.axis_index(axis)
    barrier = pltpu.get_barrier_semaphore()
    for d in range(1, n):
        pl.semaphore_signal(
            barrier, inc=1, device_id={axis: lax.rem(me + d, n)},
            device_id_type=pl.DeviceIdType.MESH,
        )
    pl.semaphore_wait(barrier, n - 1)
    copies = []
    for d in range(1, n):
        peer = lax.rem(me + d, n)
        copy = pltpu.make_async_remote_copy(
            src_ref=x_ref.at[peer] if indexed else x_ref,
            dst_ref=out_ref.at[me],
            send_sem=send_sem.at[d - 1],
            recv_sem=recv_sem.at[d - 1],
            device_id={axis: peer},
            device_id_type=pl.DeviceIdType.MESH,
        )
        copy.start()
        copies.append(copy)
    local = pltpu.make_async_copy(x_ref.at[me] if indexed else x_ref, out_ref.at[me], self_sem)
    local.start()
    for copy in copies:
        copy.wait_send()
    for copy in copies:
        copy.wait_recv()
    local.wait()


def exchange(x, axis, indexed, collective_id):
    n = lax.axis_size(axis)
    piece = x.shape[1:] if indexed else x.shape
    return pl.pallas_call(
        functools.partial(exchange_kernel, axis=axis, n=n, indexed=indexed),
        out_shape=jax.ShapeDtypeStruct((n,) + tuple(piece), x.dtype),
        in_specs=[pl.BlockSpec(memory_space=pl.ANY)],
        out_specs=pl.BlockSpec(memory_space=pl.ANY),
        scratch_shapes=[
            pltpu.SemaphoreType.DMA((n - 1,)),
            pltpu.SemaphoreType.DMA((n - 1,)),
            pltpu.SemaphoreType.DMA,
        ],
        compiler_params=pltpu.CompilerParams(collective_id=collective_id, has_side_effects=True),
    )(x)


def relay_gather_kernel(owner_ref, parent_ref, k_ref, v_ref, out_ref, info_ref, send_sem,
                        recv_sem, self_sem, *, n, prompt):
    me = lax.axis_index("ctx")
    ring = n // 2
    z = me // 2
    side = me % 2
    partner = z * 2 + (1 - side)
    up = lax.rem(z + 1, ring) * 2 + side
    down = lax.rem(z + ring - 1, ring) * 2 + side
    barrier = pltpu.get_barrier_semaphore()
    for peer in (partner, up, down):
        pl.semaphore_signal(barrier, inc=1, device_id={"ctx": peer},
                            device_id_type=pl.DeviceIdType.MESH)
    pl.semaphore_wait(barrier, 3)
    width = k_ref.shape[1]
    left = pl.ds(0, width)
    right = pl.ds(width, width)
    locals_ = [
        pltpu.make_async_copy(k_ref, out_ref.at[me, :, left], self_sem.at[0]),
        pltpu.make_async_copy(v_ref, out_ref.at[me, :, right], self_sem.at[1]),
    ]
    for copy in locals_:
        copy.start()
    sends = []

    def send(slot, target, src):
        copy = pltpu.make_async_remote_copy(
            src_ref=src, dst_ref=out_ref.at[slot], send_sem=send_sem.at[len(sends)],
            recv_sem=recv_sem.at[slot], device_id={"ctx": target},
            device_id_type=pl.DeviceIdType.MESH,
        )
        copy.start()
        sends.append(copy)

    def send_own(target):
        for src, cols in ((k_ref, left), (v_ref, right)):
            copy = pltpu.make_async_remote_copy(
                src_ref=src, dst_ref=out_ref.at[me, :, cols], send_sem=send_sem.at[len(sends)],
                recv_sem=recv_sem.at[me], device_id={"ctx": target},
                device_id_type=pl.DeviceIdType.MESH,
            )
            copy.start()
            sends.append(copy)

    def arrive(slot):
        pltpu.make_async_remote_copy(
            src_ref=out_ref.at[slot], dst_ref=out_ref.at[slot], send_sem=send_sem.at[0],
            recv_sem=recv_sem.at[slot], device_id={"ctx": partner},
            device_id_type=pl.DeviceIdType.MESH,
        ).wait_recv()

    def origin(step, offset):
        return lax.rem(z + step + 2 * ring, ring) * 2 + offset

    def send_part(slot, target, rows, sem_index):
        copy = pltpu.make_async_remote_copy(
            src_ref=out_ref.at[slot, rows], dst_ref=out_ref.at[slot, rows],
            send_sem=send_sem.at[len(sends)], recv_sem=recv_sem.at[sem_index],
            device_id={"ctx": target}, device_id_type=pl.DeviceIdType.MESH,
        )
        copy.start()
        sends.append(copy)

    def arrive_part(slot, rows, sem_index):
        pltpu.make_async_remote_copy(
            src_ref=out_ref.at[slot, rows], dst_ref=out_ref.at[slot, rows],
            send_sem=send_sem.at[0], recv_sem=recv_sem.at[sem_index],
            device_id={"ctx": partner}, device_id_type=pl.DeviceIdType.MESH,
        ).wait_recv()

    upward = ring // 2
    half = k_ref.shape[0] // 2
    top = pl.ds(0, half)
    bottom = pl.ds(half, half)
    send_own(partner)
    send_own(up)
    send_own(down)
    arrive(partner)
    send(partner, up, out_ref.at[partner])
    send(partner, down, out_ref.at[partner])
    my_tile = jnp.int32(0)
    for tile in range(owner_ref.shape[1]):
        my_tile = my_tile + jnp.where(owner_ref[0, tile] == me, tile, 0)
    trained = my_tile >= prompt
    last = owner_ref.shape[1] - 1
    above = parent_ref[0, jnp.clip(my_tile, 0, last)]
    second = jnp.logical_and(trained, above >= prompt)
    info_ref[0] = owner_ref[0, 0]
    info_ref[1] = owner_ref[0, 1]
    info_ref[2] = owner_ref[0, jnp.clip(jnp.where(second, above, 1), 0, last)]
    info_ref[3] = me
    info_ref[4] = trained.astype(jnp.int32)
    info_ref[5] = trained.astype(jnp.int32)
    info_ref[6] = second.astype(jnp.int32)
    info_ref[7] = trained.astype(jnp.int32)
    for step in range(2, upward + 1):
        for offset in (0, 1):
            slot = origin(-(step - 1), offset)
            arrive(slot)
            if step < upward:
                send(slot, up, out_ref.at[slot])
            else:
                send_part(slot, up, top, slot)
        for offset in (0, 1):
            slot = origin(step - 1, offset)
            arrive(slot)
            if step < upward:
                send(slot, down, out_ref.at[slot])
            else:
                send_part(slot, down, bottom, n + offset)
    for offset in (0, 1):
        arrive_part(origin(-upward, offset), top, origin(-upward, offset))
        arrive_part(origin(upward, offset), bottom, n + offset)
    for copy in sends:
        copy.wait_send()
    for copy in locals_:
        copy.wait()


def relay_gather(owner, parent, k, v, prompt, collective_id):
    n = lax.axis_size("ctx")
    smem = pl.BlockSpec(memory_space=pltpu.SMEM)
    return pl.pallas_call(
        functools.partial(relay_gather_kernel, n=n, prompt=prompt),
        out_shape=[
            jax.ShapeDtypeStruct((n, k.shape[0], 2 * k.shape[1]), k.dtype),
            jax.ShapeDtypeStruct((8,), jnp.int32),
        ],
        in_specs=[smem, smem, pl.BlockSpec(memory_space=pl.ANY), pl.BlockSpec(memory_space=pl.ANY)],
        out_specs=[pl.BlockSpec(memory_space=pl.ANY), smem],
        scratch_shapes=[
            pltpu.SemaphoreType.DMA((n + 4,)),
            pltpu.SemaphoreType.DMA((n + 2,)),
            pltpu.SemaphoreType.DMA((2,)),
        ],
        compiler_params=pltpu.CompilerParams(collective_id=collective_id, has_side_effects=True),
    )(owner, parent, k, v)


def relay_reduce_kernel(t_ref, x_ref, tail_ref, out_ref, tails_ref, up_in, down_in, up_out,
                        down_out, side_out, side_in, tails_in, pair_out, pair_in, send_sem,
                        recv_sem, tail_send, tail_recv, pair_sem, *, n):
    me = lax.axis_index("ctx")
    ring = n // 2
    z = me // 2
    side = me % 2
    partner = z * 2 + (1 - side)
    up = lax.rem(z + 1, ring) * 2 + side
    down = lax.rem(z + ring - 1, ring) * 2 + side
    upward = ring // 2
    barrier = pltpu.get_barrier_semaphore()
    for d in range(1, n):
        pl.semaphore_signal(barrier, inc=1, device_id={"ctx": lax.rem(me + d, n)},
                            device_id_type=pl.DeviceIdType.MESH)
    other = 1 - lax.axis_index("dp")
    pl.semaphore_signal(barrier, inc=1, device_id={"dp": other},
                        device_id_type=pl.DeviceIdType.MESH)
    pl.semaphore_wait(barrier, n)
    tail_copies = []
    for d in range(1, n):
        copy = pltpu.make_async_remote_copy(
            src_ref=tail_ref, dst_ref=tails_in.at[me], send_sem=tail_send.at[d - 1],
            recv_sem=tail_recv.at[d - 1], device_id={"ctx": lax.rem(me + d, n)},
            device_id_type=pl.DeviceIdType.MESH,
        )
        copy.start()
        tail_copies.append(copy)
    tails_in[me] = tail_ref[...]
    sends = []

    def send(src, dst, target, sem_index):
        copy = pltpu.make_async_remote_copy(
            src_ref=src, dst_ref=dst, send_sem=send_sem.at[len(sends)],
            recv_sem=recv_sem.at[sem_index], device_id={"ctx": target},
            device_id_type=pl.DeviceIdType.MESH,
        )
        copy.start()
        sends.append(copy)
        return copy

    def own(target_z):
        base = lax.rem(target_z + 2 * ring, ring) * 2
        pieces = []
        for offset in (0, 1):
            total = jnp.zeros(x_ref.shape[1:], jnp.float32)
            for j in range(x_ref.shape[0]):
                total = total + jnp.where(t_ref[j] == base + offset, x_ref[j], 0.0)
            pieces.append(total)
        return jnp.stack(pieces)

    half = x_ref.shape[1] // 2
    top = pl.ds(0, half)
    bottom = pl.ds(half, half)
    pending_up = None
    pending_down = None
    for step in range(1, upward + 1):
        term = own(z + upward - step + 1)
        if step == 1:
            up_out[0, :, top] = term[:, :half].astype(up_out.dtype)
            pending_up = send(up_out.at[0, :, top], up_in.at[0, :, top], up, 0)
        else:
            pending_up.wait_recv()
            if step == 2:
                term = jnp.concatenate(
                    [term[:, :half] + up_in[0, :, top].astype(jnp.float32), term[:, half:]], axis=1
                )
            else:
                term = term + up_in[step - 2].astype(jnp.float32)
            up_out[step - 1] = term.astype(up_out.dtype)
            pending_up = send(up_out.at[step - 1], up_in.at[step - 1], up, step - 1)
        term = own(z - (upward - step + 1))
        if step == 1:
            down_out[0, :, bottom] = term[:, half:].astype(down_out.dtype)
            pending_down = send(down_out.at[0, :, bottom], down_in.at[0, :, bottom], down,
                                upward)
        else:
            pending_down.wait_recv()
            if step == 2:
                term = jnp.concatenate(
                    [term[:, :half], term[:, half:] + down_in[0, :, bottom].astype(jnp.float32)],
                    axis=1,
                )
            else:
                term = term + down_in[step - 2].astype(jnp.float32)
            down_out[step - 1] = term.astype(down_out.dtype)
            pending_down = send(down_out.at[step - 1], down_in.at[step - 1], down,
                                upward + step - 1)
    pending_up.wait_recv()
    pending_down.wait_recv()
    mine = (own(z) + up_in[upward - 1].astype(jnp.float32)
            + down_in[upward - 1].astype(jnp.float32))
    side_out[...] = jnp.where(side == 0, mine[1], mine[0])
    across = send(side_out, side_in, partner, 2 * upward)
    across.wait_recv()
    out_ref[...] = jnp.where(side == 0, mine[0], mine[1]) + side_in[...]
    for copy in sends:
        copy.wait_send()
    for copy in tail_copies:
        copy.wait_send()
    for copy in tail_copies:
        copy.wait_recv()
    summed = tails_in[0]
    for peer in range(1, n):
        summed = summed + tails_in[peer]
    pair_out[...] = summed
    swap = pltpu.make_async_remote_copy(
        src_ref=pair_out, dst_ref=pair_in, send_sem=pair_sem.at[0], recv_sem=pair_sem.at[1],
        device_id={"dp": other}, device_id_type=pl.DeviceIdType.MESH,
    )
    swap.start()
    swap.wait_send()
    swap.wait_recv()
    tails_ref[...] = summed + pair_in[...]


def relay_reduce(targets, partial, tail, n, collective_id):
    _, rows, cols = partial.shape
    ring = n // 2
    upward = ring // 2
    downward = upward
    vmem = pl.BlockSpec(memory_space=pltpu.VMEM)
    return pl.pallas_call(
        functools.partial(relay_reduce_kernel, n=n),
        out_shape=[
            jax.ShapeDtypeStruct((rows, cols), jnp.float32),
            jax.ShapeDtypeStruct(tuple(tail.shape), jnp.float32),
        ],
        in_specs=[pl.BlockSpec(memory_space=pltpu.SMEM), vmem, vmem],
        out_specs=[vmem, vmem],
        scratch_shapes=[
            pltpu.VMEM((upward, 2, rows, cols), jnp.bfloat16),
            pltpu.VMEM((downward, 2, rows, cols), jnp.bfloat16),
            pltpu.VMEM((upward, 2, rows, cols), jnp.bfloat16),
            pltpu.VMEM((downward, 2, rows, cols), jnp.bfloat16),
            pltpu.VMEM((rows, cols), jnp.float32),
            pltpu.VMEM((rows, cols), jnp.float32),
            pltpu.VMEM((n,) + tuple(tail.shape), jnp.float32),
            pltpu.VMEM(tuple(tail.shape), jnp.float32),
            pltpu.VMEM(tuple(tail.shape), jnp.float32),
            pltpu.SemaphoreType.DMA((upward + downward + 1,)),
            pltpu.SemaphoreType.DMA((upward + downward + 1,)),
            pltpu.SemaphoreType.DMA((n - 1,)),
            pltpu.SemaphoreType.DMA((n - 1,)),
            pltpu.SemaphoreType.DMA((2,)),
        ],
        compiler_params=pltpu.CompilerParams(
            collective_id=collective_id, has_side_effects=True,
            vmem_limit_bytes=56 * 1024 * 1024,
        ),
    )(targets, partial, tail)


def on_device(query, key, value, output, output_gradient, parent, owner):
    count = lax.axis_size("ctx")
    me = lax.axis_index("ctx")
    tile = query.shape[1]
    width = key.shape[2]
    scale_factor = HEAD_WIDTH ** (-0.5)
    prompt_tiles = count // 8
    gathered, info = relay_gather(owner, parent, key[0], value[0], prompt_tiles, 0)
    dq, partial, tail = attention_grads(
        info, query[0], output_gradient[0], output[0], gathered, scale_factor
    )
    total_rows = lax.axis_size("dp") * query.shape[0] * count * tile
    norm = total_rows ** (-0.5)
    wide = query.shape[2]
    grads, summed = relay_reduce(info, partial, tail, count, 1)
    sums = summed.reshape(-1) * norm
    sum_q = sums[:wide]
    sum_k = sums[wide:wide + HEAD_WIDTH]
    sum_v = sums[wide + HEAD_WIDTH:wide + 2 * HEAD_WIDTH]
    return (
        dq[None],
        grads[:, :width].astype(jnp.bfloat16)[None],
        grads[:, width:].astype(jnp.bfloat16)[None],
        sum_q,
        sum_k,
        sum_v,
    )


def solution(mesh):
    return jax.shard_map(
        on_device,
        mesh=mesh,
        in_specs=(
            P("dp", "ctx", "head"),
            P("dp", "ctx", "head"),
            P("dp", "ctx", "head"),
            P("dp", "ctx", "head"),
            P("dp", "ctx", "head"),
            P("dp", None),
            P("dp", None),
        ),
        out_specs=(
            P("dp", "ctx", "head"),
            P("dp", "ctx", "head"),
            P("dp", "ctx", "head"),
            P("head"),
            P("head"),
            P("head"),
        ),
        check_vma=False,
    )
```
